32 devices in a mesh: seq: 4 (over z), phase: 4 (over y, x), dp: 2 (over core).
Axes of the slice: x: 2, y: 2, z: 4, core: 2. Of those that a mesh axis runs over, the one named last changes fastest.
Arguments:
- byte_embed: bfloat16 [4096, 1536], P(('dp', 'seq')), parts along dimension 0, may hold values from -6 to 6
- in_gain: float32 [1536], replicated, may hold values from 0.25 to 1.75
- w_qkv: bfloat16 [1536, 3, 1536], P('seq', None, 'phase')
- w_up: bfloat16 [1536, 3072], P('phase')
- out_gain: float32 [3072], P('phase'), may hold values from 0.25 to 1.75
- bounds: int32 [1024], P(('dp', 'seq')), parts along dimension 0, may hold values from 0 to 2047, as said below
- owner: int32 [1024, 1], P(('dp', 'seq')), parts along dimension 0, may hold values from 0 to 3; in each aligned block of 128 rows (0 to 127, 128 to 255, ...) at most 64 rows name the same one
Outputs:
- byte_states: bfloat16 [4096, 1536], P(('dp', 'seq'), 'phase'), parts along dimension 0
- stretch_states: bfloat16 [2048, 3072], P(('dp', 'seq'), 'phase'), parts along dimension 0
The draws below stay inside these ranges and needn't reach their ends.
There are 2 independent parts, one for each index of `dp`. The reference program is written for one: setup_inputs(seed, part) draws one part's arguments, and reference() takes and returns one part's arrays. A program takes and returns all parts, laid end to end along the dimension named above; an argument that names none is the same for every part. Nothing has to cross between parts.
Inputs may be any that keep to these rules, and one draw needn't show every extreme that they name: `bounds`: strictly rising; the 128 entries of block b lie in bytes b * 512 to (b + 1) * 512 - 1, and the first and last byte of each block are among them. Among the 128 stretch rows of one block no owner is named more than 64 times.
All inputs are finite; a program needn't handle non-finite values.
Results may differ from the reference program's by a relative error of at most 0.013.
Values may be sent and summed in bfloat16 or wider, within the bound.
A program may use at most 128 MiB of HBM per device.

```python
import math
import jax
import jax.numpy as jnp
import numpy as np
from jax import lax

D = 1536
DC = 3072
HD = 128
WINDOW = 1024
TOK_DEV = 512
HEADS = 12
OWNERS = 4
BYTES = 2048
CROWS = 128
SLOT = 64
N_PHASE = 4


def draw_w_qkv(key, part):
    base = jax.random.normal(key, (D, 3, D), jnp.float32) * D ** (-0.5)
    return base.astype(jnp.bfloat16)


def draw_w_up(key, part):
    base = jax.random.normal(jax.random.fold_in(key, 11), (D, DC), jnp.float32) * D ** (-0.5)
    rough = jax.random.uniform(jax.random.fold_in(key, 12), (DC,), jnp.float32, 0.7, 1.3)
    where = jnp.arange(DC, dtype=jnp.float32) / DC
    ramp = jnp.exp(where * 1.3863)
    return (base * (ramp * rough)[None, :]).astype(jnp.bfloat16)


def draw_bounds(key, part):

    def one_block(block):
        sub = jax.random.fold_in(key, block)
        inner = jax.random.permutation(sub, TOK_DEV - 2)[:CROWS - 2].astype(jnp.int32) + 1
        ends = jnp.array([0, TOK_DEV - 1], jnp.int32)
        return jnp.sort(jnp.concatenate([ends, inner])) + block * TOK_DEV
    return jax.vmap(one_block)(jnp.arange(OWNERS, dtype=jnp.int32)).reshape(-1)


def shard_levels(own_key, shape, cuts, least, largest):
    level = 1.0
    for axis_at, shards_of in cuts:
        steps = jax.random.uniform(jax.random.fold_in(jax.random.fold_in(own_key, 6), axis_at), (shards_of,), jnp.float32, least / len(cuts), largest / len(cuts))
        level = level * jnp.repeat(jnp.exp(steps), shape[axis_at] // shards_of).reshape((-1,) + (1,) * (len(shape) - 1 - axis_at))
    return level


def shared_out(rng, own, number, rows, number_of, top, bound, lean):
    sequence = jax.random.permutation(rng, number_of)
    crowded, usual = portions_of(number_of, rows * top, bound, lean, True), portions_of(number_of, rows * top, bound, lean, False)
    places = jnp.arange(number_of)

    def named(lengths, rotation):
        used = int((lengths > 0).sum())
        fixed = max(1, used // 4)
        passed = fixed + (places - fixed + rotation * (used - fixed)) % max(1, number_of - fixed)
        return jnp.zeros((number_of,), jnp.int32).at[sequence[jnp.where(places < fixed, places, passed)]].set(jnp.asarray(lengths, jnp.int32))

    lengths = jnp.where(number % 4 == 0, named(crowded, number // 4), named(usual, number - number // 4 - 1))
    mixed = jax.random.permutation(jax.random.fold_in(own, 3), number_of)
    donor, taker = mixed[0:number_of // 2 * 2:2], mixed[1:number_of // 2 * 2:2]
    room = jnp.minimum(lengths[donor] - 1, bound - lengths[taker]) // 2
    room = jnp.where((donor == sequence[0]) | (taker == sequence[0]) | (lengths[taker] == 0), 0, jnp.maximum(room, 0))
    passed = jax.random.randint(jax.random.fold_in(own, 4), (number_of // 2,), 0, 1 << 20) % (room + 1)
    lengths = lengths.at[donor].add(-passed).at[taker].add(passed)
    items = jnp.searchsorted(jnp.cumsum(lengths), jnp.arange(rows * top), side="right").astype(jnp.int32)
    grid = items.reshape(top, rows).T
    grid = grid[jax.random.permutation(jax.random.fold_in(own, 1), rows)]
    rotation = jax.random.randint(jax.random.fold_in(own, 2), (rows, 1), 0, top)
    return jnp.take_along_axis(grid, (jnp.arange(top)[None, :] + rotation) % top, axis=1)


def portions_of(amount, total, bound, lean, full):
    weights = [(1 << 20) // math.isqrt(grade ** lean) + 1 for grade in range(1, amount + 1)]
    largest = bound if full else min(bound, max(-(-total // amount), total * weights[0] // sum(weights)))
    least = 1 if total - largest >= amount - 1 else 0
    counts, spare = [largest] + [least] * (amount - 1), total - largest - least * (amount - 1)
    while spare > 0:
        movable = [i for i in range(1, amount) if counts[i] < largest] or [i for i in range(1, amount) if counts[i] < bound]
        mass, left = sum([weights[i] for i in movable]), spare
        for i in movable:
            more = min(bound - counts[i], max(1, left * weights[i] // mass), spare)
            counts[i] = counts[i] + more
            spare = spare - more
    return np.array(counts)


def scatter_about(own_key, extent, width, limit, split=(), kind=jnp.bfloat16):
    loudness = shard_levels(own_key, extent, split, -0.22, 0.18) if split else 1.0
    drawn = jax.random.normal(own_key, extent, jnp.float32) * width * loudness
    return jnp.minimum(jnp.maximum(drawn, -limit), limit).astype(kind)


def setup_inputs(seed: int = 0, part: int = 0) -> dict:
    splits = jax.random.split(jax.random.key(seed), 8)
    part_keys = jax.random.split(jax.random.fold_in(splits[7], part), 8)
    byte_embed = scatter_about(part_keys[0], (BYTES, D), 1.0, 6.0, ((0, 4),))
    in_gain = jnp.clip(1.0 + 0.15 * jax.random.normal(splits[1], (D,), jnp.float32), 0.25, 1.75)
    w_qkv = draw_w_qkv(jax.random.fold_in(splits[7], 71), part)
    w_up = draw_w_up(jax.random.fold_in(splits[7], 71), part)
    out_gain = jnp.clip(1.0 + 0.15 * jax.random.normal(splits[4], (DC,), jnp.float32), 0.25, 1.75)
    bounds = draw_bounds(jax.random.fold_in(jax.random.fold_in(splits[7], part), 71), part)
    owner_keys = jax.random.split(jax.random.fold_in(part_keys[6], 1), (OWNERS * CROWS) // CROWS)
    owner_turns = jax.random.permutation(jax.random.fold_in(part_keys[6], 3), (OWNERS * CROWS) // CROWS)
    owner = jax.vmap(lambda own, number: shared_out(jax.random.fold_in(part_keys[6], 2), own, number, CROWS, OWNERS, 1, SLOT, 2))(owner_keys, owner_turns).reshape((OWNERS * CROWS, 1))
    return dict(byte_embed=byte_embed, in_gain=in_gain, w_qkv=w_qkv, w_up=w_up, out_gain=out_gain, bounds=bounds, owner=owner)


def reference(byte_embed, in_gain, w_qkv, w_up, out_gain, bounds, owner):
    x32 = byte_embed.astype(jnp.float32)
    normed = (x32 * lax.rsqrt(lax.optimization_barrier(jnp.mean(x32 * x32, axis=1, keepdims=True)) + 1e-05) * in_gain).astype(jnp.bfloat16)
    qkv = jnp.dot(normed, w_qkv.reshape(D, 3 * D), preferred_element_type=jnp.float32).astype(jnp.bfloat16)
    qkv = qkv.reshape(BYTES, 3, HEADS, HD)
    query = qkv[:, 0]
    keys = qkv[:, 1]
    values = qkv[:, 2]
    padding = jnp.zeros((WINDOW, HEADS, HD), jnp.bfloat16)
    keys_pad = jnp.concatenate([padding, keys], axis=0)
    values_pad = jnp.concatenate([padding, values], axis=0)
    span = WINDOW + TOK_DEV

    def block(index):
        start = (index * TOK_DEV).astype(jnp.int32)
        q_blk = lax.dynamic_slice_in_dim(query, start, TOK_DEV, 0).astype(jnp.float32)
        k_blk = lax.dynamic_slice_in_dim(keys_pad, start, span, 0).astype(jnp.float32)
        v_blk = lax.dynamic_slice_in_dim(values_pad, start, span, 0).astype(jnp.float32)
        scores = jnp.einsum('ihd,jhd->hij', q_blk, k_blk) * HD ** (-0.5)
        q_pos = start + jnp.arange(TOK_DEV, dtype=jnp.int32)
        k_pos = start - WINDOW + jnp.arange(span, dtype=jnp.int32)
        keep = (k_pos[None, :] <= q_pos[:, None]) & (k_pos[None, :] > q_pos[:, None] - WINDOW) & (k_pos[None, :] >= 0)
        scores = jnp.where(keep[None], scores, -jnp.inf)
        top = lax.optimization_barrier(jnp.max(scores, axis=2, keepdims=True))
        expo = jnp.exp(scores - top)
        probs = (expo / lax.optimization_barrier(jnp.sum(expo, axis=2, keepdims=True))).astype(jnp.bfloat16)
        return jnp.einsum('hij,jhd->ihd', probs.astype(jnp.float32), v_blk).astype(jnp.bfloat16)
    attended = lax.map(block, jnp.arange(OWNERS, dtype=jnp.int32)).reshape(BYTES, D)
    byte_states = (x32 + attended.astype(jnp.float32)).astype(jnp.bfloat16)
    stretch_rows = byte_states[bounds]
    group = D // N_PHASE
    projected = jnp.zeros((OWNERS * CROWS, DC), jnp.float32)
    for part in range(N_PHASE):
        piece = jnp.dot(stretch_rows[:, part * group:(part + 1) * group], w_up[part * group:(part + 1) * group], preferred_element_type=jnp.float32)
        projected = projected + piece.astype(jnp.bfloat16).astype(jnp.float32)
    main_in = (projected * lax.rsqrt(lax.optimization_barrier(jnp.mean(projected * projected, axis=1, keepdims=True)) + 1e-05) * out_gain).astype(jnp.bfloat16)
    owners = owner[:, 0].reshape(OWNERS, CROWS)
    place = jnp.arange(CROWS, dtype=jnp.int32)
    earlier = (owners[:, :, None] == owners[:, None, :]) & (place[None, None, :] < place[None, :, None])
    rank = lax.optimization_barrier(jnp.sum(earlier.astype(jnp.int32), axis=2))
    source = jnp.arange(OWNERS, dtype=jnp.int32)[:, None]
    target = (owners * (OWNERS * SLOT) + source * SLOT + rank).reshape(-1)
    stretch_states = jnp.zeros((OWNERS * OWNERS * SLOT, DC), jnp.bfloat16).at[target].set(main_in)
    return (byte_states, stretch_states)
```

```python
import functools
import math
import jax
import jax.numpy as jnp
from jax import lax
from jax.experimental import pallas as pl
from jax.experimental.pallas import tpu as pltpu
from jax.sharding import PartitionSpec as P

DC = 3072
HD = 128
WINDOW = 1024
MESH = pl.DeviceIdType.MESH
NEG = -0.7 * 3.4e38


def fused_kernel(
    dims,
    x_ref,
    gain_ref,
    w_ref,
    up_ref,
    og_ref,
    bounds_ref,
    owner_ref,
    bs_ref,
    ss_ref,
    xbuf,
    gain,
    og,
    bnd,
    own,
    normed,
    halo,
    wbuf,
    upbuf,
    qbuf,
    kbuf,
    vbuf,
    obuf,
    mbuf,
    lbuf,
    place,
    outrows,
    arrived,
    acc,
    sqbuf,
    loc_sem,
    w_send,
    w_recv,
    p_send,
    p_recv,
    up_send,
    up_recv,
    upp_send,
    upp_recv,
    h_send,
    h_recv,
    g_send,
    g_recv,
    row_send,
    row_recv,
    all_send,
    all_recv,
    sq_send,
    sq_recv,
):
    n_seq, n_phase, reach, slot = dims
    tok, d = xbuf.shape
    rows, width = w_ref.shape[1:]
    half = rows // 2
    heads = width // HD
    last = heads - 1
    crows = bnd.shape[1]
    cols = og.shape[1]
    z = lax.axis_index("seq")
    p = lax.axis_index("phase")
    c = lax.axis_index("dp")

    own_x = pltpu.make_async_copy(x_ref, xbuf, loc_sem.at[0])
    own_x.start()
    small = []
    for i, (src, dst) in enumerate(
        ((gain_ref, gain.at[0]), (bounds_ref, bnd), (owner_ref, own), (og_ref, og.at[0]))
    ):
        small.append(pltpu.make_async_copy(src, dst, loc_sem.at[2 + heads + i]))
        small[i].start()

    twin_core = {"dp": 1 - c}
    peers = (
        [{"seq": lax.rem(z + k, n_seq)} for k in range(1, n_seq)]
        + [{"phase": lax.rem(p + k, n_phase)} for k in range(1, n_phase)]
        + [twin_core]
    )
    barrier = pltpu.get_barrier_semaphore()
    for peer in peers:
        pl.semaphore_signal(barrier, inc=1, device_id=peer, device_id_type=MESH)

    own_w = []
    for h in range(heads):
        own_w.append(
            pltpu.make_async_copy(
                w_ref.at[:, :, pl.ds(h * HD, HD)],
                wbuf.at[h, :, pl.ds(pl.multiple_of(z * rows, rows), rows), :],
                loc_sem.at[2 + h],
            )
        )
        own_w[h].start()
    own_up = pltpu.make_async_copy(
        up_ref.at[:, pl.ds(pl.multiple_of(p * cols, 128), cols)], upbuf.at[p], loc_sem.at[1]
    )
    own_up.start()
    pl.semaphore_wait(barrier, len(peers))

    pending = []

    def when(cond, action):
        if cond is None:
            action()
        else:
            pl.when(cond)(action)

    def send(src, dst, ssem, rsem, peer, cond=None):
        copy = pltpu.make_async_remote_copy(
            src_ref=src, dst_ref=dst, send_sem=ssem, recv_sem=rsem, device_id=peer, device_id_type=MESH
        )
        when(cond, copy.start)
        pending.append((cond, copy))
        return copy

    right, left = {"seq": z + 1}, {"seq": z - 1}
    has_right, has_left = z < n_seq - 1, z > 0
    ways = ((right, has_right, -1), (left, has_left, 1))
    RIGHTWARD, LEFTWARD = 0, 1

    def chunk(h, shard):
        at = pl.multiple_of(shard * rows + c * half, half)
        return wbuf.at[h, :, pl.ds(at, half), :]

    def slot_of(t, way):
        return t - 1 if way == LEFTWARD else n_seq - t - 1

    def issue_own(h, way, also=None):
        src = chunk(h, z)
        peer, cond, sign = ways[way]
        cond = cond if also is None else cond & also
        send(src, chunk(h, z), w_send.at[way, h, 0], w_recv.at[h, slot_of(1, way)], peer, cond)

    twins = {}

    def relay(h, t, way, also=None):
        if t >= n_seq:
            return
        peer, cond, sign = ways[way]
        shard = z + sign * t
        here = (shard >= 0) & (shard < n_seq)
        there = here if also is None else here & also
        piece = chunk(h, jnp.clip(shard, 0, n_seq - 1))
        got = pltpu.make_async_remote_copy(
            src_ref=piece,
            dst_ref=piece,
            send_sem=w_send.at[way, h, t - 1],
            recv_sem=w_recv.at[h, slot_of(t, way)],
            device_id=peer,
            device_id_type=MESH,
        )
        pl.when(there)(got.wait_recv)
        if t < n_seq - 1:
            send(piece, piece, w_send.at[way, h, t], w_recv.at[h, slot_of(t + 1, way)], peer, there & cond)
        twins[h, t, way] = (
            here,
            send(piece, piece, p_send.at[h, slot_of(t, way)], p_recv.at[h, slot_of(t, way)], twin_core, there),
        )

    def finish(h):
        for t in range(1, n_seq):
            for way in range(2):
                there, twin = twins[h, t, way]
                pl.when(there)(twin.wait_recv)

    across = {1: {"phase": p + 1 - 2 * lax.rem(p, 2)}, 2: {"phase": lax.rem(p + 2, n_phase)}}
    spots = {k: v["phase"] for k, v in across.items()}
    mine = {}

    def halo_start(dist, cond):
        own_part = normed.at[:, pl.ds(pl.multiple_of(p * width, 128), width)]
        src = own_part if dist == 1 else halo.at[dist - 2, p]
        mine[dist] = send(src, halo.at[dist - 1, p], h_send.at[dist - 1], h_recv.at[dist - 1], right, cond)

    gathers = {}

    def halo_spread(dist):
        there = z >= dist
        pl.when(there)(mine[dist].wait_recv)
        if dist < reach:
            halo_start(dist + 1, there & has_right)
        for k in (1, 2):
            piece = halo.at[dist - 1, p]
            gathers[dist, k] = send(
                piece, piece, g_send.at[dist - 1, k - 1], g_recv.at[dist - 1, k - 1], across[k], there
            )

    def halo_pass(dist, also=None):
        there = z >= dist
        if also is not None:
            there = there & also
        for k in (1, 2):
            pl.when(there)(gathers[dist, k].wait_recv)
            part = pl.ds((k - 1) * (tok // 2), tok // 2)
            piece = halo.at[dist - 1, spots[k], part]
            gathers[dist, 2 + k] = send(
                piece, piece, g_send.at[dist - 1, k + 1], g_recv.at[dist - 1, k + 1], across[3 - k], there
            )

    def halo_wait(dist):
        @pl.when(z >= dist)
        def _():
            for k in (1, 2):
                gathers[dist, 2 + k].wait_recv()

    own_w[0].wait()
    issue_own(0, RIGHTWARD)
    issue_own(0, LEFTWARD)
    for h in range(1, heads):
        own_w[h].wait()
        issue_own(h, LEFTWARD)
    up_rows = up_ref.shape[0] // 2
    up_half = pl.ds(pl.multiple_of(c * up_rows, up_rows), up_rows)
    up_copies, up_twins = [], []
    for k in range(1, n_phase):
        other = lax.rem(p + k, n_phase)
        part = pl.ds(pl.multiple_of(other * cols, 128), cols)
        up_copies.append(
            send(
                up_ref.at[up_half, part],
                upbuf.at[p, up_half],
                up_send.at[k - 1],
                up_recv.at[k - 1],
                {"phase": other},
            )
        )

    own_x.wait()
    small[0].wait()
    step_rows = 64


    @pl.loop(0, tok // step_rows)
    def _(i):
        r = pl.ds(pl.multiple_of(i * step_rows, step_rows), step_rows)
        xx = xbuf[r, :].astype(jnp.float32)
        scale = lax.rsqrt(jnp.mean(xx * xx, axis=1, keepdims=True) + 1e-05)
        normed[r, :] = (xx * scale * gain[...]).astype(jnp.bfloat16)

    halo_start(1, has_right)
    first, second, final = z == 0, z == 1, z == n_seq - 1
    for h in range(1, heads):
        issue_own(h, RIGHTWARD, first)

    def column(ref):
        wide = jnp.broadcast_to(ref[...].astype(jnp.float32), (crows, crows))
        return wide.T

    relay(0, 1, RIGHTWARD)
    relay(0, 1, LEFTWARD)
    for copy in small[1:]:
        copy.wait()
    local = column(bnd)[:, 0:1] - (z * tok).astype(jnp.float32)
    spot = lax.broadcasted_iota(jnp.int32, (crows, tok), 1).astype(jnp.float32)
    pick = jnp.where(local == spot, 1.0, 0.0).astype(jnp.bfloat16)
    same = column(own) == own[...].astype(jnp.float32)
    before = lax.broadcasted_iota(jnp.int32, (crows, crows), 0) < lax.broadcasted_iota(
        jnp.int32, (crows, crows), 1
    )
    rank = jnp.sum(jnp.where(same & before, 1, 0), axis=0, keepdims=True)
    target = own[...] * slot + rank
    route = jnp.where(
        target == lax.broadcasted_iota(jnp.int32, (n_seq * slot, crows), 0), 1.0, 0.0
    ).astype(jnp.bfloat16)
    place[...] = jnp.dot(route, pick, preferred_element_type=jnp.float32).astype(jnp.bfloat16)

    tq = min(tok, 256)
    scale = HD ** (-0.5) * math.log2(math.e)

    def attend(dist, h):
        for q0 in range(0, tok, tq):
            r = pl.ds(q0, tq)
            low = max(0, q0 + dist * tok - WINDOW + 1) // 128 * 128
            keys = slice(low, tok if dist else q0 + tq)
            s = lax.dot_general(
                qbuf[h, r, :],
                kbuf[dist, keys],
                (((1,), (1,)), ((), ())),
                preferred_element_type=jnp.float32,
            )
            if dist == 0 or (dist + 1) * tok - 1 >= WINDOW:
                qi = q0 + lax.broadcasted_iota(jnp.int32, s.shape, 0)
                kj = lax.broadcasted_iota(jnp.int32, s.shape, 1) + (low - dist * tok)
                s = jnp.where((kj <= qi) & (kj > qi - WINDOW), s, NEG)
            top = jnp.max(s, axis=1, keepdims=True)
            if dist > 0:
                old = mbuf[h, r, :]
                top = jnp.maximum(top, old)
            e = jnp.exp2(s * scale - top * scale)
            total = jnp.sum(e, axis=1, keepdims=True)
            o = jnp.dot(e.astype(jnp.bfloat16), vbuf[dist, keys], preferred_element_type=jnp.float32)
            if dist > 0:
                fade = jnp.exp2((old - top) * scale)
                total = total + fade * lbuf[h, r, :]
                o = o + fade * obuf[h, r, :]
            mbuf[h, r, :] = top
            lbuf[h, r, :] = total
            obuf[h, r, :] = o

    def own_block(h):
        w = jnp.concatenate([wbuf[h, j] for j in range(3)], axis=1)
        got = jnp.dot(normed[...], w, preferred_element_type=jnp.float32).astype(jnp.bfloat16)
        qbuf[h] = got[:, :HD]
        kbuf[0] = got[:, HD : 2 * HD]
        vbuf[0] = got[:, 2 * HD :]
        attend(0, h)

    def earlier_block(h, dist):
        @pl.when(z >= dist)
        def _():
            w = jnp.concatenate([wbuf[h, j] for j in range(1, 3)], axis=1)
            rows_in = jnp.concatenate([halo[dist - 1, q] for q in range(n_phase)], axis=1)
            got = jnp.dot(rows_in, w, preferred_element_type=jnp.float32).astype(jnp.bfloat16)
            kbuf[dist] = got[:, :HD]
            vbuf[dist] = got[:, HD:]
            attend(dist, h)

    def close(h):
        at = slice(h * HD, (h + 1) * HD)
        res = xbuf[:, pl.ds(pl.multiple_of(p * width + h * HD, HD), HD)].astype(jnp.float32)
        att = (obuf[h] / lbuf[h]).astype(jnp.bfloat16).astype(jnp.float32)
        states = (res + att).astype(jnp.bfloat16)
        bs_ref[:, at] = states
        routed = jnp.dot(place[...], states, preferred_element_type=jnp.float32).astype(jnp.bfloat16)
        for s in range(n_seq):
            outrows[h, s] = routed[s * slot : (s + 1) * slot]
        for k in range(1, n_seq):
            other = lax.rem(z + k, n_seq)
            send(
                outrows.at[h, other],
                arrived.at[h, p, z],
                row_send.at[h, k - 1],
                row_recv.at[h, z],
                {"seq": other},
            )
        arrived[h, p, z] = outrows[h, z]

    def rows_wait(h, s, cond=None):
        here = arrived.at[h, p, s]
        got = pltpu.make_async_remote_copy(
            src_ref=here,
            dst_ref=here,
            send_sem=row_send.at[h, 0],
            recv_sem=row_recv.at[h, s],
            device_id={"seq": lax.rem(z + 1, n_seq)},
            device_id_type=MESH,
        )
        pl.when(z != s if cond is None else (z != s) & cond)(got.wait_recv)

    spreads = {}

    def spread(h, j, cond=None):
        sources = [n_seq - 1] if j else list(range(n_seq - 1))
        if (h, j) not in spreads:
            piece = arrived.at[h, p, pl.ds(sources[0], len(sources))]
            spreads[h, j] = [
                pltpu.make_async_remote_copy(
                    src_ref=piece,
                    dst_ref=piece,
                    send_sem=all_send.at[h, j, k - 1],
                    recv_sem=all_recv.at[h, j, k - 1],
                    device_id={"phase": lax.rem(p + k, n_phase)},
                    device_id_type=MESH,
                )
                for k in range(1, n_phase)
            ]
            pending.extend((None, copy) for copy in spreads[h, j])
        for s in sources:
            rows_wait(h, s, cond)
        for copy in spreads[h, j]:
            when(cond, copy.start)

    for h in range(1, heads):
        relay(h, 1, LEFTWARD)
    halo_spread(1)
    for k in range(1, n_phase):
        up_copies[k - 1].wait_recv()
        piece = upbuf.at[lax.rem(p + n_phase - k, n_phase), up_half]
        up_twins.append(send(piece, piece, upp_send.at[k - 1], upp_recv.at[k - 1], twin_core))
    for h in range(1, heads):
        issue_own(h, RIGHTWARD, second)
        relay(h, 1, RIGHTWARD, second)
    relay(0, 2, RIGHTWARD)
    issue_own(1, RIGHTWARD, z > 1)
    for t in range(2, n_seq):
        for h in range(heads):
            relay(h, t, LEFTWARD)
    for dist in range(2, reach + 1):
        halo_pass(dist - 1)
        halo_spread(dist)
    for t in range(3, n_seq):
        relay(0, t, RIGHTWARD)
    finish(0)
    own_block(0)
    relay(1, 1, RIGHTWARD, (z > 1) & (z < n_seq - 1))
    relay(1, 2, RIGHTWARD, z < n_seq - 1)
    issue_own(2, RIGHTWARD, z > 1)
    for dist in range(1, reach):
        halo_wait(dist)
        earlier_block(0, dist)
    relay(1, 1, RIGHTWARD, final)
    relay(1, 2, RIGHTWARD, final)
    halo_pass(reach, final)
    for t in range(3, n_seq):
        relay(1, t, RIGHTWARD)
    finish(1)
    own_block(1)
    relay(2, 1, RIGHTWARD, (z > 1) & (z < n_seq - 1))
    for dist in range(1, reach):
        earlier_block(1, dist)
    halo_pass(reach, z < n_seq - 1)
    relay(2, 1, RIGHTWARD, final)
    relay(2, 2, RIGHTWARD, z < n_seq - 1)
    halo_wait(reach)
    earlier_block(0, reach)
    close(0)
    for h in range(1, last):
        earlier_block(h, reach)
        close(h)
    relay(2, 2, RIGHTWARD, final)
    for h in range(last):
        spread(h, 0, z >= n_seq - 2)
        spread(h, 1, final)
    for t in range(3, n_seq):
        relay(2, t, RIGHTWARD)
    finish(last)
    own_block(last)
    for dist in range(1, reach + 1):
        earlier_block(last, dist)
    close(last)
    for h in range(last):
        spread(h, 0, z < n_seq - 2)
    for h in range(last):
        spread(h, 1, z < n_seq - 1)
    spread(last, 0)
    own_up.wait()
    for twin in up_twins:
        twin.wait_recv()
    for k in range(1, n_phase):
        for h in range(last):
            for j in range(2):
                spreads[h, j][k - 1].wait_recv()
    full = n_seq * slot

    def rows_of(s, hs):
        return jnp.concatenate([arrived[h, s].reshape(full, HD) for h in hs], axis=1)

    for k in range(n_phase):
        s = lax.rem(p + n_phase - k, n_phase)
        acc[k] = jnp.dot(
            rows_of(s, range(last)), upbuf[s, : last * HD, :], preferred_element_type=jnp.float32
        )
    spread(last, 1)

    def piece_of(k):
        s = lax.rem(p + n_phase - k, n_phase)
        got = acc[k] + jnp.dot(
            rows_of(s, [last]), upbuf[s, last * HD :, :], preferred_element_type=jnp.float32
        )
        return got.astype(jnp.bfloat16).astype(jnp.float32)

    projected = piece_of(0)
    for k in range(1, n_phase):
        for j in range(2):
            spreads[last, j][k - 1].wait_recv()
        projected = projected + piece_of(k)
    sq = jnp.sum(projected * projected, axis=1, keepdims=True)
    sqbuf[p] = jnp.broadcast_to(sq, (full, 128)).T[0:8, :]
    sq_copies = []
    for k in range(1, n_phase):
        other = lax.rem(p + k, n_phase)
        sq_copies.append(
            send(sqbuf.at[p], sqbuf.at[p], sq_send.at[k - 1], sq_recv.at[k - 1], {"phase": other})
        )
    for copy in sq_copies:
        copy.wait_recv()
    all_sq = sqbuf[0]
    for k in range(1, n_phase):
        all_sq = all_sq + sqbuf[k]
    all_sq = jnp.broadcast_to(all_sq[0:1, :], (128, full)).T[:, 0:1]
    norm = lax.rsqrt(all_sq / (n_phase * cols) + 1e-05)
    ss_ref[...] = (projected * norm * og[...]).astype(jnp.bfloat16)
    for cond, copy in pending:
        when(cond, copy.wait_send)


def fused(n_seq, n_phase, byte_embed, in_gain, w_qkv, w_up, out_gain, bounds, owner):
    tok, d = byte_embed.shape
    rows, _, width = w_qkv.shape
    heads = width // HD
    crows = bounds.shape[0]
    cols = out_gain.shape[0]
    slot = 2 * crows // n_seq
    reach = -(-WINDOW // tok)
    bf, f32 = jnp.bfloat16, jnp.float32
    vmem = pl.BlockSpec(memory_space=pltpu.VMEM)
    hbm = pl.BlockSpec(memory_space=pltpu.HBM)
    dma = pltpu.SemaphoreType.DMA
    in_hbm = lambda a: pltpu.with_memory_space_constraint(a, pltpu.HBM)
    states, stretch = pl.pallas_call(
        functools.partial(fused_kernel, (n_seq, n_phase, reach, slot)),
        out_shape=(
            jax.ShapeDtypeStruct((tok, width), bf),
            jax.ShapeDtypeStruct((n_seq * slot, cols), bf),
        ),
        in_specs=[hbm] * 7,
        out_specs=(vmem, vmem),
        scratch_shapes=[
            pltpu.VMEM((tok, d), bf),
            pltpu.VMEM((1, d), f32),
            pltpu.VMEM((1, cols), f32),
            pltpu.VMEM((1, crows), jnp.int32),
            pltpu.VMEM((1, crows), jnp.int32),
            pltpu.VMEM((tok, d), bf),
            pltpu.VMEM((reach, n_phase, tok, width), bf),
            pltpu.VMEM((heads, 3, n_seq * rows, HD), bf),
            pltpu.VMEM((n_phase, w_up.shape[0], cols), bf),
            pltpu.VMEM((heads, tok, HD), bf),
            pltpu.VMEM((reach + 1, tok, HD), bf),
            pltpu.VMEM((reach + 1, tok, HD), bf),
            pltpu.VMEM((heads, tok, HD), f32),
            pltpu.VMEM((heads, tok, 1), f32),
            pltpu.VMEM((heads, tok, 1), f32),
            pltpu.VMEM((n_seq * slot, tok), bf),
            pltpu.VMEM((heads, n_seq, slot, HD), bf),
            pltpu.VMEM((heads, n_phase, n_seq, slot, HD), bf),
            pltpu.VMEM((n_phase, n_seq * slot, cols), f32),
            pltpu.VMEM((n_phase, 8, n_seq * slot), f32),
            dma((6 + heads,)),
            dma((2, heads, n_seq - 1)),
            dma((heads, n_seq - 1)),
            dma((heads, n_seq - 1)),
            dma((heads, n_seq - 1)),
            dma((n_phase - 1,)),
            dma((n_phase - 1,)),
            dma((n_phase - 1,)),
            dma((n_phase - 1,)),
            dma((reach,)),
            dma((reach,)),
            dma((reach, 4)),
            dma((reach, 4)),
            dma((heads, n_seq - 1)),
            dma((heads, n_seq)),
            dma((heads, 2, n_phase - 1)),
            dma((heads, 2, n_phase - 1)),
            dma((n_phase - 1,)),
            dma((n_phase - 1,)),
        ],
        compiler_params=pltpu.CompilerParams(
            collective_id=0, has_side_effects=True, vmem_limit_bytes=48 * 1024 * 1024
        ),
    )(
        in_hbm(byte_embed),
        in_hbm(in_gain),
        in_hbm(jnp.transpose(w_qkv, (1, 0, 2))),
        in_hbm(w_up),
        in_hbm(out_gain),
        in_hbm(bounds.reshape(1, crows)),
        in_hbm(owner.reshape(1, crows)),
    )
    return states, stretch


def passed_along(value, axis, by):
    devices = lax.axis_size(axis)
    pairs = [(i, i + by) for i in range(devices) if 0 <= i + by < devices]
    return lax.ppermute(value, axis, pairs)


def project_rows(rows, w_up, out_gain):
    groups = lax.axis_size("phase")
    full_rows = lax.all_gather(rows, "phase", axis=1, tiled=True)
    w_cols = lax.all_to_all(w_up, "phase", split_axis=1, concat_axis=0, tiled=True)
    count = full_rows.shape[0]
    width = rows.shape[1]
    columns = w_cols.shape[1]
    pieces = jnp.einsum(
        "nsg,sgc->snc",
        full_rows.reshape(count, groups, width),
        w_cols.reshape(groups, width, columns),
        preferred_element_type=jnp.float32,
    )
    projected = jnp.sum(pieces.astype(jnp.bfloat16).astype(jnp.float32), axis=0)
    squares = lax.psum(jnp.sum(projected * projected, axis=1), "phase")
    scale = lax.rsqrt(squares / DC + 1e-05)
    return (projected * scale[:, None] * out_gain).astype(jnp.bfloat16)


def on_device(byte_embed, in_gain, w_qkv, w_up, out_gain, bounds, owner):
    tok = byte_embed.shape[0]
    n_seq = lax.axis_size("seq")
    mine = lax.axis_index("seq")
    section = lax.axis_index("phase")
    width_dev = w_qkv.shape[2]
    heads_dev = width_dev // HD
    x32 = byte_embed.astype(jnp.float32)
    normed = (x32 * lax.rsqrt(jnp.mean(x32 * x32, axis=1, keepdims=True) + 1e-05) * in_gain).astype(
        jnp.bfloat16
    )
    piece = lax.all_gather(w_qkv, "seq", axis=0, tiled=True)
    qkv = jnp.dot(
        normed, piece.reshape(piece.shape[0], 3 * width_dev), preferred_element_type=jnp.float32
    ).astype(jnp.bfloat16)
    qkv = qkv.reshape(tok, 3, heads_dev, HD)
    query = qkv[:, 0]
    keys = qkv[:, 1]
    values = qkv[:, 2]
    reach = -(-WINDOW // tok)
    key_list = [keys]
    value_list = [values]
    for distance in range(1, reach + 1):
        earlier_keys, earlier_values = passed_along((keys, values), "seq", distance)
        key_list = [earlier_keys] + key_list
        value_list = [earlier_values] + value_list
    key_all = jnp.concatenate(key_list, axis=0)
    value_all = jnp.concatenate(value_list, axis=0)
    scores = jnp.einsum(
        "ihd,jhd->hij", query, key_all, preferred_element_type=jnp.float32
    ) * HD ** (-0.5)
    q_pos = mine * tok + jnp.arange(tok, dtype=jnp.int32)
    k_pos = mine * tok - reach * tok + jnp.arange((reach + 1) * tok, dtype=jnp.int32)
    keep = (
        (k_pos[None, :] <= q_pos[:, None])
        & (k_pos[None, :] > q_pos[:, None] - WINDOW)
        & (k_pos[None, :] >= 0)
    )
    scores = jnp.where(keep[None], scores, -jnp.inf)
    top = jnp.max(scores, axis=2, keepdims=True)
    expo = jnp.exp(scores - top)
    probs = (expo / jnp.sum(expo, axis=2, keepdims=True)).astype(jnp.bfloat16)
    attended = jnp.einsum(
        "hij,jhd->ihd", probs, value_all, preferred_element_type=jnp.float32
    ).astype(jnp.bfloat16)
    attended = attended.reshape(tok, width_dev)
    residual = lax.dynamic_slice_in_dim(x32, section * width_dev, width_dev, 1)
    byte_states = (residual + attended.astype(jnp.float32)).astype(jnp.bfloat16)
    local = bounds - mine * tok
    stretch_rows = jnp.take(byte_states, local, axis=0)
    owners = owner[:, 0]
    crows = owners.shape[0]
    slot_count = 2 * crows // n_seq
    place = jnp.arange(crows, dtype=jnp.int32)
    earlier = (owners[:, None] == owners[None, :]) & (place[None, :] < place[:, None])
    rank = jnp.sum(earlier.astype(jnp.int32), axis=1)
    target = owners * slot_count + rank
    placing = (target[None, :] == jnp.arange(n_seq * slot_count, dtype=jnp.int32)[:, None]).astype(
        jnp.bfloat16
    )
    outgoing = jnp.dot(placing, stretch_rows, preferred_element_type=jnp.float32).astype(
        jnp.bfloat16
    )
    outgoing = outgoing.reshape(n_seq, slot_count, width_dev)
    arrived = lax.all_to_all(outgoing, "seq", split_axis=0, concat_axis=0, tiled=True).reshape(
        n_seq * slot_count, width_dev
    )
    stretch_states = project_rows(arrived, w_up, out_gain)
    return (byte_states, stretch_states)


def solution(mesh):
    n_seq, n_phase, n_dp = (mesh.shape[axis] for axis in ("seq", "phase", "dp"))

    def body(byte_embed, in_gain, w_qkv, *rest):
        tok, (rows, _, width) = byte_embed.shape[0], w_qkv.shape
        slot = 2 * rest[2].shape[0] // n_seq
        tiled = rows % 128 == 0 and width % HD == 0 and tok % 256 == 0 and slot % 16 == 0
        if tiled and n_dp == 2 and n_phase == 4 and w_qkv.shape[0] == rest[0].shape[0]:
            return fused(n_seq, n_phase, byte_embed, in_gain, w_qkv, *rest)
        return on_device(byte_embed, in_gain, w_qkv, *rest)

    return jax.shard_map(
        body,
        mesh=mesh,
        in_specs=(
            P(("dp", "seq"), None),
            P(),
            P("seq", None, "phase"),
            P("phase", None),
            P("phase"),
            P(("dp", "seq")),
            P(("dp", "seq"), None),
        ),
        out_specs=(P(("dp", "seq"), "phase"), P(("dp", "seq"), "phase")),
        check_vma=False,
    )
```

```python
import functools
import math
import jax
import jax.numpy as jnp
from jax import lax
from jax.experimental import pallas as pl
from jax.experimental.pallas import tpu as pltpu
from jax.sharding import PartitionSpec as P

DC = 3072
HD = 128
WINDOW = 1024
MESH = pl.DeviceIdType.MESH
NEG = -0.7 * 3.4e38


def fused_kernel(
    dims,
    x_ref,
    gain_ref,
    w_ref,
    up_ref,
    og_ref,
    bounds_ref,
    owner_ref,
    bs_ref,
    ss_ref,
    xbuf,
    gain,
    og,
    bnd,
    own,
    normed,
    halo,
    wbuf,
    upbuf,
    qbuf,
    kbuf,
    vbuf,
    obuf,
    mbuf,
    lbuf,
    place,
    outrows,
    arrived,
    acc,
    partial,
    sqbuf,
    loc_sem,
    w_send,
    w_recv,
    p_send,
    p_recv,
    up_send,
    up_recv,
    upp_send,
    upp_recv,
    h_send,
    h_recv,
    g_send,
    g_recv,
    row_send,
    row_recv,
    all_send,
    all_recv,
    sq_send,
    sq_recv,
):
    n_seq, n_phase, reach, slot = dims
    tok, d = xbuf.shape
    rows, width = w_ref.shape[1:]
    half = rows // 2
    heads = width // HD
    last = heads - 1
    crows = bnd.shape[1]
    cols = og.shape[1]
    z = lax.axis_index("seq")
    p = lax.axis_index("phase")
    c = lax.axis_index("dp")

    own_x = pltpu.make_async_copy(x_ref, xbuf, loc_sem.at[0])
    own_x.start()
    small = []
    for i, (src, dst) in enumerate(
        ((gain_ref, gain.at[0]), (bounds_ref, bnd), (owner_ref, own), (og_ref, og.at[0]))
    ):
        small.append(pltpu.make_async_copy(src, dst, loc_sem.at[2 + heads + i]))
        small[i].start()

    twin_core = {"dp": 1 - c}
    peers = (
        [{"seq": lax.rem(z + k, n_seq)} for k in range(1, n_seq)]
        + [{"phase": lax.rem(p + k, n_phase)} for k in range(1, n_phase)]
        + [twin_core]
    )
    barrier = pltpu.get_barrier_semaphore()
    for peer in peers:
        pl.semaphore_signal(barrier, inc=1, device_id=peer, device_id_type=MESH)

    own_w = []
    for h in range(heads):
        own_w.append(
            pltpu.make_async_copy(
                w_ref.at[:, :, pl.ds(h * HD, HD)],
                wbuf.at[h, :, pl.ds(pl.multiple_of(z * rows, rows), rows), :],
                loc_sem.at[2 + h],
            )
        )
        own_w[h].start()
    own_up = pltpu.make_async_copy(
        up_ref.at[:, pl.ds(pl.multiple_of(p * cols, 128), cols)], upbuf.at[p], loc_sem.at[1]
    )
    own_up.start()
    pl.semaphore_wait(barrier, len(peers))

    def when(cond, action):
        if cond is None:
            action()
        else:
            pl.when(cond)(action)

    def move(src, dst, ssem, rsem, peer):
        return pltpu.make_async_remote_copy(
            src_ref=src, dst_ref=dst, send_sem=ssem, recv_sem=rsem, device_id=peer, device_id_type=MESH
        )

    def send(src, dst, ssem, rsem, peer, cond=None):
        copy = move(src, dst, ssem, rsem, peer)
        when(cond, copy.start)
        return copy

    def sent(ref, ssem, cond=None):
        when(cond, move(ref, ref, ssem, ssem, twin_core).wait_send)

    def landed(ref, rsem, cond=None):
        when(cond, move(ref, ref, rsem, rsem, twin_core).wait_recv)

    right, left = {"seq": z + 1}, {"seq": z - 1}
    has_right, has_left = z < n_seq - 1, z > 0
    ways = ((right, has_right, -1), (left, has_left, 1))
    RIGHTWARD, LEFTWARD = 0, 1

    def chunk(h, shard):
        at = pl.multiple_of(shard * rows + c * half, half)
        return wbuf.at[h, :, pl.ds(at, half), :]

    def slot_of(t, way):
        return t - 1 if way == LEFTWARD else n_seq - t - 1

    def issue_own(h, way, also=None):
        src = chunk(h, z)
        peer, cond, sign = ways[way]
        cond = cond if also is None else cond & also
        send(src, chunk(h, z), w_send, w_recv.at[h, slot_of(1, way)], peer, cond)

    def relay(h, t, way, also=None):
        if t >= n_seq:
            return
        peer, cond, sign = ways[way]
        shard = z + sign * t
        here = (shard >= 0) & (shard < n_seq)
        there = here if also is None else here & also
        piece = chunk(h, jnp.clip(shard, 0, n_seq - 1))
        landed(piece, w_recv.at[h, slot_of(t, way)], there)
        if t < n_seq - 1:
            send(piece, piece, w_send, w_recv.at[h, slot_of(t + 1, way)], peer, there & cond)
        late = (way == RIGHTWARD) & (t == z)
        group = jnp.where(late, last + 1, h) if h == last else h
        send(piece, piece, p_send, p_recv.at[group], twin_core, there)

    def finish(h, late=None, also=True):
        if h < last:
            landed(wbuf.at[h, :, pl.ds(0, (n_seq - 1) * half)], p_recv.at[h])
        elif late:
            landed(wbuf.at[h, :, pl.ds(0, half)], p_recv.at[last + 1], (z > 0) & also)
        else:
            landed(wbuf.at[h, :, pl.ds(0, (n_seq - 2) * half)], p_recv.at[h], (z > 0) & also)
            landed(wbuf.at[h, :, pl.ds(0, (n_seq - 1) * half)], p_recv.at[h], (z == 0) & also)

    across = {1: {"phase": p + 1 - 2 * lax.rem(p, 2)}, 2: {"phase": lax.rem(p + 2, n_phase)}}
    spots = {k: v["phase"] for k, v in across.items()}
    mine = {}

    def halo_start(dist, cond):
        own_part = normed.at[:, pl.ds(pl.multiple_of(p * width, 128), width)]
        src = own_part if dist == 1 else halo.at[dist - 2, p]
        mine[dist] = send(src, halo.at[dist - 1, p], h_send.at[dist - 1], h_recv.at[dist - 1], right, cond)

    gathers = {}

    def halo_spread(dist):
        there = z >= dist
        pl.when(there)(mine[dist].wait_recv)
        if dist < reach:
            halo_start(dist + 1, there & has_right)
        for k in (1, 2):
            piece = halo.at[dist - 1, p]
            gathers[dist, k] = send(
                piece, piece, g_send.at[dist - 1], g_recv.at[dist - 1, k - 1], across[k], there
            )

    def halo_pass(dist, also=None):
        there = z >= dist
        if also is not None:
            there = there & also
        for k in (1, 2):
            pl.when(there)(gathers[dist, k].wait_recv)
            part = pl.ds((k - 1) * (tok // 2), tok // 2)
            piece = halo.at[dist - 1, spots[k], part]
            gathers[dist, 2 + k] = send(
                piece, piece, g_send.at[dist - 1], g_recv.at[dist - 1, 2], across[3 - k], there
            )

    def halo_wait(dist):
        @pl.when(z >= dist)
        def _():
            landed(halo.at[dist - 1, 0], g_recv.at[dist - 1, 2])

    own_w[0].wait()
    issue_own(0, RIGHTWARD)
    issue_own(0, LEFTWARD)
    for h in range(1, heads):
        own_w[h].wait()
        issue_own(h, LEFTWARD)
    up_rows = up_ref.shape[0] // 2
    up_half = pl.ds(pl.multiple_of(c * up_rows, up_rows), up_rows)
    for k in range(1, n_phase):
        other = lax.rem(p + k, n_phase)
        part = pl.ds(pl.multiple_of(other * cols, 128), cols)
        send(up_ref.at[up_half, part], upbuf.at[p, up_half], up_send, up_recv, {"phase": other})

    own_x.wait()
    small[0].wait()
    step_rows = 64


    @pl.loop(0, tok // step_rows)
    def _(i):
        r = pl.ds(pl.multiple_of(i * step_rows, step_rows), step_rows)
        xx = xbuf[r, :].astype(jnp.float32)
        scale = lax.rsqrt(jnp.mean(xx * xx, axis=1, keepdims=True) + 1e-05)
        normed[r, :] = (xx * scale * gain[...]).astype(jnp.bfloat16)

    halo_start(1, has_right)
    first, second, final = z == 0, z == 1, z == n_seq - 1
    for h in range(1, heads):
        issue_own(h, RIGHTWARD, first)

    def column(ref):
        wide = jnp.broadcast_to(ref[...].astype(jnp.float32), (crows, crows))
        return wide.T

    relay(0, 1, RIGHTWARD)
    relay(0, 1, LEFTWARD)
    for copy in small[1:]:
        copy.wait()
    local = column(bnd)[:, 0:1] - (z * tok).astype(jnp.float32)
    spot = lax.broadcasted_iota(jnp.int32, (crows, tok), 1).astype(jnp.float32)
    pick = jnp.where(local == spot, 1.0, 0.0).astype(jnp.bfloat16)
    same = column(own) == own[...].astype(jnp.float32)
    before = lax.broadcasted_iota(jnp.int32, (crows, crows), 0) < lax.broadcasted_iota(
        jnp.int32, (crows, crows), 1
    )
    rank = jnp.sum(jnp.where(same & before, 1, 0), axis=0, keepdims=True)
    target = own[...] * slot + rank
    route = jnp.where(
        target == lax.broadcasted_iota(jnp.int32, (n_seq * slot, crows), 0), 1.0, 0.0
    ).astype(jnp.bfloat16)
    place[...] = jnp.dot(route, pick, preferred_element_type=jnp.float32).astype(jnp.bfloat16)

    tq = min(tok, 256)
    scale = HD ** (-0.5) * math.log2(math.e)

    def attend(dist, h):
        for q0 in range(0, tok, tq):
            r = pl.ds(q0, tq)
            low = max(0, q0 + dist * tok - WINDOW + 1) // 128 * 128
            keys = slice(low, tok if dist else q0 + tq)
            s = lax.dot_general(
                qbuf[h, r, :],
                kbuf[dist, keys],
                (((1,), (1,)), ((), ())),
                preferred_element_type=jnp.float32,
            )
            if dist == 0 or (dist + 1) * tok - 1 >= WINDOW:
                qi = q0 + lax.broadcasted_iota(jnp.int32, s.shape, 0)
                kj = lax.broadcasted_iota(jnp.int32, s.shape, 1) + (low - dist * tok)
                s = jnp.where((kj <= qi) & (kj > qi - WINDOW), s, NEG)
            top = jnp.max(s, axis=1, keepdims=True)
            if dist > 0:
                old = mbuf[h, r, :]
                top = jnp.maximum(top, old)
            e = jnp.exp2(s * scale - top * scale)
            total = jnp.sum(e, axis=1, keepdims=True)
            o = jnp.dot(e.astype(jnp.bfloat16), vbuf[dist, keys], preferred_element_type=jnp.float32)
            if dist > 0:
                fade = jnp.exp2((old - top) * scale)
                total = total + fade * lbuf[h, r, :]
                o = o + fade * obuf[h, r, :]
            mbuf[h, r, :] = top
            lbuf[h, r, :] = total
            obuf[h, r, :] = o

    def own_block(h, also=None):
        if also is not None:
            pl.when(also)(lambda: own_block(h))
            return
        w = jnp.concatenate([wbuf[h, j] for j in range(3)], axis=1)
        got = jnp.dot(normed[...], w, preferred_element_type=jnp.float32).astype(jnp.bfloat16)
        qbuf[h] = got[:, :HD]
        kbuf[0] = got[:, HD : 2 * HD]
        vbuf[0] = got[:, 2 * HD :]
        attend(0, h)

    def earlier_block(h, dist, also=True):
        @pl.when((z >= dist) & also)
        def _():
            w = jnp.concatenate([wbuf[h, j] for j in range(1, 3)], axis=1)
            rows_in = jnp.concatenate([halo[dist - 1, q] for q in range(n_phase)], axis=1)
            got = jnp.dot(rows_in, w, preferred_element_type=jnp.float32).astype(jnp.bfloat16)
            kbuf[dist] = got[:, :HD]
            vbuf[dist] = got[:, HD:]
            attend(dist, h)

    def split_rows(dist):
        if dist == 0:
            return normed[:, :rows], normed[:, rows:]
        pieces = [halo[dist - 1, q] for q in range(n_phase)]
        return pieces[0], jnp.concatenate(pieces[1:], axis=1)

    def some_weights(dist, r):
        return jnp.concatenate([wbuf[last, j, r, :] for j in range(min(dist, 1), 3)], axis=1)

    def project_early(dist, also):
        @pl.when((z >= dist) & also)
        def _():
            got = jnp.dot(
                split_rows(dist)[1], some_weights(dist, slice(rows, None)), preferred_element_type=jnp.float32
            )
            partial[dist, :, pl.ds(min(dist, 1) * HD, got.shape[1])] = got

    def project_late(dist, also):
        @pl.when((z >= dist) & also)
        def _():
            got = jnp.dot(
                split_rows(dist)[0], some_weights(dist, slice(0, rows)), preferred_element_type=jnp.float32
            )
            start = min(dist, 1) * HD
            got = (got + partial[dist, :, pl.ds(start, got.shape[1])]).astype(jnp.bfloat16)
            if dist == 0:
                qbuf[last] = got[:, :HD]
            kbuf[dist] = got[:, HD - start : 2 * HD - start]
            vbuf[dist] = got[:, 2 * HD - start :]
            attend(dist, last)

    def close(h):
        at = slice(h * HD, (h + 1) * HD)
        res = xbuf[:, pl.ds(pl.multiple_of(p * width + h * HD, HD), HD)].astype(jnp.float32)
        att = (obuf[h] / lbuf[h]).astype(jnp.bfloat16).astype(jnp.float32)
        states = (res + att).astype(jnp.bfloat16)
        bs_ref[:, at] = states
        routed = jnp.dot(place[...], states, preferred_element_type=jnp.float32).astype(jnp.bfloat16)
        for s in range(n_seq):
            outrows[h, s] = routed[s * slot : (s + 1) * slot]
        arrived[h, p, z] = outrows[h, z]
        rows_out(h, False)

    def rows_out(h, held):
        for k in range(1, n_seq):
            other = lax.rem(z + k, n_seq)
            wait = (other > z) & (other >= n_seq - 2)
            send(
                outrows.at[h, other],
                arrived.at[h, p, z],
                row_send,
                row_recv.at[h, jnp.maximum(z - (n_seq - 3), 0)],
                {"seq": other},
                wait if held else jnp.logical_not(wait),
            )

    outer = n_seq - 2

    def rows_in(h, j, cond):
        if j == 0:
            landed(arrived.at[h, p, pl.ds(0, outer)], row_recv.at[h, 0], cond & (z >= outer))
            landed(arrived.at[h, p, pl.ds(0, outer - 1)], row_recv.at[h, 0], cond & (z < outer))
        else:
            src = outer + j - 1
            landed(arrived.at[h, p, src], row_recv.at[h, j], cond & (z != src))

    def spread(h, j, cond, waited=False):
        if not waited:
            rows_in(h, j, cond)
        piece = arrived.at[h, p, pl.ds(0, outer) if j == 0 else pl.ds(outer + j - 1, 1)]
        group = 1 + j // 2 if h == last else 0
        for k in range(1, n_phase):
            send(piece, piece, all_send, all_recv.at[group], {"phase": lax.rem(p + k, n_phase)}, cond)

    for h in range(1, heads):
        relay(h, 1, LEFTWARD)
    halo_spread(1)
    landed(upbuf.at[pl.ds(0, n_phase - 1), up_half], up_recv)
    for k in range(1, n_phase):
        piece = upbuf.at[lax.rem(p + n_phase - k, n_phase), up_half]
        send(piece, piece, upp_send, upp_recv, twin_core)
    for h in range(1, heads):
        issue_own(h, RIGHTWARD, second)
        relay(h, 1, RIGHTWARD, second)
    relay(0, 2, RIGHTWARD)
    issue_own(1, RIGHTWARD, z > 1)
    for t in range(2, n_seq):
        for h in range(heads):
            relay(h, t, LEFTWARD)
    for dist in range(2, reach + 1):
        halo_pass(dist - 1)
        halo_spread(dist)
    for t in range(3, n_seq):
        relay(0, t, RIGHTWARD)
    finish(0)
    own_block(0)
    relay(1, 1, RIGHTWARD, (z > 1) & (z < n_seq - 1))
    relay(1, 2, RIGHTWARD, z < n_seq - 1)
    issue_own(2, RIGHTWARD, z > 1)
    for dist in range(1, reach):
        halo_wait(dist)
        earlier_block(0, dist)
    relay(1, 1, RIGHTWARD, final)
    relay(1, 2, RIGHTWARD, final)
    halo_pass(reach, final)
    for t in range(3, n_seq):
        relay(1, t, RIGHTWARD)
    finish(1)
    own_block(1)
    relay(2, 1, RIGHTWARD, (z > 1) & (z < n_seq - 1))
    for dist in range(1, reach):
        earlier_block(1, dist)
    halo_pass(reach, z < n_seq - 1)
    relay(2, 1, RIGHTWARD, final)
    relay(2, 2, RIGHTWARD, z < n_seq - 1)
    inner = z < n_seq - 1
    finish(last, False, inner)
    finish(last, True, inner)
    own_block(last, inner)
    for dist in range(1, reach):
        earlier_block(last, dist, inner)
    halo_wait(reach)
    outside = z < outer
    for h in range(last):
        earlier_block(h, reach)
        if h == last - 1:
            for t in range(3, n_seq):
                relay(last, t, RIGHTWARD, c == 1)
        close(h)
        if h == 0:
            relay(last, 2, RIGHTWARD, final)
    for h in range(last):
        spread(h, 2, final)
    finish(last, False, final)
    for dist in range(reach):
        project_early(dist, final)
    for t in range(3, n_seq):
        relay(last, t, RIGHTWARD, c == 0)
    project_early(reach, final)
    finish(last, True, final)
    for dist in range(reach + 1):
        project_late(dist, final)
        if dist == 0:
            for h in range(last):
                spread(h, 1, final)
    for h in range(last):
        spread(h, 1, z == outer)
    rows_in(0, 2, z == outer)
    for h in range(last):
        pl.when(z == outer)(lambda h=h: rows_out(h, True))
    earlier_block(last, reach, inner)
    close(last)
    pl.when(z == outer)(lambda: rows_out(last, True))
    spread(last, 1, z == outer)
    spread(last, 2, final)
    for h in range(heads):
        spread(h, 0, outside)
    rows_in(0, 2, outside)
    for h in range(heads):
        pl.when(outside)(lambda h=h: rows_out(h, True))
    spread(0, 1, outside)
    spread(0, 2, inner, waited=True)
    for h in range(1, last):
        spread(h, 1, outside)
        spread(h, 2, inner)
    for h in range(heads):
        spread(h, 0, z >= outer)
    spread(last, 1, z != outer)
    own_up.wait()
    landed(upbuf.at[pl.ds(0, n_phase - 1), up_half], upp_recv)
    landed(arrived.at[pl.ds(0, last), pl.ds(0, n_phase - 1)], all_recv.at[0])
    full = n_seq * slot
    cut = full - slot

    def rows_of(s, hs):
        return jnp.concatenate([arrived[h, s].reshape(full, HD) for h in hs], axis=1)

    for k in range(n_phase):
        s = lax.rem(p + n_phase - k, n_phase)
        acc[k] = jnp.dot(
            rows_of(s, range(last)), upbuf[s, : last * HD, :], preferred_element_type=jnp.float32
        )

    def complete(j):
        r = slice(0, cut) if j == 0 else slice(cut, full)
        projected = 0.0
        for k in range(n_phase):
            s = lax.rem(p + n_phase - k, n_phase)
            srcs = pl.ds(0, n_seq - 1) if j == 0 else pl.ds(n_seq - 1, 1)
            lhs = arrived[last, s, srcs].reshape(r.stop - r.start, HD)
            got = acc[k, r, :] + jnp.dot(lhs, upbuf[s, last * HD :, :], preferred_element_type=jnp.float32)
            projected = projected + got.astype(jnp.bfloat16).astype(jnp.float32)
        acc[0, r, :] = projected
        sq = jnp.sum(projected * projected, axis=1, keepdims=True)
        return jnp.broadcast_to(sq, (r.stop - r.start, 128))

    landed(arrived.at[last, pl.ds(0, n_phase - 1), pl.ds(0, n_seq - 1)], all_recv.at[1])
    sq_top = complete(0)
    spread(last, 2, inner)
    landed(arrived.at[last, pl.ds(0, n_phase - 1), pl.ds(0, 1)], all_recv.at[2])
    sq_all = jnp.concatenate([sq_top, complete(1)], axis=0)
    sqbuf[p] = sq_all.T[0:8, :]
    for k in range(1, n_phase):
        send(sqbuf.at[p], sqbuf.at[p], sq_send, sq_recv, {"phase": lax.rem(p + k, n_phase)})
    landed(sqbuf.at[pl.ds(0, n_phase - 1)], sq_recv)
    all_sq = sqbuf[0]
    for k in range(1, n_phase):
        all_sq = all_sq + sqbuf[k]
    all_sq = jnp.broadcast_to(all_sq[0:1, :], (128, full)).T[:, 0:1]
    norm = lax.rsqrt(all_sq / (n_phase * cols) + 1e-05)
    ss_ref[...] = (acc[0] * norm * og[...]).astype(jnp.bfloat16)
    sent(wbuf.at[:, :, pl.ds(0, half)], w_send, first | final)
    sent(wbuf.at[:, :, pl.ds(0, (n_seq + 1) * half)], w_send, jnp.logical_not(first | final))
    sent(wbuf.at[:, :, pl.ds(0, (n_seq - 1) * half)], p_send)
    sent(upbuf.at[pl.ds(0, n_phase - 1), up_half], up_send)
    sent(upbuf.at[pl.ds(0, n_phase - 1), up_half], upp_send)
    for dist in range(1, reach + 1):
        sent(halo.at[dist - 1, 0], h_send.at[dist - 1], (z >= dist - 1) & has_right)
        sent(halo.at[dist - 1, pl.ds(0, 3)], g_send.at[dist - 1], z >= dist)
    sent(outrows.at[:, pl.ds(0, n_seq - 1)], row_send)
    sent(arrived.at[:, pl.ds(0, n_phase - 1)], all_send)
    sent(sqbuf.at[pl.ds(0, n_phase - 1)], sq_send)


def fused(n_seq, n_phase, byte_embed, in_gain, w_qkv, w_up, out_gain, bounds, owner):
    tok, d = byte_embed.shape
    rows, _, width = w_qkv.shape
    heads = width // HD
    crows = bounds.shape[0]
    cols = out_gain.shape[0]
    slot = 2 * crows // n_seq
    reach = -(-WINDOW // tok)
    bf, f32 = jnp.bfloat16, jnp.float32
    vmem = pl.BlockSpec(memory_space=pltpu.VMEM)
    hbm = pl.BlockSpec(memory_space=pltpu.HBM)
    dma = pltpu.SemaphoreType.DMA
    in_hbm = lambda a: pltpu.with_memory_space_constraint(a, pltpu.HBM)
    states, stretch = pl.pallas_call(
        functools.partial(fused_kernel, (n_seq, n_phase, reach, slot)),
        out_shape=(
            jax.ShapeDtypeStruct((tok, width), bf),
            jax.ShapeDtypeStruct((n_seq * slot, cols), bf),
        ),
        in_specs=[hbm] * 7,
        out_specs=(vmem, vmem),
        scratch_shapes=[
            pltpu.VMEM((tok, d), bf),
            pltpu.VMEM((1, d), f32),
            pltpu.VMEM((1, cols), f32),
            pltpu.VMEM((1, crows), jnp.int32),
            pltpu.VMEM((1, crows), jnp.int32),
            pltpu.VMEM((tok, d), bf),
            pltpu.VMEM((reach, n_phase, tok, width), bf),
            pltpu.VMEM((heads, 3, n_seq * rows, HD), bf),
            pltpu.VMEM((n_phase, w_up.shape[0], cols), bf),
            pltpu.VMEM((heads, tok, HD), bf),
            pltpu.VMEM((reach + 1, tok, HD), bf),
            pltpu.VMEM((reach + 1, tok, HD), bf),
            pltpu.VMEM((heads, tok, HD), f32),
            pltpu.VMEM((heads, tok, 1), f32),
            pltpu.VMEM((heads, tok, 1), f32),
            pltpu.VMEM((n_seq * slot, tok), bf),
            pltpu.VMEM((heads, n_seq, slot, HD), bf),
            pltpu.VMEM((heads, n_phase, n_seq, slot, HD), bf),
            pltpu.VMEM((n_phase, n_seq * slot, cols), f32),
            pltpu.VMEM((reach + 1, tok, 3 * HD), f32),
            pltpu.VMEM((n_phase, 8, n_seq * slot), f32),
            dma((6 + heads,)),
            dma(()),
            dma((heads, n_seq - 1)),
            dma(()),
            dma((heads + 1,)),
            dma(()),
            dma(()),
            dma(()),
            dma(()),
            dma((reach,)),
            dma((reach,)),
            dma((reach,)),
            dma((reach, 3)),
            dma(()),
            dma((heads, 3)),
            dma(()),
            dma((3,)),
            dma(()),
            dma(()),
        ],
        compiler_params=pltpu.CompilerParams(
            collective_id=0, has_side_effects=True, vmem_limit_bytes=48 * 1024 * 1024
        ),
    )(
        in_hbm(byte_embed),
        in_hbm(in_gain),
        in_hbm(jnp.transpose(w_qkv, (1, 0, 2))),
        in_hbm(w_up),
        in_hbm(out_gain),
        in_hbm(bounds.reshape(1, crows)),
        in_hbm(owner.reshape(1, crows)),
    )
    return states, stretch


def passed_along(value, axis, by):
    devices = lax.axis_size(axis)
    pairs = [(i, i + by) for i in range(devices) if 0 <= i + by < devices]
    return lax.ppermute(value, axis, pairs)


def project_rows(rows, w_up, out_gain):
    groups = lax.axis_size("phase")
    full_rows = lax.all_gather(rows, "phase", axis=1, tiled=True)
    w_cols = lax.all_to_all(w_up, "phase", split_axis=1, concat_axis=0, tiled=True)
    count = full_rows.shape[0]
    width = rows.shape[1]
    columns = w_cols.shape[1]
    pieces = jnp.einsum(
        "nsg,sgc->snc",
        full_rows.reshape(count, groups, width),
        w_cols.reshape(groups, width, columns),
        preferred_element_type=jnp.float32,
    )
    projected = jnp.sum(pieces.astype(jnp.bfloat16).astype(jnp.float32), axis=0)
    squares = lax.psum(jnp.sum(projected * projected, axis=1), "phase")
    scale = lax.rsqrt(squares / DC + 1e-05)
    return (projected * scale[:, None] * out_gain).astype(jnp.bfloat16)


def on_device(byte_embed, in_gain, w_qkv, w_up, out_gain, bounds, owner):
    tok = byte_embed.shape[0]
    n_seq = lax.axis_size("seq")
    mine = lax.axis_index("seq")
    section = lax.axis_index("phase")
    width_dev = w_qkv.shape[2]
    heads_dev = width_dev // HD
    x32 = byte_embed.astype(jnp.float32)
    normed = (x32 * lax.rsqrt(jnp.mean(x32 * x32, axis=1, keepdims=True) + 1e-05) * in_gain).astype(
        jnp.bfloat16
    )
    piece = lax.all_gather(w_qkv, "seq", axis=0, tiled=True)
    qkv = jnp.dot(
        normed, piece.reshape(piece.shape[0], 3 * width_dev), preferred_element_type=jnp.float32
    ).astype(jnp.bfloat16)
    qkv = qkv.reshape(tok, 3, heads_dev, HD)
    query = qkv[:, 0]
    keys = qkv[:, 1]
    values = qkv[:, 2]
    reach = -(-WINDOW // tok)
    key_list = [keys]
    value_list = [values]
    for distance in range(1, reach + 1):
        earlier_keys, earlier_values = passed_along((keys, values), "seq", distance)
        key_list = [earlier_keys] + key_list
        value_list = [earlier_values] + value_list
    key_all = jnp.concatenate(key_list, axis=0)
    value_all = jnp.concatenate(value_list, axis=0)
    scores = jnp.einsum(
        "ihd,jhd->hij", query, key_all, preferred_element_type=jnp.float32
    ) * HD ** (-0.5)
    q_pos = mine * tok + jnp.arange(tok, dtype=jnp.int32)
    k_pos = mine * tok - reach * tok + jnp.arange((reach + 1) * tok, dtype=jnp.int32)
    keep = (
        (k_pos[None, :] <= q_pos[:, None])
        & (k_pos[None, :] > q_pos[:, None] - WINDOW)
        & (k_pos[None, :] >= 0)
    )
    scores = jnp.where(keep[None], scores, -jnp.inf)
    top = jnp.max(scores, axis=2, keepdims=True)
    expo = jnp.exp(scores - top)
    probs = (expo / jnp.sum(expo, axis=2, keepdims=True)).astype(jnp.bfloat16)
    attended = jnp.einsum(
        "hij,jhd->ihd", probs, value_all, preferred_element_type=jnp.float32
    ).astype(jnp.bfloat16)
    attended = attended.reshape(tok, width_dev)
    residual = lax.dynamic_slice_in_dim(x32, section * width_dev, width_dev, 1)
    byte_states = (residual + attended.astype(jnp.float32)).astype(jnp.bfloat16)
    local = bounds - mine * tok
    stretch_rows = jnp.take(byte_states, local, axis=0)
    owners = owner[:, 0]
    crows = owners.shape[0]
    slot_count = 2 * crows // n_seq
    place = jnp.arange(crows, dtype=jnp.int32)
    earlier = (owners[:, None] == owners[None, :]) & (place[None, :] < place[:, None])
    rank = jnp.sum(earlier.astype(jnp.int32), axis=1)
    target = owners * slot_count + rank
    placing = (target[None, :] == jnp.arange(n_seq * slot_count, dtype=jnp.int32)[:, None]).astype(
        jnp.bfloat16
    )
    outgoing = jnp.dot(placing, stretch_rows, preferred_element_type=jnp.float32).astype(
        jnp.bfloat16
    )
    outgoing = outgoing.reshape(n_seq, slot_count, width_dev)
    arrived = lax.all_to_all(outgoing, "seq", split_axis=0, concat_axis=0, tiled=True).reshape(
        n_seq * slot_count, width_dev
    )
    stretch_states = project_rows(arrived, w_up, out_gain)
    return (byte_states, stretch_states)


def solution(mesh):
    n_seq, n_phase, n_dp = (mesh.shape[axis] for axis in ("seq", "phase", "dp"))

    def body(byte_embed, in_gain, w_qkv, *rest):
        tok, (rows, _, width) = byte_embed.shape[0], w_qkv.shape
        slot = 2 * rest[2].shape[0] // n_seq
        tiled = rows % 128 == 0 and width % HD == 0 and tok % 256 == 0 and slot % 16 == 0
        fits = n_seq == n_phase and width == 3 * HD and WINDOW == 2 * tok
        if tiled and fits and n_dp == 2 and n_phase == 4 and w_qkv.shape[0] == rest[0].shape[0]:
            return fused(n_seq, n_phase, byte_embed, in_gain, w_qkv, *rest)
        return on_device(byte_embed, in_gain, w_qkv, *rest)

    return jax.shard_map(
        body,
        mesh=mesh,
        in_specs=(
            P(("dp", "seq"), None),
            P(),
            P("seq", None, "phase"),
            P("phase", None),
            P("phase"),
            P(("dp", "seq")),
            P(("dp", "seq"), None),
        ),
        out_specs=(P(("dp", "seq"), "phase"), P(("dp", "seq"), "phase")),
        check_vma=False,
    )
```

```python
import functools
import math
import jax
import jax.numpy as jnp
from jax import lax
from jax.experimental import pallas as pl
from jax.experimental.pallas import tpu as pltpu
from jax.sharding import PartitionSpec as P

DC = 3072
HD = 128
WINDOW = 1024
MESH = pl.DeviceIdType.MESH
NEG = -0.7 * 3.4e38


def fused_kernel(
    dims,
    x_ref,
    gain_ref,
    w_ref,
    up_ref,
    og_ref,
    bounds_ref,
    owner_ref,
    bs_ref,
    ss_ref,
    xbuf,
    gain,
    og,
    bnd,
    own,
    normed,
    halo,
    wbuf,
    upbuf,
    qbuf,
    kbuf,
    vbuf,
    place,
    outrows,
    arrived,
    acc,
    partial,
    sqbuf,
    loc_sem,
    w_send,
    w_recv,
    p_send,
    p_recv,
    up_send,
    up_recv,
    upp_send,
    upp_recv,
    h_send,
    h_recv,
    g_send,
    g_recv,
    row_send,
    row_recv,
    all_send,
    all_recv,
    sq_send,
    sq_recv,
    go,
):
    n_seq, n_phase, reach, slot = dims
    tok, d = xbuf.shape
    rows, width = w_ref.shape[1:]
    half = rows // 2
    heads = width // HD
    last = heads - 1
    crows = bnd.shape[1]
    cols = og.shape[1]
    z = lax.axis_index("seq")
    p = lax.axis_index("phase")
    c = lax.axis_index("dp")

    own_x = pltpu.make_async_copy(x_ref, xbuf, loc_sem.at[0])
    own_x.start()
    small = []
    for i, (src, dst) in enumerate(
        ((gain_ref, gain.at[0]), (bounds_ref, bnd), (owner_ref, own), (og_ref, og.at[0]))
    ):
        small.append(pltpu.make_async_copy(src, dst, loc_sem.at[2 + heads + i]))
        small[i].start()

    twin_core = {"dp": 1 - c}
    peers = (
        [{"seq": lax.rem(z + k, n_seq)} for k in range(1, n_seq)]
        + [{"phase": lax.rem(p + k, n_phase)} for k in range(1, n_phase)]
        + [twin_core]
    )
    barrier = pltpu.get_barrier_semaphore()
    for peer in peers:
        pl.semaphore_signal(barrier, inc=1, device_id=peer, device_id_type=MESH)

    own_w = []
    for h in range(heads):
        own_w.append(
            pltpu.make_async_copy(
                w_ref.at[:, :, pl.ds(h * HD, HD)],
                wbuf.at[h, :, pl.ds(pl.multiple_of(z * rows, rows), rows), :],
                loc_sem.at[2 + h],
            )
        )
        own_w[h].start()
    own_up = pltpu.make_async_copy(
        up_ref.at[:, pl.ds(pl.multiple_of(p * cols, 128), cols)], upbuf.at[p], loc_sem.at[1]
    )
    own_up.start()
    pl.semaphore_wait(barrier, len(peers))

    def when(cond, action):
        if cond is None:
            action()
        else:
            pl.when(cond)(action)

    def move(src, dst, ssem, rsem, peer):
        return pltpu.make_async_remote_copy(
            src_ref=src, dst_ref=dst, send_sem=ssem, recv_sem=rsem, device_id=peer, device_id_type=MESH
        )

    def send(src, dst, ssem, rsem, peer, cond=None):
        copy = move(src, dst, ssem, rsem, peer)
        when(cond, copy.start)
        return copy

    def sent(ref, ssem, cond=None):
        when(cond, move(ref, ref, ssem, ssem, twin_core).wait_send)

    def landed(ref, rsem, cond=None):
        when(cond, move(ref, ref, rsem, rsem, twin_core).wait_recv)

    right, left = {"seq": z + 1}, {"seq": z - 1}
    has_right, has_left = z < n_seq - 1, z > 0
    ways = ((right, has_right, -1), (left, has_left, 1))
    RIGHTWARD, LEFTWARD = 0, 1

    def chunk(h, shard):
        at = pl.multiple_of(shard * rows + c * half, half)
        return wbuf.at[h, :, pl.ds(at, half), :]

    def slot_of(t, way):
        return t - 1 if way == LEFTWARD else n_seq - t - 1

    def issue_own(h, way, also=None):
        src = chunk(h, z)
        peer, cond, sign = ways[way]
        cond = cond if also is None else cond & also
        send(src, chunk(h, z), w_send, w_recv.at[h, slot_of(1, way)], peer, cond)

    def relay(h, t, way, also=None):
        if t >= n_seq:
            return
        peer, cond, sign = ways[way]
        shard = z + sign * t
        here = (shard >= 0) & (shard < n_seq)
        there = here if also is None else here & also
        piece = chunk(h, jnp.clip(shard, 0, n_seq - 1))
        landed(piece, w_recv.at[h, slot_of(t, way)], there)
        if t < n_seq - 1:
            send(piece, piece, w_send, w_recv.at[h, slot_of(t + 1, way)], peer, there & cond)
        late = (way == RIGHTWARD) & (t == z)
        group = jnp.where(late, last + 1, h) if h == last else h
        send(piece, piece, p_send, p_recv.at[group], twin_core, there)

    def finish(h, late=None, also=True):
        if h < last:
            landed(wbuf.at[h, :, pl.ds(0, (n_seq - 1) * half)], p_recv.at[h])
        elif late:
            landed(wbuf.at[h, :, pl.ds(0, half)], p_recv.at[last + 1], (z > 0) & also)
        else:
            landed(wbuf.at[h, :, pl.ds(0, (n_seq - 2) * half)], p_recv.at[h], (z > 0) & also)
            landed(wbuf.at[h, :, pl.ds(0, (n_seq - 1) * half)], p_recv.at[h], (z == 0) & also)

    across = {1: {"phase": p + 1 - 2 * lax.rem(p, 2)}, 2: {"phase": lax.rem(p + 2, n_phase)}}
    spots = {k: v["phase"] for k, v in across.items()}
    mine = {}

    def halo_start(dist, cond):
        own_part = normed.at[:, pl.ds(pl.multiple_of(p * width, 128), width)]
        src = own_part if dist == 1 else halo.at[dist - 2, p]
        mine[dist] = send(src, halo.at[dist - 1, p], h_send.at[dist - 1], h_recv.at[dist - 1], right, cond)

    gathers = {}

    def halo_spread(dist):
        there = z >= dist
        pl.when(there)(mine[dist].wait_recv)
        if dist < reach:
            halo_start(dist + 1, there & has_right)
        for k in (1, 2):
            piece = halo.at[dist - 1, p]
            gathers[dist, k] = send(
                piece, piece, g_send.at[dist - 1], g_recv.at[dist - 1, k - 1], across[k], there
            )

    def halo_pass(dist, also=None):
        there = z >= dist
        if also is not None:
            there = there & also
        for k in (1, 2):
            pl.when(there)(gathers[dist, k].wait_recv)
            part = pl.ds((k - 1) * (tok // 2), tok // 2)
            piece = halo.at[dist - 1, spots[k], part]
            gathers[dist, 2 + k] = send(
                piece, piece, g_send.at[dist - 1], g_recv.at[dist - 1, 2], across[3 - k], there
            )

    def halo_wait(dist):
        @pl.when(z >= dist)
        def _():
            landed(halo.at[dist - 1, 0], g_recv.at[dist - 1, 2])

    own_w[0].wait()
    issue_own(0, RIGHTWARD)
    issue_own(0, LEFTWARD)
    for h in range(1, heads):
        own_w[h].wait()
        issue_own(h, LEFTWARD)
    up_rows = up_ref.shape[0] // 2
    up_half = pl.ds(pl.multiple_of(c * up_rows, up_rows), up_rows)
    for k in range(1, n_phase):
        other = lax.rem(p + k, n_phase)
        part = pl.ds(pl.multiple_of(other * cols, 128), cols)
        send(up_ref.at[up_half, part], upbuf.at[p, up_half], up_send, up_recv, {"phase": other})

    own_x.wait()
    small[0].wait()
    step_rows = 64


    @pl.loop(0, tok // step_rows)
    def _(i):
        r = pl.ds(pl.multiple_of(i * step_rows, step_rows), step_rows)
        xx = xbuf[r, :].astype(jnp.float32)
        scale = lax.rsqrt(jnp.mean(xx * xx, axis=1, keepdims=True) + 1e-05)
        normed[r, :] = (xx * scale * gain[...]).astype(jnp.bfloat16)

    halo_start(1, has_right)
    first, second, final = z == 0, z == 1, z == n_seq - 1
    for h in range(1, heads):
        issue_own(h, RIGHTWARD, first)

    def column(ref):
        wide = jnp.broadcast_to(ref[...].astype(jnp.float32), (crows, crows))
        return wide.T

    relay(0, 1, RIGHTWARD)
    relay(0, 1, LEFTWARD)
    for copy in small[1:]:
        copy.wait()
    local = column(bnd)[:, 0:1] - (z * tok).astype(jnp.float32)
    spot = lax.broadcasted_iota(jnp.int32, (crows, tok), 1).astype(jnp.float32)
    pick = jnp.where(local == spot, 1.0, 0.0).astype(jnp.bfloat16)
    same = column(own) == own[...].astype(jnp.float32)
    before = lax.broadcasted_iota(jnp.int32, (crows, crows), 0) < lax.broadcasted_iota(
        jnp.int32, (crows, crows), 1
    )
    rank = jnp.sum(jnp.where(same & before, 1, 0), axis=0, keepdims=True)
    target = own[...] * slot + rank
    route = jnp.where(
        target == lax.broadcasted_iota(jnp.int32, (n_seq * slot, crows), 0), 1.0, 0.0
    ).astype(jnp.bfloat16)
    place[...] = jnp.dot(route, pick, preferred_element_type=jnp.float32).astype(jnp.bfloat16)

    tq = min(tok, 256)
    scale = HD ** (-0.5) * math.log2(math.e)

    def scores(h, r, q0, dist, k0, size):
        s = lax.dot_general(
            qbuf[h, r, :],
            kbuf[h, dist, k0 : k0 + size],
            (((1,), (1,)), ((), ())),
            preferred_element_type=jnp.float32,
        )
        ahead = k0 - dist * tok - q0
        if ahead + size - 1 > 0 or ahead - (tq - 1) <= -WINDOW:
            gap = lax.broadcasted_iota(jnp.int32, s.shape, 1) - lax.broadcasted_iota(jnp.int32, s.shape, 0)
            s = jnp.where((gap <= -ahead) & (gap > -ahead - WINDOW), s, NEG)
        return s

    def chunks(dist, q0, size=256):
        out = []
        for k0 in range(0, tok, size):
            ahead = k0 - dist * tok - q0
            if ahead - (tq - 1) <= 0 and ahead + size - 1 > -WINDOW:
                out.append((dist, k0, size))
        return out

    def attend(h, dists):
        tiles = []
        for q0 in range(0, tok, tq):
            r = pl.ds(q0, tq)
            where = [at for dist in dists for at in chunks(dist, q0)]
            tiles.append((r, where, [scores(h, r, q0, *at) for at in where]))
        for r, where, parts in tiles:
            top = jnp.max(functools.reduce(jnp.maximum, parts), axis=1, keepdims=True)
            low = top * scale
            es = [jnp.exp2(s * scale - low) for s in parts]
            total = jnp.sum(functools.reduce(jnp.add, es), axis=1, keepdims=True)
            e = jnp.concatenate([e.astype(jnp.bfloat16) for e in es], axis=1)
            v = jnp.concatenate([vbuf[h, dist, k0 : k0 + size] for dist, k0, size in where], axis=0)
            o = jnp.dot(e, v, preferred_element_type=jnp.float32)
            att = (o / total).astype(jnp.bfloat16).astype(jnp.float32)
            res = xbuf[r, pl.ds(pl.multiple_of(p * width + h * HD, HD), HD)].astype(jnp.float32)
            bs_ref[r, h * HD : (h + 1) * HD] = (res + att).astype(jnp.bfloat16)

    def store(h, dist, got):
        start = min(dist, 1) * HD
        if dist == 0:
            qbuf[h] = got[:, :HD]
        kbuf[h, dist] = got[:, HD - start : 2 * HD - start]
        vbuf[h, dist] = got[:, 2 * HD - start :]

    def project(h, dist, also=True):
        @pl.when((z >= dist) & also)
        def _():
            w = jnp.concatenate([wbuf[h, j] for j in range(min(dist, 1), 3)], axis=1)
            rows_in = (
                jnp.concatenate([halo[dist - 1, q] for q in range(n_phase)], axis=1)
                if dist
                else normed[...]
            )
            got = jnp.dot(rows_in, w, preferred_element_type=jnp.float32)
            store(h, dist, got.astype(jnp.bfloat16))

    def split_rows(dist):
        if dist == 0:
            return normed[:, :rows], normed[:, rows:]
        pieces = [halo[dist - 1, q] for q in range(n_phase)]
        return pieces[0], jnp.concatenate(pieces[1:], axis=1)

    def some_weights(dist, r):
        return jnp.concatenate([wbuf[last, j, r, :] for j in range(min(dist, 1), 3)], axis=1)

    def project_early(dist, also):
        @pl.when((z >= dist) & also)
        def _():
            got = jnp.dot(
                split_rows(dist)[1], some_weights(dist, slice(rows, None)), preferred_element_type=jnp.float32
            )
            partial[dist, :, pl.ds(min(dist, 1) * HD, got.shape[1])] = got

    def project_late(dist, also):
        @pl.when((z >= dist) & also)
        def _():
            got = jnp.dot(
                split_rows(dist)[0], some_weights(dist, slice(0, rows)), preferred_element_type=jnp.float32
            )
            start = min(dist, 1) * HD
            store(last, dist, (got + partial[dist, :, pl.ds(start, got.shape[1])]).astype(jnp.bfloat16))

    def close(h):
        for n in range(reach + 1):

            @pl.when(z == n if n < reach else z >= n)
            def _():
                attend(h, list(range(n, -1, -1)))

        states = bs_ref[:, h * HD : (h + 1) * HD]
        routed = jnp.dot(place[...], states, preferred_element_type=jnp.float32).astype(jnp.bfloat16)
        for s in range(n_seq):
            outrows[h, s] = routed[s * slot : (s + 1) * slot]
        arrived[h, p, z] = outrows[h, z]
        rows_out(h, False)

    outer = n_seq - 2

    def rows_out(h, held):
        for k in range(1, n_seq):
            other = lax.rem(z + k, n_seq)
            wait = (z < outer) & (other >= outer)
            send(
                outrows.at[h, other],
                arrived.at[h, p, z],
                row_send,
                row_recv.at[h, jnp.maximum(z - (n_seq - 3), 0)],
                {"seq": other},
                wait if held else jnp.logical_not(wait),
            )

    def rows_in(h, j, cond):
        if j == 0:
            landed(arrived.at[h, p, pl.ds(0, outer)], row_recv.at[h, 0], cond & (z >= outer))
            landed(arrived.at[h, p, pl.ds(0, outer - 1)], row_recv.at[h, 0], cond & (z < outer))
        else:
            src = outer + j - 1
            landed(arrived.at[h, p, src], row_recv.at[h, j], cond & (z != src))

    def spread(h, j, cond):
        rows_in(h, j, cond)
        piece = arrived.at[h, p, pl.ds(0, outer) if j == 0 else pl.ds(outer + j - 1, 1)]
        group = 1 + j // 2 if h == last else 0
        for k in range(1, n_phase):
            send(piece, piece, all_send, all_recv.at[group], {"phase": lax.rem(p + k, n_phase)}, cond)

    for h in range(1, heads):
        relay(h, 1, LEFTWARD)
    halo_spread(1)
    landed(upbuf.at[pl.ds(0, n_phase - 1), up_half], up_recv)
    for k in range(1, n_phase):
        piece = upbuf.at[lax.rem(p + n_phase - k, n_phase), up_half]
        send(piece, piece, upp_send, upp_recv, twin_core)
    for h in range(1, heads):
        issue_own(h, RIGHTWARD, second)
        relay(h, 1, RIGHTWARD, second)
    relay(0, 2, RIGHTWARD)
    issue_own(1, RIGHTWARD, z > 1)
    for t in range(2, n_seq):
        for h in range(heads):
            relay(h, t, LEFTWARD)
    for dist in range(2, reach + 1):
        halo_pass(dist - 1)
        halo_spread(dist)
    for t in range(3, n_seq):
        relay(0, t, RIGHTWARD)
    finish(0)
    project(0, 0)
    relay(1, 1, RIGHTWARD, (z > 1) & (z < n_seq - 1))
    relay(1, 2, RIGHTWARD, z < n_seq - 1)
    issue_own(2, RIGHTWARD, z > 1)
    for dist in range(1, reach):
        halo_wait(dist)
        project(0, dist)
    relay(1, 1, RIGHTWARD, final)
    relay(1, 2, RIGHTWARD, final)
    halo_pass(reach, final)
    for t in range(3, n_seq):
        relay(1, t, RIGHTWARD)
    finish(1)
    project(1, 0)
    relay(2, 1, RIGHTWARD, (z > 1) & (z < n_seq - 1))
    for dist in range(1, reach):
        project(1, dist)
    halo_pass(reach, z < n_seq - 1)
    relay(2, 1, RIGHTWARD, final)
    relay(2, 2, RIGHTWARD, z < n_seq - 1)
    inner = z < n_seq - 1
    finish(last, False, inner)
    finish(last, True, inner)
    project(last, 0, inner)
    for dist in range(1, reach):
        project(last, dist, inner)
    halo_wait(reach)
    outside = z < outer
    for h in range(last):
        project(h, reach)
        close(h)
        if h == 0:
            relay(last, 2, RIGHTWARD, final)

            @pl.when(final)
            def _():
                for far in range(outer):
                    pl.semaphore_signal(go, inc=1, device_id={"seq": far}, device_id_type=MESH)

    for t in range(3, n_seq):
        relay(last, t, RIGHTWARD, c == 1)
    for h in range(last):
        spread(h, 2, final)
    finish(last, False, final)
    project_early(0, final)
    for t in range(3, n_seq):
        relay(last, t, RIGHTWARD, c == 0)
    for dist in range(1, reach + 1):
        project_early(dist, final)
    for h in range(last):
        spread(h, 1, final)
    finish(last, True, final)
    for dist in range(reach + 1):
        project_late(dist, final)
    for h in range(last):
        spread(h, 1, z == outer)
    project(last, reach, inner)
    close(last)
    spread(last, 1, z == outer)
    spread(last, 2, final)
    for h in range(heads):
        spread(h, 0, final)
    for h in range(heads):
        spread(h, 0, outside)

    @pl.when(outside)
    def _():
        pl.semaphore_wait(go, 1)
        for h in range(heads):
            rows_out(h, True)

    for h in range(last):
        spread(h, 1, outside)
        spread(h, 2, inner)
    for h in range(heads):
        spread(h, 0, z == outer)
    spread(last, 1, z != outer)
    own_up.wait()
    landed(upbuf.at[pl.ds(0, n_phase - 1), up_half], upp_recv)
    landed(arrived.at[pl.ds(0, last), pl.ds(0, n_phase - 1)], all_recv.at[0])
    full = n_seq * slot
    cut = full - slot

    def rows_of(s, hs):
        return jnp.concatenate([arrived[h, s].reshape(full, HD) for h in hs], axis=1)

    for k in range(n_phase):
        s = lax.rem(p + n_phase - k, n_phase)
        acc[k] = jnp.dot(
            rows_of(s, range(last)), upbuf[s, : last * HD, :], preferred_element_type=jnp.float32
        )

    def complete(j):
        r = slice(0, cut) if j == 0 else slice(cut, full)
        projected = 0.0
        for k in range(n_phase):
            s = lax.rem(p + n_phase - k, n_phase)
            srcs = pl.ds(0, n_seq - 1) if j == 0 else pl.ds(n_seq - 1, 1)
            lhs = arrived[last, s, srcs].reshape(r.stop - r.start, HD)
            got = acc[k, r, :] + jnp.dot(lhs, upbuf[s, last * HD :, :], preferred_element_type=jnp.float32)
            projected = projected + got.astype(jnp.bfloat16).astype(jnp.float32)
        acc[0, r, :] = projected
        sq = jnp.sum(projected * projected, axis=1, keepdims=True)
        return jnp.broadcast_to(sq, (r.stop - r.start, 128))

    spread(last, 2, inner)
    landed(arrived.at[last, pl.ds(0, n_phase - 1), pl.ds(0, n_seq - 1)], all_recv.at[1])
    sq_top = complete(0)
    landed(arrived.at[last, pl.ds(0, n_phase - 1), pl.ds(0, 1)], all_recv.at[2])
    sq_all = jnp.concatenate([sq_top, complete(1)], axis=0)
    sqbuf[p] = sq_all.T[0:8, :]
    for k in range(1, n_phase):
        send(sqbuf.at[p], sqbuf.at[p], sq_send, sq_recv, {"phase": lax.rem(p + k, n_phase)})
    landed(sqbuf.at[pl.ds(0, n_phase - 1)], sq_recv)
    all_sq = sqbuf[0]
    for k in range(1, n_phase):
        all_sq = all_sq + sqbuf[k]
    all_sq = jnp.broadcast_to(all_sq[0:1, :], (128, full)).T[:, 0:1]
    norm = lax.rsqrt(all_sq / (n_phase * cols) + 1e-05)
    ss_ref[...] = (acc[0] * norm * og[...]).astype(jnp.bfloat16)
    sent(wbuf.at[:, :, pl.ds(0, half)], w_send, first | final)
    sent(wbuf.at[:, :, pl.ds(0, (n_seq + 1) * half)], w_send, jnp.logical_not(first | final))
    sent(wbuf.at[:, :, pl.ds(0, (n_seq - 1) * half)], p_send)
    sent(upbuf.at[pl.ds(0, n_phase - 1), up_half], up_send)
    sent(upbuf.at[pl.ds(0, n_phase - 1), up_half], upp_send)
    for dist in range(1, reach + 1):
        sent(halo.at[dist - 1, 0], h_send.at[dist - 1], (z >= dist - 1) & has_right)
        sent(halo.at[dist - 1, pl.ds(0, 3)], g_send.at[dist - 1], z >= dist)
    sent(outrows.at[:, pl.ds(0, n_seq - 1)], row_send)
    sent(arrived.at[:, pl.ds(0, n_phase - 1)], all_send)
    sent(sqbuf.at[pl.ds(0, n_phase - 1)], sq_send)


def flush_kernel(a_ref, b_ref, a_out, b_out, sems):
    copies = [
        pltpu.make_async_copy(a_ref, a_out, sems.at[0]),
        pltpu.make_async_copy(b_ref, b_out, sems.at[1]),
    ]
    for copy in copies:
        copy.start()
    for copy in copies:
        copy.wait()


def fused(n_seq, n_phase, byte_embed, in_gain, w_qkv, w_up, out_gain, bounds, owner):
    tok, d = byte_embed.shape
    rows, _, width = w_qkv.shape
    heads = width // HD
    crows = bounds.shape[0]
    cols = out_gain.shape[0]
    slot = 2 * crows // n_seq
    reach = -(-WINDOW // tok)
    bf, f32 = jnp.bfloat16, jnp.float32
    vmem = pl.BlockSpec(memory_space=pltpu.VMEM)
    hbm = pl.BlockSpec(memory_space=pltpu.HBM)
    dma = pltpu.SemaphoreType.DMA
    in_hbm = lambda a: pltpu.with_memory_space_constraint(a, pltpu.HBM)
    states, stretch = pl.pallas_call(
        functools.partial(fused_kernel, (n_seq, n_phase, reach, slot)),
        out_shape=(
            jax.ShapeDtypeStruct((tok, width), bf),
            jax.ShapeDtypeStruct((n_seq * slot, cols), bf),
        ),
        in_specs=[hbm] * 7,
        out_specs=(vmem, vmem),
        scratch_shapes=[
            pltpu.VMEM((tok, d), bf),
            pltpu.VMEM((1, d), f32),
            pltpu.VMEM((1, cols), f32),
            pltpu.VMEM((1, crows), jnp.int32),
            pltpu.VMEM((1, crows), jnp.int32),
            pltpu.VMEM((tok, d), bf),
            pltpu.VMEM((reach, n_phase, tok, width), bf),
            pltpu.VMEM((heads, 3, n_seq * rows, HD), bf),
            pltpu.VMEM((n_phase, w_up.shape[0], cols), bf),
            pltpu.VMEM((heads, tok, HD), bf),
            pltpu.VMEM((heads, reach + 1, tok, HD), bf),
            pltpu.VMEM((heads, reach + 1, tok, HD), bf),
            pltpu.VMEM((n_seq * slot, tok), bf),
            pltpu.VMEM((heads, n_seq, slot, HD), bf),
            pltpu.VMEM((heads, n_phase, n_seq, slot, HD), bf),
            pltpu.VMEM((n_phase, n_seq * slot, cols), f32),
            pltpu.VMEM((reach + 1, tok, 3 * HD), f32),
            pltpu.VMEM((n_phase, 8, n_seq * slot), f32),
            dma((6 + heads,)),
            dma(()),
            dma((heads, n_seq - 1)),
            dma(()),
            dma((heads + 1,)),
            dma(()),
            dma(()),
            dma(()),
            dma(()),
            dma((reach,)),
            dma((reach,)),
            dma((reach,)),
            dma((reach, 3)),
            dma(()),
            dma((heads, 3)),
            dma(()),
            dma((3,)),
            dma(()),
            dma(()),
            pltpu.SemaphoreType.REGULAR,
        ],
        compiler_params=pltpu.CompilerParams(
            collective_id=0, has_side_effects=True, vmem_limit_bytes=48 * 1024 * 1024
        ),
    )(
        in_hbm(byte_embed),
        in_hbm(in_gain),
        in_hbm(jnp.transpose(w_qkv, (1, 0, 2))),
        in_hbm(w_up),
        in_hbm(out_gain),
        in_hbm(bounds.reshape(1, crows)),
        in_hbm(owner.reshape(1, crows)),
    )
    return pl.pallas_call(
        flush_kernel,
        out_shape=(
            jax.ShapeDtypeStruct(states.shape, bf),
            jax.ShapeDtypeStruct(stretch.shape, bf),
        ),
        in_specs=[vmem] * 2,
        out_specs=(hbm, hbm),
        scratch_shapes=[dma((2,))],
        compiler_params=pltpu.CompilerParams(vmem_limit_bytes=4 * 1024 * 1024),
    )(states, stretch)


def passed_along(value, axis, by):
    devices = lax.axis_size(axis)
    pairs = [(i, i + by) for i in range(devices) if 0 <= i + by < devices]
    return lax.ppermute(value, axis, pairs)


def project_rows(rows, w_up, out_gain):
    groups = lax.axis_size("phase")
    full_rows = lax.all_gather(rows, "phase", axis=1, tiled=True)
    w_cols = lax.all_to_all(w_up, "phase", split_axis=1, concat_axis=0, tiled=True)
    count = full_rows.shape[0]
    width = rows.shape[1]
    columns = w_cols.shape[1]
    pieces = jnp.einsum(
        "nsg,sgc->snc",
        full_rows.reshape(count, groups, width),
        w_cols.reshape(groups, width, columns),
        preferred_element_type=jnp.float32,
    )
    projected = jnp.sum(pieces.astype(jnp.bfloat16).astype(jnp.float32), axis=0)
    squares = lax.psum(jnp.sum(projected * projected, axis=1), "phase")
    scale = lax.rsqrt(squares / DC + 1e-05)
    return (projected * scale[:, None] * out_gain).astype(jnp.bfloat16)


def on_device(byte_embed, in_gain, w_qkv, w_up, out_gain, bounds, owner):
    tok = byte_embed.shape[0]
    n_seq = lax.axis_size("seq")
    mine = lax.axis_index("seq")
    section = lax.axis_index("phase")
    width_dev = w_qkv.shape[2]
    heads_dev = width_dev // HD
    x32 = byte_embed.astype(jnp.float32)
    normed = (x32 * lax.rsqrt(jnp.mean(x32 * x32, axis=1, keepdims=True) + 1e-05) * in_gain).astype(
        jnp.bfloat16
    )
    piece = lax.all_gather(w_qkv, "seq", axis=0, tiled=True)
    qkv = jnp.dot(
        normed, piece.reshape(piece.shape[0], 3 * width_dev), preferred_element_type=jnp.float32
    ).astype(jnp.bfloat16)
    qkv = qkv.reshape(tok, 3, heads_dev, HD)
    query = qkv[:, 0]
    keys = qkv[:, 1]
    values = qkv[:, 2]
    reach = -(-WINDOW // tok)
    key_list = [keys]
    value_list = [values]
    for distance in range(1, reach + 1):
        earlier_keys, earlier_values = passed_along((keys, values), "seq", distance)
        key_list = [earlier_keys] + key_list
        value_list = [earlier_values] + value_list
    key_all = jnp.concatenate(key_list, axis=0)
    value_all = jnp.concatenate(value_list, axis=0)
    scores = jnp.einsum(
        "ihd,jhd->hij", query, key_all, preferred_element_type=jnp.float32
    ) * HD ** (-0.5)
    q_pos = mine * tok + jnp.arange(tok, dtype=jnp.int32)
    k_pos = mine * tok - reach * tok + jnp.arange((reach + 1) * tok, dtype=jnp.int32)
    keep = (
        (k_pos[None, :] <= q_pos[:, None])
        & (k_pos[None, :] > q_pos[:, None] - WINDOW)
        & (k_pos[None, :] >= 0)
    )
    scores = jnp.where(keep[None], scores, -jnp.inf)
    top = jnp.max(scores, axis=2, keepdims=True)
    expo = jnp.exp(scores - top)
    probs = (expo / jnp.sum(expo, axis=2, keepdims=True)).astype(jnp.bfloat16)
    attended = jnp.einsum(
        "hij,jhd->ihd", probs, value_all, preferred_element_type=jnp.float32
    ).astype(jnp.bfloat16)
    attended = attended.reshape(tok, width_dev)
    residual = lax.dynamic_slice_in_dim(x32, section * width_dev, width_dev, 1)
    byte_states = (residual + attended.astype(jnp.float32)).astype(jnp.bfloat16)
    local = bounds - mine * tok
    stretch_rows = jnp.take(byte_states, local, axis=0)
    owners = owner[:, 0]
    crows = owners.shape[0]
    slot_count = 2 * crows // n_seq
    place = jnp.arange(crows, dtype=jnp.int32)
    earlier = (owners[:, None] == owners[None, :]) & (place[None, :] < place[:, None])
    rank = jnp.sum(earlier.astype(jnp.int32), axis=1)
    target = owners * slot_count + rank
    placing = (target[None, :] == jnp.arange(n_seq * slot_count, dtype=jnp.int32)[:, None]).astype(
        jnp.bfloat16
    )
    outgoing = jnp.dot(placing, stretch_rows, preferred_element_type=jnp.float32).astype(
        jnp.bfloat16
    )
    outgoing = outgoing.reshape(n_seq, slot_count, width_dev)
    arrived = lax.all_to_all(outgoing, "seq", split_axis=0, concat_axis=0, tiled=True).reshape(
        n_seq * slot_count, width_dev
    )
    stretch_states = project_rows(arrived, w_up, out_gain)
    return (byte_states, stretch_states)


def solution(mesh):
    n_seq, n_phase, n_dp = (mesh.shape[axis] for axis in ("seq", "phase", "dp"))

    def body(byte_embed, in_gain, w_qkv, *rest):
        tok, (rows, _, width) = byte_embed.shape[0], w_qkv.shape
        slot = 2 * rest[2].shape[0] // n_seq
        tiled = rows % 128 == 0 and width % HD == 0 and tok % 256 == 0 and slot % 16 == 0
        fits = n_seq == n_phase and width == 3 * HD and WINDOW == 2 * tok
        if tiled and fits and n_dp == 2 and n_phase == 4 and w_qkv.shape[0] == rest[0].shape[0]:
            return fused(n_seq, n_phase, byte_embed, in_gain, w_qkv, *rest)
        return on_device(byte_embed, in_gain, w_qkv, *rest)

    return jax.shard_map(
        body,
        mesh=mesh,
        in_specs=(
            P(("dp", "seq"), None),
            P(),
            P("seq", None, "phase"),
            P("phase", None),
            P("phase"),
            P(("dp", "seq")),
            P(("dp", "seq"), None),
        ),
        out_specs=(P(("dp", "seq"), "phase"), P(("dp", "seq"), "phase")),
        check_vma=False,
    )
```

```python
import functools
import math
import jax
import jax.numpy as jnp
from jax import lax
from jax.experimental import pallas as pl
from jax.experimental.pallas import tpu as pltpu
from jax.sharding import PartitionSpec as P

DC = 3072
HD = 128
WINDOW = 1024
MESH = pl.DeviceIdType.MESH
NEG = -0.7 * 3.4e38


def fused_kernel(
    dims,
    x_ref,
    gain_ref,
    w_ref,
    up_ref,
    og_ref,
    bounds_ref,
    owner_ref,
    bs_ref,
    ss_ref,
    xbuf,
    gain,
    og,
    bnd,
    own,
    normed,
    halo,
    wbuf,
    upbuf,
    qbuf,
    kbuf,
    vbuf,
    place,
    outrows,
    arrived,
    acc,
    partial,
    sqbuf,
    loc_sem,
    w_send,
    w_recv,
    p_send,
    p_recv,
    up_send,
    up_recv,
    upp_send,
    upp_recv,
    h_send,
    h_recv,
    g_send,
    g_recv,
    row_send,
    row_recv,
    all_send,
    all_recv,
    sq_send,
    sq_recv,
    go,
):
    n_seq, n_phase, reach, slot = dims
    tok, d = xbuf.shape
    rows, width = w_ref.shape[1:]
    half = rows // 2
    heads = width // HD
    last = heads - 1
    crows = bnd.shape[1]
    cols = og.shape[1]
    z = lax.axis_index("seq")
    p = lax.axis_index("phase")
    c = lax.axis_index("dp")

    own_x = pltpu.make_async_copy(x_ref, xbuf, loc_sem.at[0])
    own_x.start()
    small = []
    for i, (src, dst) in enumerate(
        ((gain_ref, gain.at[0]), (bounds_ref, bnd), (owner_ref, own), (og_ref, og.at[0]))
    ):
        small.append(pltpu.make_async_copy(src, dst, loc_sem.at[2 + heads + i]))
        small[i].start()

    twin_core = {"dp": 1 - c}
    peers = (
        [{"seq": lax.rem(z + k, n_seq)} for k in range(1, n_seq)]
        + [{"phase": lax.rem(p + k, n_phase)} for k in range(1, n_phase)]
        + [twin_core]
    )
    barrier = pltpu.get_barrier_semaphore()
    for peer in peers:
        pl.semaphore_signal(barrier, inc=1, device_id=peer, device_id_type=MESH)

    own_w = []
    for h in range(heads):
        own_w.append(
            pltpu.make_async_copy(
                w_ref.at[:, :, pl.ds(h * HD, HD)],
                wbuf.at[h, :, pl.ds(pl.multiple_of(z * rows, rows), rows), :],
                loc_sem.at[2 + h],
            )
        )
        own_w[h].start()
    own_up = pltpu.make_async_copy(
        up_ref.at[:, pl.ds(pl.multiple_of(p * cols, 128), cols)], upbuf.at[p], loc_sem.at[1]
    )
    own_up.start()
    pl.semaphore_wait(barrier, len(peers))

    def when(cond, action):
        if cond is None:
            action()
        else:
            pl.when(cond)(action)

    def move(src, dst, ssem, rsem, peer):
        return pltpu.make_async_remote_copy(
            src_ref=src, dst_ref=dst, send_sem=ssem, recv_sem=rsem, device_id=peer, device_id_type=MESH
        )

    def send(src, dst, ssem, rsem, peer, cond=None):
        copy = move(src, dst, ssem, rsem, peer)
        when(cond, copy.start)
        return copy

    def sent(ref, ssem, cond=None):
        when(cond, move(ref, ref, ssem, ssem, twin_core).wait_send)

    def landed(ref, rsem, cond=None):
        when(cond, move(ref, ref, rsem, rsem, twin_core).wait_recv)

    right, left = {"seq": z + 1}, {"seq": z - 1}
    has_right, has_left = z < n_seq - 1, z > 0
    ways = ((right, has_right, -1), (left, has_left, 1))
    RIGHTWARD, LEFTWARD = 0, 1

    def chunk(h, shard):
        at = pl.multiple_of(shard * rows + c * half, half)
        return wbuf.at[h, :, pl.ds(at, half), :]

    def slot_of(t, way):
        return t - 1 if way == LEFTWARD else n_seq - t - 1

    def issue_own(h, way, also=None):
        src = chunk(h, z)
        peer, cond, sign = ways[way]
        cond = cond if also is None else cond & also
        send(src, chunk(h, z), w_send, w_recv.at[h, slot_of(1, way)], peer, cond)

    def relay(h, t, way, also=None):
        if t >= n_seq:
            return
        peer, cond, sign = ways[way]
        shard = z + sign * t
        here = (shard >= 0) & (shard < n_seq)
        there = here if also is None else here & also
        piece = chunk(h, jnp.clip(shard, 0, n_seq - 1))
        landed(piece, w_recv.at[h, slot_of(t, way)], there)
        if t < n_seq - 1:
            send(piece, piece, w_send, w_recv.at[h, slot_of(t + 1, way)], peer, there & cond)
        late = (way == RIGHTWARD) & (t == z)
        group = jnp.where(late, last + 1, h) if h == last else h
        send(piece, piece, p_send, p_recv.at[group], twin_core, there)

    def finish(h, late=None, also=True):
        if h < last:
            landed(wbuf.at[h, :, pl.ds(0, (n_seq - 1) * half)], p_recv.at[h])
        elif late:
            landed(wbuf.at[h, :, pl.ds(0, half)], p_recv.at[last + 1], (z > 0) & also)
        else:
            landed(wbuf.at[h, :, pl.ds(0, (n_seq - 2) * half)], p_recv.at[h], (z > 0) & also)
            landed(wbuf.at[h, :, pl.ds(0, (n_seq - 1) * half)], p_recv.at[h], (z == 0) & also)

    across = {1: {"phase": p + 1 - 2 * lax.rem(p, 2)}, 2: {"phase": lax.rem(p + 2, n_phase)}}
    spots = {k: v["phase"] for k, v in across.items()}
    parts = [pl.ds(i * (tok // 2), tok // 2) for i in range(2)]
    mine, gathers = {}, {}

    def halo_start(dist, i, cond):
        if dist == 1:
            src = normed.at[parts[i], pl.ds(pl.multiple_of(p * width, 128), width)]
        else:
            src = halo.at[dist - 2, p, parts[i]]
        mine[dist, i] = send(
            src, halo.at[dist - 1, p, parts[i]], h_send.at[dist - 1], h_recv.at[dist - 1, i], right, cond
        )

    def halo_spread(dist, i):
        there = z >= dist
        pl.when(there)(mine[dist, i].wait_recv)
        if dist < reach:
            halo_start(dist + 1, i, there & has_right)
        piece = halo.at[dist - 1, p, parts[i]]
        for k in (1, 2):
            gathers[dist, i, k] = send(
                piece, piece, g_send.at[dist - 1], g_recv.at[dist - 1, 2 * i + k - 1], across[k], there
            )

    def halo_pass(dist, i, also=True):
        there = (z >= dist) & also
        k = i + 1
        pl.when(there)(gathers[dist, i, k].wait_recv)
        piece = halo.at[dist - 1, spots[k], parts[i]]
        send(piece, piece, g_send.at[dist - 1], g_recv.at[dist - 1, 4], across[3 - k], there)

    def halo_wait(dist):
        @pl.when(z >= dist)
        def _():
            gathers[dist, 0, 2].wait_recv()
            gathers[dist, 1, 1].wait_recv()
            landed(halo.at[dist - 1, 0], g_recv.at[dist - 1, 4])

    own_w[0].wait()
    issue_own(0, RIGHTWARD)
    issue_own(0, LEFTWARD)
    for h in range(1, heads):
        own_w[h].wait()
        issue_own(h, LEFTWARD)
    up_rows = up_ref.shape[0] // 2
    up_half = pl.ds(pl.multiple_of(c * up_rows, up_rows), up_rows)

    def up_out(k):
        other = spots[k] if k < 3 else n_phase - 1 - p
        part = pl.ds(pl.multiple_of(other * cols, 128), cols)
        group = 0 if k < 3 else 1
        send(up_ref.at[up_half, part], upbuf.at[p, up_half], up_send, up_recv.at[group], {"phase": other})

    def up_in(k):
        piece = upbuf.at[spots[k] if k < 3 else n_phase - 1 - p, up_half]
        send(piece, piece, upp_send, upp_recv, twin_core)

    for k in (1, 2):
        up_out(k)

    own_x.wait()
    small[0].wait()
    step_rows = 64


    @pl.loop(0, tok // step_rows)
    def _(i):
        r = pl.ds(pl.multiple_of(i * step_rows, step_rows), step_rows)
        xx = xbuf[r, :].astype(jnp.float32)
        scale = lax.rsqrt(jnp.mean(xx * xx, axis=1, keepdims=True) + 1e-05)
        normed[r, :] = (xx * scale * gain[...]).astype(jnp.bfloat16)

    for i in range(2):
        halo_start(1, i, has_right)
    first, second, final = z == 0, z == 1, z == n_seq - 1
    for h in range(1, heads):
        issue_own(h, RIGHTWARD, first)

    def column(ref):
        wide = jnp.broadcast_to(ref[...].astype(jnp.float32), (crows, crows))
        return wide.T

    relay(0, 1, RIGHTWARD)
    relay(0, 1, LEFTWARD)
    for copy in small[1:]:
        copy.wait()
    local = column(bnd)[:, 0:1] - (z * tok).astype(jnp.float32)
    spot = lax.broadcasted_iota(jnp.int32, (crows, tok), 1).astype(jnp.float32)
    pick = jnp.where(local == spot, 1.0, 0.0).astype(jnp.bfloat16)
    same = column(own) == own[...].astype(jnp.float32)
    before = lax.broadcasted_iota(jnp.int32, (crows, crows), 0) < lax.broadcasted_iota(
        jnp.int32, (crows, crows), 1
    )
    rank = jnp.sum(jnp.where(same & before, 1, 0), axis=0, keepdims=True)
    target = own[...] * slot + rank
    route = jnp.where(
        target == lax.broadcasted_iota(jnp.int32, (n_seq * slot, crows), 0), 1.0, 0.0
    ).astype(jnp.bfloat16)
    place[...] = jnp.dot(route, pick, preferred_element_type=jnp.float32).astype(jnp.bfloat16)

    tq = min(tok, 256)
    scale = HD ** (-0.5) * math.log2(math.e)

    def scores(h, r, q0, dist, k0, size):
        s = lax.dot_general(
            qbuf[h, r, :],
            kbuf[h, dist, k0 : k0 + size],
            (((1,), (1,)), ((), ())),
            preferred_element_type=jnp.float32,
        )
        ahead = k0 - dist * tok - q0
        if ahead + size - 1 > 0 or ahead - (tq - 1) <= -WINDOW:
            gap = lax.broadcasted_iota(jnp.int32, s.shape, 1) - lax.broadcasted_iota(jnp.int32, s.shape, 0)
            s = jnp.where((gap <= -ahead) & (gap > -ahead - WINDOW), s, NEG)
        return s

    def chunks(dist, q0, size=256):
        out = []
        for k0 in range(0, tok, size):
            ahead = k0 - dist * tok - q0
            if ahead - (tq - 1) <= 0 and ahead + size - 1 > -WINDOW:
                out.append((dist, k0, size))
        return out

    def attend(h, dists):
        tiles = []
        for q0 in range(0, tok, tq):
            r = pl.ds(q0, tq)
            where = [at for dist in dists for at in chunks(dist, q0)]
            tiles.append((r, where, [scores(h, r, q0, *at) for at in where]))
        for r, where, parts in tiles:
            top = jnp.max(functools.reduce(jnp.maximum, parts), axis=1, keepdims=True)
            low = top * scale
            es = [jnp.exp2(s * scale - low) for s in parts]
            total = jnp.sum(functools.reduce(jnp.add, es), axis=1, keepdims=True)
            e = jnp.concatenate([e.astype(jnp.bfloat16) for e in es], axis=1)
            v = jnp.concatenate([vbuf[h, dist, k0 : k0 + size] for dist, k0, size in where], axis=0)
            o = jnp.dot(e, v, preferred_element_type=jnp.float32)
            att = (o / total).astype(jnp.bfloat16).astype(jnp.float32)
            res = xbuf[r, pl.ds(pl.multiple_of(p * width + h * HD, HD), HD)].astype(jnp.float32)
            bs_ref[r, h * HD : (h + 1) * HD] = (res + att).astype(jnp.bfloat16)

    def store(h, dist, got):
        start = min(dist, 1) * HD
        if dist == 0:
            qbuf[h] = got[:, :HD]
        kbuf[h, dist] = got[:, HD - start : 2 * HD - start]
        vbuf[h, dist] = got[:, 2 * HD - start :]

    def project(h, dist, also=True):
        @pl.when((z >= dist) & also)
        def _():
            w = jnp.concatenate([wbuf[h, j] for j in range(min(dist, 1), 3)], axis=1)
            rows_in = (
                jnp.concatenate([halo[dist - 1, q] for q in range(n_phase)], axis=1)
                if dist
                else normed[...]
            )
            got = jnp.dot(rows_in, w, preferred_element_type=jnp.float32)
            store(h, dist, got.astype(jnp.bfloat16))

    def split_rows(dist):
        if dist == 0:
            return normed[:, :rows], normed[:, rows:]
        pieces = [halo[dist - 1, q] for q in range(n_phase)]
        return pieces[0], jnp.concatenate(pieces[1:], axis=1)

    def some_weights(dist, r):
        return jnp.concatenate([wbuf[last, j, r, :] for j in range(min(dist, 1), 3)], axis=1)

    def project_early(dist, also):
        @pl.when((z >= dist) & also)
        def _():
            got = jnp.dot(
                split_rows(dist)[1], some_weights(dist, slice(rows, None)), preferred_element_type=jnp.float32
            )
            partial[dist, :, pl.ds(min(dist, 1) * HD, got.shape[1])] = got

    def project_late(dist, also):
        @pl.when((z >= dist) & also)
        def _():
            got = jnp.dot(
                split_rows(dist)[0], some_weights(dist, slice(0, rows)), preferred_element_type=jnp.float32
            )
            start = min(dist, 1) * HD
            store(last, dist, (got + partial[dist, :, pl.ds(start, got.shape[1])]).astype(jnp.bfloat16))

    def heed(h):
        for n in range(reach + 1):

            @pl.when(z == n if n < reach else z >= n)
            def _():
                attend(h, list(range(n, -1, -1)))

    def hand_over(h):
        states = bs_ref[:, h * HD : (h + 1) * HD]
        routed = jnp.dot(place[...], states, preferred_element_type=jnp.float32).astype(jnp.bfloat16)
        for s in range(n_seq):
            outrows[h, s] = routed[s * slot : (s + 1) * slot]
        arrived[h, p, z] = outrows[h, z]
        rows_out(h, False)

    outer = n_seq - 2

    def close(h):
        heed(h)
        hand_over(h)

    def rows_out(h, held):
        for k in range(1, n_seq):
            other = lax.rem(z + k, n_seq)
            wait = (z < outer) & (other >= outer)
            send(
                outrows.at[h, other],
                arrived.at[h, p, z],
                row_send,
                row_recv.at[h, jnp.maximum(z - (n_seq - 3), 0)],
                {"seq": other},
                wait if held else jnp.logical_not(wait),
            )

    def rows_in(h, j, cond):
        if j == 0:
            landed(arrived.at[h, p, pl.ds(0, outer)], row_recv.at[h, 0], cond & (z >= outer))
            landed(arrived.at[h, p, pl.ds(0, outer - 1)], row_recv.at[h, 0], cond & (z < outer))
        else:
            src = outer + j - 1
            landed(arrived.at[h, p, src], row_recv.at[h, j], cond & (z != src))

    def spread(h, j, cond):
        rows_in(h, j, cond)
        piece = arrived.at[h, p, pl.ds(0, outer) if j == 0 else pl.ds(outer + j - 1, 1)]
        group = 1 + j // 2 if h == last else 0
        for k in range(1, n_phase):
            send(piece, piece, all_send, all_recv.at[group], {"phase": lax.rem(p + k, n_phase)}, cond)

    relay(1, 1, LEFTWARD)
    halo_spread(1, 0)
    relay(2, 1, LEFTWARD)
    landed(upbuf.at[pl.ds(0, 2), up_half], up_recv.at[0])
    for k in (1, 2):
        up_in(k)
    halo_spread(1, 1)
    for h in range(1, heads):
        issue_own(h, RIGHTWARD, second)
        relay(h, 1, RIGHTWARD, second)
    halo_pass(1, 0)
    relay(0, 2, RIGHTWARD)
    issue_own(1, RIGHTWARD, z > 1)
    halo_pass(1, 1)
    for t in range(2, n_seq):
        for h in range(heads):
            relay(h, t, LEFTWARD)
    for dist in range(2, reach + 1):
        for i in range(2):
            halo_spread(dist, i)
    for t in range(3, n_seq):
        relay(0, t, RIGHTWARD)
    inner, outside = z < n_seq - 1, z < outer
    halo_pass(reach, 0, final)
    finish(0)
    project(0, 0)
    relay(1, 1, RIGHTWARD, (z > 1) & inner)
    halo_pass(reach, 0, inner)
    relay(1, 2, RIGHTWARD, inner)
    issue_own(2, RIGHTWARD, z > 1)
    for dist in range(1, reach):
        halo_wait(dist)
        project(0, dist)
    halo_pass(reach, 1)
    relay(1, 1, RIGHTWARD, final)
    relay(1, 2, RIGHTWARD, final)
    up_out(3)
    for t in range(3, n_seq):
        relay(1, t, RIGHTWARD)

    @pl.when(final)
    def _():
        halo_wait(reach)
        project(0, reach)
        heed(0)

    finish(1)
    project(1, 0)
    relay(2, 1, RIGHTWARD, (z > 1) & inner)
    for dist in range(1, reach):
        project(1, dist)
    relay(2, 1, RIGHTWARD, final)
    relay(2, 2, RIGHTWARD, inner)
    finish(last, False, inner)
    finish(last, True, inner)
    project(last, 0, inner)
    for dist in range(1, reach):
        project(last, dist, inner)

    @pl.when(inner)
    def _():
        halo_wait(reach)
        project(0, reach)
        heed(0)

    hand_over(0)
    for h in range(1, last):
        project(h, reach)
        close(h)

    @pl.when(final)
    def _():
        for far in range(outer):
            pl.semaphore_signal(go, inc=1, device_id={"seq": far}, device_id_type=MESH)

    relay(last, 2, RIGHTWARD, final)
    for t in range(3, n_seq):
        relay(last, t, RIGHTWARD, c == 1)
    for h in range(last):
        spread(h, 2, final)
    finish(last, False, final)
    for dist in range(reach + 1):
        project_early(dist, final)
    for t in range(3, n_seq):
        relay(last, t, RIGHTWARD, c == 0)
    for h in range(last):
        spread(h, 1, final)
    finish(last, True, final)
    for dist in range(reach + 1):
        project_late(dist, final)
    for h in range(last):
        spread(h, 1, z == outer)
    project(last, reach, inner)
    close(last)
    spread(last, 1, z == outer)
    spread(last, 2, final)
    for h in range(heads):
        spread(h, 0, final)
    landed(upbuf.at[0, up_half], up_recv.at[1])
    up_in(3)
    for h in range(heads):
        spread(h, 0, outside)

    @pl.when(outside)
    def _():
        pl.semaphore_wait(go, 1)
        for h in range(heads):
            rows_out(h, True)

    for h in range(last):
        spread(h, 1, outside)
        spread(h, 2, inner)
    for h in range(heads):
        spread(h, 0, z == outer)
    spread(last, 1, z != outer)
    own_up.wait()
    landed(upbuf.at[pl.ds(0, n_phase - 1), up_half], upp_recv)
    landed(arrived.at[pl.ds(0, last), pl.ds(0, n_phase - 1)], all_recv.at[0])
    full = n_seq * slot
    cut = full - slot

    def rows_of(s, hs):
        return jnp.concatenate([arrived[h, s].reshape(full, HD) for h in hs], axis=1)

    for k in range(n_phase):
        s = lax.rem(p + n_phase - k, n_phase)
        acc[k] = jnp.dot(
            rows_of(s, range(last)), upbuf[s, : last * HD, :], preferred_element_type=jnp.float32
        )

    def complete(j):
        r = slice(0, cut) if j == 0 else slice(cut, full)
        projected = 0.0
        for k in range(n_phase):
            s = lax.rem(p + n_phase - k, n_phase)
            srcs = pl.ds(0, n_seq - 1) if j == 0 else pl.ds(n_seq - 1, 1)
            lhs = arrived[last, s, srcs].reshape(r.stop - r.start, HD)
            got = acc[k, r, :] + jnp.dot(lhs, upbuf[s, last * HD :, :], preferred_element_type=jnp.float32)
            projected = projected + got.astype(jnp.bfloat16).astype(jnp.float32)
        acc[0, r, :] = projected
        sq = jnp.sum(projected * projected, axis=1, keepdims=True)
        return jnp.broadcast_to(sq, (r.stop - r.start, 128))

    spread(last, 2, inner)
    landed(arrived.at[last, pl.ds(0, n_phase - 1), pl.ds(0, n_seq - 1)], all_recv.at[1])
    sq_top = complete(0)
    landed(arrived.at[last, pl.ds(0, n_phase - 1), pl.ds(0, 1)], all_recv.at[2])
    sq_all = jnp.concatenate([sq_top, complete(1)], axis=0)
    sqbuf[p] = sq_all.T[0:8, :]
    for k in range(1, n_phase):
        send(sqbuf.at[p], sqbuf.at[p], sq_send, sq_recv, {"phase": lax.rem(p + k, n_phase)})
    landed(sqbuf.at[pl.ds(0, n_phase - 1)], sq_recv)
    all_sq = sqbuf[0]
    for k in range(1, n_phase):
        all_sq = all_sq + sqbuf[k]
    all_sq = jnp.broadcast_to(all_sq[0:1, :], (128, full)).T[:, 0:1]
    norm = lax.rsqrt(all_sq / (n_phase * cols) + 1e-05)
    ss_ref[...] = (acc[0] * norm * og[...]).astype(jnp.bfloat16)
    sent(wbuf.at[:, :, pl.ds(0, half)], w_send, first | final)
    sent(wbuf.at[:, :, pl.ds(0, (n_seq + 1) * half)], w_send, jnp.logical_not(first | final))
    sent(wbuf.at[:, :, pl.ds(0, (n_seq - 1) * half)], p_send)
    sent(upbuf.at[pl.ds(0, n_phase - 1), up_half], up_send)
    sent(upbuf.at[pl.ds(0, n_phase - 1), up_half], upp_send)
    for dist in range(1, reach + 1):
        sent(halo.at[dist - 1, 0], h_send.at[dist - 1], (z >= dist - 1) & has_right)
        sent(halo.at[dist - 1, pl.ds(0, 3)], g_send.at[dist - 1], z >= dist)
    sent(outrows.at[:, pl.ds(0, n_seq - 1)], row_send)
    sent(arrived.at[:, pl.ds(0, n_phase - 1)], all_send)
    sent(sqbuf.at[pl.ds(0, n_phase - 1)], sq_send)


def flush_kernel(a_ref, b_ref, a_out, b_out, sems):
    copies = [
        pltpu.make_async_copy(a_ref, a_out, sems.at[0]),
        pltpu.make_async_copy(b_ref, b_out, sems.at[1]),
    ]
    for copy in copies:
        copy.start()
    for copy in copies:
        copy.wait()


def fused(n_seq, n_phase, byte_embed, in_gain, w_qkv, w_up, out_gain, bounds, owner):
    tok, d = byte_embed.shape
    rows, _, width = w_qkv.shape
    heads = width // HD
    crows = bounds.shape[0]
    cols = out_gain.shape[0]
    slot = 2 * crows // n_seq
    reach = -(-WINDOW // tok)
    bf, f32 = jnp.bfloat16, jnp.float32
    vmem = pl.BlockSpec(memory_space=pltpu.VMEM)
    hbm = pl.BlockSpec(memory_space=pltpu.HBM)
    dma = pltpu.SemaphoreType.DMA
    in_hbm = lambda a: pltpu.with_memory_space_constraint(a, pltpu.HBM)
    states, stretch = pl.pallas_call(
        functools.partial(fused_kernel, (n_seq, n_phase, reach, slot)),
        out_shape=(
            jax.ShapeDtypeStruct((tok, width), bf),
            jax.ShapeDtypeStruct((n_seq * slot, cols), bf),
        ),
        in_specs=[hbm] * 7,
        out_specs=(vmem, vmem),
        scratch_shapes=[
            pltpu.VMEM((tok, d), bf),
            pltpu.VMEM((1, d), f32),
            pltpu.VMEM((1, cols), f32),
            pltpu.VMEM((1, crows), jnp.int32),
            pltpu.VMEM((1, crows), jnp.int32),
            pltpu.VMEM((tok, d), bf),
            pltpu.VMEM((reach, n_phase, tok, width), bf),
            pltpu.VMEM((heads, 3, n_seq * rows, HD), bf),
            pltpu.VMEM((n_phase, w_up.shape[0], cols), bf),
            pltpu.VMEM((heads, tok, HD), bf),
            pltpu.VMEM((heads, reach + 1, tok, HD), bf),
            pltpu.VMEM((heads, reach + 1, tok, HD), bf),
            pltpu.VMEM((n_seq * slot, tok), bf),
            pltpu.VMEM((heads, n_seq, slot, HD), bf),
            pltpu.VMEM((heads, n_phase, n_seq, slot, HD), bf),
            pltpu.VMEM((n_phase, n_seq * slot, cols), f32),
            pltpu.VMEM((reach + 1, tok, 3 * HD), f32),
            pltpu.VMEM((n_phase, 8, n_seq * slot), f32),
            dma((6 + heads,)),
            dma(()),
            dma((heads, n_seq - 1)),
            dma(()),
            dma((heads + 1,)),
            dma(()),
            dma((2,)),
            dma(()),
            dma(()),
            dma((reach,)),
            dma((reach, 2)),
            dma((reach,)),
            dma((reach, 5)),
            dma(()),
            dma((heads, 3)),
            dma(()),
            dma((3,)),
            dma(()),
            dma(()),
            pltpu.SemaphoreType.REGULAR,
        ],
        compiler_params=pltpu.CompilerParams(
            collective_id=0, has_side_effects=True, vmem_limit_bytes=48 * 1024 * 1024
        ),
    )(
        in_hbm(byte_embed),
        in_hbm(in_gain),
        in_hbm(jnp.transpose(w_qkv, (1, 0, 2))),
        in_hbm(w_up),
        in_hbm(out_gain),
        in_hbm(bounds.reshape(1, crows)),
        in_hbm(owner.reshape(1, crows)),
    )
    return pl.pallas_call(
        flush_kernel,
        out_shape=(
            jax.ShapeDtypeStruct(states.shape, bf),
            jax.ShapeDtypeStruct(stretch.shape, bf),
        ),
        in_specs=[vmem] * 2,
        out_specs=(hbm, hbm),
        scratch_shapes=[dma((2,))],
        compiler_params=pltpu.CompilerParams(vmem_limit_bytes=4 * 1024 * 1024),
    )(states, stretch)


def passed_along(value, axis, by):
    devices = lax.axis_size(axis)
    pairs = [(i, i + by) for i in range(devices) if 0 <= i + by < devices]
    return lax.ppermute(value, axis, pairs)


def project_rows(rows, w_up, out_gain):
    groups = lax.axis_size("phase")
    full_rows = lax.all_gather(rows, "phase", axis=1, tiled=True)
    w_cols = lax.all_to_all(w_up, "phase", split_axis=1, concat_axis=0, tiled=True)
    count = full_rows.shape[0]
    width = rows.shape[1]
    columns = w_cols.shape[1]
    pieces = jnp.einsum(
        "nsg,sgc->snc",
        full_rows.reshape(count, groups, width),
        w_cols.reshape(groups, width, columns),
        preferred_element_type=jnp.float32,
    )
    projected = jnp.sum(pieces.astype(jnp.bfloat16).astype(jnp.float32), axis=0)
    squares = lax.psum(jnp.sum(projected * projected, axis=1), "phase")
    scale = lax.rsqrt(squares / DC + 1e-05)
    return (projected * scale[:, None] * out_gain).astype(jnp.bfloat16)


def on_device(byte_embed, in_gain, w_qkv, w_up, out_gain, bounds, owner):
    tok = byte_embed.shape[0]
    n_seq = lax.axis_size("seq")
    mine = lax.axis_index("seq")
    section = lax.axis_index("phase")
    width_dev = w_qkv.shape[2]
    heads_dev = width_dev // HD
    x32 = byte_embed.astype(jnp.float32)
    normed = (x32 * lax.rsqrt(jnp.mean(x32 * x32, axis=1, keepdims=True) + 1e-05) * in_gain).astype(
        jnp.bfloat16
    )
    piece = lax.all_gather(w_qkv, "seq", axis=0, tiled=True)
    qkv = jnp.dot(
        normed, piece.reshape(piece.shape[0], 3 * width_dev), preferred_element_type=jnp.float32
    ).astype(jnp.bfloat16)
    qkv = qkv.reshape(tok, 3, heads_dev, HD)
    query = qkv[:, 0]
    keys = qkv[:, 1]
    values = qkv[:, 2]
    reach = -(-WINDOW // tok)
    key_list = [keys]
    value_list = [values]
    for distance in range(1, reach + 1):
        earlier_keys, earlier_values = passed_along((keys, values), "seq", distance)
        key_list = [earlier_keys] + key_list
        value_list = [earlier_values] + value_list
    key_all = jnp.concatenate(key_list, axis=0)
    value_all = jnp.concatenate(value_list, axis=0)
    scores = jnp.einsum(
        "ihd,jhd->hij", query, key_all, preferred_element_type=jnp.float32
    ) * HD ** (-0.5)
    q_pos = mine * tok + jnp.arange(tok, dtype=jnp.int32)
    k_pos = mine * tok - reach * tok + jnp.arange((reach + 1) * tok, dtype=jnp.int32)
    keep = (
        (k_pos[None, :] <= q_pos[:, None])
        & (k_pos[None, :] > q_pos[:, None] - WINDOW)
        & (k_pos[None, :] >= 0)
    )
    scores = jnp.where(keep[None], scores, -jnp.inf)
    top = jnp.max(scores, axis=2, keepdims=True)
    expo = jnp.exp(scores - top)
    probs = (expo / jnp.sum(expo, axis=2, keepdims=True)).astype(jnp.bfloat16)
    attended = jnp.einsum(
        "hij,jhd->ihd", probs, value_all, preferred_element_type=jnp.float32
    ).astype(jnp.bfloat16)
    attended = attended.reshape(tok, width_dev)
    residual = lax.dynamic_slice_in_dim(x32, section * width_dev, width_dev, 1)
    byte_states = (residual + attended.astype(jnp.float32)).astype(jnp.bfloat16)
    local = bounds - mine * tok
    stretch_rows = jnp.take(byte_states, local, axis=0)
    owners = owner[:, 0]
    crows = owners.shape[0]
    slot_count = 2 * crows // n_seq
    place = jnp.arange(crows, dtype=jnp.int32)
    earlier = (owners[:, None] == owners[None, :]) & (place[None, :] < place[:, None])
    rank = jnp.sum(earlier.astype(jnp.int32), axis=1)
    target = owners * slot_count + rank
    placing = (target[None, :] == jnp.arange(n_seq * slot_count, dtype=jnp.int32)[:, None]).astype(
        jnp.bfloat16
    )
    outgoing = jnp.dot(placing, stretch_rows, preferred_element_type=jnp.float32).astype(
        jnp.bfloat16
    )
    outgoing = outgoing.reshape(n_seq, slot_count, width_dev)
    arrived = lax.all_to_all(outgoing, "seq", split_axis=0, concat_axis=0, tiled=True).reshape(
        n_seq * slot_count, width_dev
    )
    stretch_states = project_rows(arrived, w_up, out_gain)
    return (byte_states, stretch_states)


def solution(mesh):
    n_seq, n_phase, n_dp = (mesh.shape[axis] for axis in ("seq", "phase", "dp"))

    def body(byte_embed, in_gain, w_qkv, *rest):
        tok, (rows, _, width) = byte_embed.shape[0], w_qkv.shape
        slot = 2 * rest[2].shape[0] // n_seq
        tiled = rows % 128 == 0 and width % HD == 0 and tok % 256 == 0 and slot % 16 == 0
        fits = n_seq == n_phase and width == 3 * HD and WINDOW == 2 * tok
        if tiled and fits and n_dp == 2 and n_phase == 4 and w_qkv.shape[0] == rest[0].shape[0]:
            return fused(n_seq, n_phase, byte_embed, in_gain, w_qkv, *rest)
        return on_device(byte_embed, in_gain, w_qkv, *rest)

    return jax.shard_map(
        body,
        mesh=mesh,
        in_specs=(
            P(("dp", "seq"), None),
            P(),
            P("seq", None, "phase"),
            P("phase", None),
            P("phase"),
            P(("dp", "seq")),
            P(("dp", "seq"), None),
        ),
        out_specs=(P(("dp", "seq"), "phase"), P(("dp", "seq"), "phase")),
        check_vma=False,
    )
```

```python
import functools
import math
import jax
import jax.numpy as jnp
from jax import lax
from jax.experimental import pallas as pl
from jax.experimental.pallas import tpu as pltpu
from jax.sharding import PartitionSpec as P

DC = 3072
HD = 128
WINDOW = 1024
MESH = pl.DeviceIdType.MESH
NEG = -0.7 * 3.4e38


def fused_kernel(
    dims,
    x_ref,
    gain_ref,
    w_ref,
    up_ref,
    og_ref,
    bounds_ref,
    owner_ref,
    bs_ref,
    ss_ref,
    xbuf,
    gain,
    og,
    bnd,
    own,
    normed,
    halo,
    wbuf,
    upbuf,
    qbuf,
    kbuf,
    vbuf,
    place,
    outrows,
    arrived,
    acc,
    partial,
    sqbuf,
    loc_sem,
    w_send,
    w_recv,
    p_send,
    p_recv,
    up_send,
    up_recv,
    upp_send,
    upp_recv,
    h_send,
    h_recv,
    g_send,
    g_recv,
    row_send,
    row_recv,
    all_send,
    all_recv,
    sq_send,
    sq_recv,
    go,
):
    n_seq, n_phase, reach, slot = dims
    tok, d = xbuf.shape
    rows, width = w_ref.shape[1:]
    half = rows // 2
    heads = width // HD
    last = heads - 1
    crows = bnd.shape[1]
    cols = og.shape[1]
    z = lax.axis_index("seq")
    p = lax.axis_index("phase")
    c = lax.axis_index("dp")

    own_x = pltpu.make_async_copy(x_ref, xbuf, loc_sem.at[0])
    own_x.start()
    small = []
    for i, (src, dst) in enumerate(
        ((gain_ref, gain.at[0]), (bounds_ref, bnd), (owner_ref, own), (og_ref, og.at[0]))
    ):
        small.append(pltpu.make_async_copy(src, dst, loc_sem.at[3 + i]))
        small[i].start()

    twin_core = {"dp": 1 - c}
    peers = (
        [{"seq": lax.rem(z + k, n_seq)} for k in range(1, n_seq)]
        + [{"phase": lax.rem(p + k, n_phase)} for k in range(1, n_phase)]
        + [twin_core]
    )
    barrier = pltpu.get_barrier_semaphore()
    for peer in peers:
        pl.semaphore_signal(barrier, inc=1, device_id=peer, device_id_type=MESH)

    pl.semaphore_wait(barrier, len(peers))

    def when(cond, action):
        if cond is None:
            action()
        else:
            pl.when(cond)(action)

    def move(src, dst, ssem, rsem, peer):
        return pltpu.make_async_remote_copy(
            src_ref=src, dst_ref=dst, send_sem=ssem, recv_sem=rsem, device_id=peer, device_id_type=MESH
        )

    def send(src, dst, ssem, rsem, peer, cond=None):
        copy = move(src, dst, ssem, rsem, peer)
        when(cond, copy.start)
        return copy

    def sent(ref, ssem, cond=None):
        when(cond, move(ref, ref, ssem, ssem, twin_core).wait_send)

    def landed(ref, rsem, cond=None):
        when(cond, move(ref, ref, rsem, rsem, twin_core).wait_recv)

    right, left = {"seq": z + 1}, {"seq": z - 1}
    has_right, has_left = z < n_seq - 1, z > 0
    ways = ((right, has_right, -1), (left, has_left, 1))
    RIGHTWARD, LEFTWARD = 0, 1

    def chunk(h, shard):
        at = pl.multiple_of(shard * rows + c * half, half)
        return wbuf.at[h, :, pl.ds(at, half), :]

    def slot_of(t, way):
        return t - 1 if way == LEFTWARD else n_seq - t - 1

    def issue_own(h, way, also=None):
        src = w_ref.at[:, pl.ds(pl.multiple_of(c * half, half), half), pl.ds(h * HD, HD)]
        peer, cond, sign = ways[way]
        cond = cond if also is None else cond & also
        send(src, chunk(h, z), w_send, w_recv.at[h, slot_of(1, way)], peer, cond)

    def relay(h, t, way, also=None):
        if t >= n_seq:
            return
        peer, cond, sign = ways[way]
        shard = z + sign * t
        here = (shard >= 0) & (shard < n_seq)
        there = here if also is None else here & also
        piece = chunk(h, jnp.clip(shard, 0, n_seq - 1))
        landed(piece, w_recv.at[h, slot_of(t, way)], there)
        if t < n_seq - 1:
            send(piece, piece, w_send, w_recv.at[h, slot_of(t + 1, way)], peer, there & cond)
        late = (way == RIGHTWARD) & (t == z)
        group = jnp.where(late, last + 1, h) if h == last else h
        send(piece, piece, p_send, p_recv.at[group], twin_core, there)

    def finish(h, late=None, also=True):
        if h < last:
            landed(wbuf.at[h, :, pl.ds(0, (n_seq - 1) * half)], p_recv.at[h])
        elif late:
            landed(wbuf.at[h, :, pl.ds(0, half)], p_recv.at[last + 1], (z > 0) & also)
        else:
            landed(wbuf.at[h, :, pl.ds(0, (n_seq - 2) * half)], p_recv.at[h], (z > 0) & also)
            landed(wbuf.at[h, :, pl.ds(0, (n_seq - 1) * half)], p_recv.at[h], (z == 0) & also)

    across = {1: {"phase": p + 1 - 2 * lax.rem(p, 2)}, 2: {"phase": lax.rem(p + 2, n_phase)}}
    spots = {k: v["phase"] for k, v in across.items()}
    partners = (n_phase - 1 - p, spots[1], spots[2])
    parts = [pl.ds(i * (tok // 2), tok // 2) for i in range(2)]
    mine, gathers = {}, {}

    def halo_start(dist, i, cond):
        if dist == 1:
            src = normed.at[parts[i], pl.ds(pl.multiple_of(p * width, 128), width)]
        else:
            src = halo.at[dist - 2, p, parts[i]]
        mine[dist, i] = send(
            src, halo.at[dist - 1, p, parts[i]], h_send.at[dist - 1], h_recv.at[dist - 1, i], right, cond
        )

    def halo_spread(dist, i):
        there = z >= dist
        pl.when(there)(mine[dist, i].wait_recv)
        if dist < reach:
            halo_start(dist + 1, i, there & has_right)
        piece = halo.at[dist - 1, p, parts[i]]
        for k in (1, 2):
            group = i if k == i + 1 else 2
            gathers[dist, i, k] = send(
                piece, piece, g_send.at[dist - 1], g_recv.at[dist - 1, group], across[k], there
            )

    def halo_pass(dist, i, also=True):
        there = (z >= dist) & also
        k = i + 1
        pl.when(there)(gathers[dist, i, k].wait_recv)
        piece = halo.at[dist - 1, spots[k], parts[i]]
        send(piece, piece, g_send.at[dist - 1], g_recv.at[dist - 1, 2], across[3 - k], there)

    def halo_wait(dist):
        @pl.when(z >= dist)
        def _():
            landed(halo.at[dist - 1, pl.ds(0, 2)], g_recv.at[dist - 1, 2])

    issue_own(0, RIGHTWARD)
    for h in range(heads):
        issue_own(h, LEFTWARD)
    up_rows = up_ref.shape[0] // 2
    up_half = pl.ds(pl.multiple_of(c * up_rows, up_rows), up_rows)

    def up_out(k, also=None):
        other = spots[k] if k < 3 else n_phase - 1 - p
        part = pl.ds(pl.multiple_of(other * cols, 128), cols)
        group = 0 if k < 3 else 1
        dst = upbuf.at[p, up_half]
        send(up_ref.at[up_half, part], dst, up_send, up_recv.at[group], {"phase": other}, also)

    def up_in(k):
        piece = upbuf.at[spots[k] if k < 3 else n_phase - 1 - p, up_half]
        send(piece, piece, upp_send, upp_recv, twin_core)

    for k in (1, 2):
        up_out(k)
    mine_w = wbuf.at[:, :, pl.ds(pl.multiple_of(z * rows, rows), rows), :]
    for h in range(heads):
        pltpu.make_async_copy(
            w_ref.at[:, :, pl.ds(h * HD, HD)],
            wbuf.at[h, :, pl.ds(pl.multiple_of(z * rows, rows), rows), :],
            loc_sem.at[2],
        ).start()
    own_up = pltpu.make_async_copy(
        up_ref.at[:, pl.ds(pl.multiple_of(p * cols, 128), cols)], upbuf.at[p], loc_sem.at[1]
    )
    own_up.start()

    own_x.wait()
    small[0].wait()
    step_rows = 64


    @pl.loop(0, tok // step_rows)
    def _(i):
        r = pl.ds(pl.multiple_of(i * step_rows, step_rows), step_rows)
        xx = xbuf[r, :].astype(jnp.float32)
        scale = lax.rsqrt(jnp.mean(xx * xx, axis=1, keepdims=True) + 1e-05)
        normed[r, :] = (xx * scale * gain[...]).astype(jnp.bfloat16)

    for i in range(2):
        halo_start(1, i, has_right)
    first, second, final = z == 0, z == 1, z == n_seq - 1
    for h in range(1, heads):
        issue_own(h, RIGHTWARD, first)

    def column(ref):
        wide = jnp.broadcast_to(ref[...].astype(jnp.float32), (crows, crows))
        return wide.T

    relay(0, 1, RIGHTWARD)
    relay(0, 1, LEFTWARD)
    pltpu.make_async_copy(mine_w, mine_w, loc_sem.at[2]).wait()
    for copy in small[1:]:
        copy.wait()
    local = column(bnd)[:, 0:1] - (z * tok).astype(jnp.float32)
    spot = lax.broadcasted_iota(jnp.int32, (crows, tok), 1).astype(jnp.float32)
    pick = jnp.where(local == spot, 1.0, 0.0).astype(jnp.bfloat16)
    same = column(own) == own[...].astype(jnp.float32)
    before = lax.broadcasted_iota(jnp.int32, (crows, crows), 0) < lax.broadcasted_iota(
        jnp.int32, (crows, crows), 1
    )
    rank = jnp.sum(jnp.where(same & before, 1, 0), axis=0, keepdims=True)
    target = own[...] * slot + rank
    route = jnp.where(
        target == lax.broadcasted_iota(jnp.int32, (n_seq * slot, crows), 0), 1.0, 0.0
    ).astype(jnp.bfloat16)
    place[...] = jnp.dot(route, pick, preferred_element_type=jnp.float32).astype(jnp.bfloat16)

    tq = min(tok, 256)
    scale = HD ** (-0.5) * math.log2(math.e)

    def scores(h, r, q0, dist, k0, size):
        s = lax.dot_general(
            qbuf[h, r, :],
            kbuf[h, dist, k0 : k0 + size],
            (((1,), (1,)), ((), ())),
            preferred_element_type=jnp.float32,
        )
        ahead = k0 - dist * tok - q0
        if ahead + size - 1 > 0 or ahead - (tq - 1) <= -WINDOW:
            gap = lax.broadcasted_iota(jnp.int32, s.shape, 1) - lax.broadcasted_iota(jnp.int32, s.shape, 0)
            s = jnp.where((gap <= -ahead) & (gap > -ahead - WINDOW), s, NEG)
        return s

    def chunks(dist, q0, size=256):
        out = []
        for k0 in range(0, tok, size):
            ahead = k0 - dist * tok - q0
            if ahead - (tq - 1) <= 0 and ahead + size - 1 > -WINDOW:
                out.append((dist, k0, size))
        return out

    def attend(h, dists):
        tiles = []
        for q0 in range(0, tok, tq):
            r = pl.ds(q0, tq)
            where = [at for dist in dists for at in chunks(dist, q0)]
            tiles.append((r, where, [scores(h, r, q0, *at) for at in where]))
        for r, where, parts in tiles:
            top = jnp.max(functools.reduce(jnp.maximum, parts), axis=1, keepdims=True)
            low = top * scale
            es = [jnp.exp2(s * scale - low) for s in parts]
            total = jnp.sum(functools.reduce(jnp.add, es), axis=1, keepdims=True)
            e = jnp.concatenate([e.astype(jnp.bfloat16) for e in es], axis=1)
            v = jnp.concatenate([vbuf[h, dist, k0 : k0 + size] for dist, k0, size in where], axis=0)
            o = jnp.dot(e, v, preferred_element_type=jnp.float32)
            att = (o / total).astype(jnp.bfloat16).astype(jnp.float32)
            res = xbuf[r, pl.ds(pl.multiple_of(p * width + h * HD, HD), HD)].astype(jnp.float32)
            bs_ref[r, h * HD : (h + 1) * HD] = (res + att).astype(jnp.bfloat16)

    def store(h, dist, got):
        start = min(dist, 1) * HD
        if dist == 0:
            qbuf[h] = got[:, :HD]
        kbuf[h, dist] = got[:, HD - start : 2 * HD - start]
        vbuf[h, dist] = got[:, 2 * HD - start :]

    def project(h, dist, also=True):
        @pl.when((z >= dist) & also)
        def _():
            w = jnp.concatenate([wbuf[h, j] for j in range(min(dist, 1), 3)], axis=1)
            rows_in = (
                jnp.concatenate([halo[dist - 1, q] for q in range(n_phase)], axis=1)
                if dist
                else normed[...]
            )
            got = jnp.dot(rows_in, w, preferred_element_type=jnp.float32)
            store(h, dist, got.astype(jnp.bfloat16))

    def split_rows(dist):
        if dist == 0:
            return normed[:, :rows], normed[:, rows:]
        pieces = [halo[dist - 1, q] for q in range(n_phase)]
        return pieces[0], jnp.concatenate(pieces[1:], axis=1)

    def some_weights(dist, r):
        return jnp.concatenate([wbuf[last, j, r, :] for j in range(min(dist, 1), 3)], axis=1)

    def project_early(dist, also):
        @pl.when((z >= dist) & also)
        def _():
            got = jnp.dot(
                split_rows(dist)[1], some_weights(dist, slice(rows, None)), preferred_element_type=jnp.float32
            )
            partial[dist, :, pl.ds(min(dist, 1) * HD, got.shape[1])] = got

    def project_late(dist, also):
        @pl.when((z >= dist) & also)
        def _():
            got = jnp.dot(
                split_rows(dist)[0], some_weights(dist, slice(0, rows)), preferred_element_type=jnp.float32
            )
            start = min(dist, 1) * HD
            store(last, dist, (got + partial[dist, :, pl.ds(start, got.shape[1])]).astype(jnp.bfloat16))

    def heed(h):
        for n in range(reach + 1):

            @pl.when(z == n if n < reach else z >= n)
            def _():
                attend(h, list(range(n, -1, -1)))

    def hand_over(h):
        states = bs_ref[:, h * HD : (h + 1) * HD]
        routed = jnp.dot(place[...], states, preferred_element_type=jnp.float32).astype(jnp.bfloat16)
        for s in range(n_seq):
            outrows[h, s] = routed[s * slot : (s + 1) * slot]
        arrived[h, p, z] = outrows[h, z]
        rows_out(h, False)

    outer = n_seq - 2

    def close(h):
        heed(h)
        hand_over(h)

    def release(cond):
        @pl.when(cond)
        def _():
            for far in range(outer):
                pl.semaphore_signal(go, inc=1, device_id={"seq": far}, device_id_type=MESH)

    def rows_out(h, held):
        for k in range(1, n_seq):
            other = lax.rem(z + k, n_seq)
            wait = (z < outer) & (other >= outer)
            send(
                outrows.at[h, other],
                arrived.at[h, p, z],
                row_send,
                row_recv.at[h, jnp.maximum(z - (n_seq - 3), 0)],
                {"seq": other},
                wait if held else jnp.logical_not(wait),
            )

    def rows_in(h, j, cond):
        if j == 0:
            landed(arrived.at[h, p, pl.ds(0, outer)], row_recv.at[h, 0], cond & (z >= outer))
            landed(arrived.at[h, p, pl.ds(0, outer - 1)], row_recv.at[h, 0], cond & (z < outer))
        else:
            src = outer + j - 1
            landed(arrived.at[h, p, src], row_recv.at[h, j], cond & (z != src))

    def spread(h, j, cond):
        rows_in(h, j, cond)
        piece = arrived.at[h, p, pl.ds(0, outer) if j == 0 else pl.ds(outer + j - 1, 1)]
        group = 1 + j // 2 if h == last else 0
        for other in partners:
            send(piece, piece, all_send, all_recv.at[group], {"phase": other}, cond)

    relay(1, 1, LEFTWARD)
    halo_spread(1, 0)
    relay(2, 1, LEFTWARD)
    landed(upbuf.at[pl.ds(0, 2), up_half], up_recv.at[0])
    for k in (1, 2):
        up_in(k)
    halo_spread(1, 1)
    for h in range(1, heads):
        issue_own(h, RIGHTWARD, second)
        relay(h, 1, RIGHTWARD, second)
    halo_pass(1, 0)
    relay(0, 2, RIGHTWARD)
    issue_own(1, RIGHTWARD, z > 1)
    halo_pass(1, 1)
    for t in range(2, n_seq):
        for h in range(heads):
            relay(h, t, LEFTWARD)
    for dist in range(2, reach + 1):
        for i in range(2):
            halo_spread(dist, i)
    for t in range(3, n_seq):
        relay(0, t, RIGHTWARD)
    inner, outside = z < n_seq - 1, z < outer
    halo_pass(reach, 0, final)
    finish(0)
    project(0, 0)
    relay(1, 1, RIGHTWARD, (z > 1) & inner)
    halo_pass(reach, 0, inner)
    relay(1, 2, RIGHTWARD, inner)
    issue_own(2, RIGHTWARD, z > 1)
    for dist in range(1, reach):
        halo_wait(dist)
        project(0, dist)
    halo_pass(reach, 1)
    relay(1, 1, RIGHTWARD, final)
    relay(1, 2, RIGHTWARD, final)
    up_out(3, inner)
    for t in range(3, n_seq):
        relay(1, t, RIGHTWARD)

    @pl.when(final)
    def _():
        halo_wait(reach)
        project(0, reach)
        heed(0)

    up_out(3, final)
    finish(1)
    project(1, 0)
    relay(2, 1, RIGHTWARD, (z > 1) & inner)
    for dist in range(1, reach):
        project(1, dist)
    relay(2, 1, RIGHTWARD, final)
    relay(2, 2, RIGHTWARD, inner)
    finish(last, False, inner)
    finish(last, True, inner)
    project(last, 0, inner)
    for dist in range(1, reach):
        project(last, dist, inner)

    @pl.when(inner)
    def _():
        halo_wait(reach)
        project(0, reach)
        heed(0)

    hand_over(0)
    for h in range(1, last):
        project(h, reach)
        close(h)
    relay(last, 2, RIGHTWARD, final)
    release(final)
    for t in range(3, n_seq):
        relay(last, t, RIGHTWARD, c == 1)
    for h in range(last):
        spread(h, 2, final)
    finish(last, False, final)
    for dist in range(reach + 1):
        project_early(dist, final)
    for t in range(3, n_seq):
        relay(last, t, RIGHTWARD, c == 0)
    spread(0, 1, final)
    finish(last, True, final)
    for dist in range(reach + 1):
        project_late(dist, final)
    for h in range(last):
        spread(h, 1, z == outer)
    project(last, reach, inner)
    close(last)
    spread(last, 1, z == outer)
    spread(last, 2, final)
    for h in range(1, last):
        spread(h, 1, final)
    for h in range(heads):
        spread(h, 0, final)
    landed(upbuf.at[0, up_half], up_recv.at[1])
    up_in(3)
    for h in range(heads):
        spread(h, 0, outside)

    @pl.when(outside)
    def _():
        pl.semaphore_wait(go, 1)
        for h in range(heads):
            rows_out(h, True)

    for h in range(last):
        spread(h, 1, outside)
        spread(h, 2, inner)
    for h in range(heads):
        spread(h, 0, z == outer)
    spread(last, 1, z != outer)
    spread(last, 2, z == outer)
    own_up.wait()
    landed(upbuf.at[pl.ds(0, n_phase - 1), up_half], upp_recv)
    landed(arrived.at[pl.ds(0, last), pl.ds(0, n_phase - 1)], all_recv.at[0])
    full = n_seq * slot
    cut = full - slot

    def rows_of(s, hs):
        return jnp.concatenate([arrived[h, s].reshape(full, HD) for h in hs], axis=1)

    for k in range(n_phase):
        s = lax.rem(p + n_phase - k, n_phase)
        acc[k] = jnp.dot(
            rows_of(s, range(last)), upbuf[s, : last * HD, :], preferred_element_type=jnp.float32
        )

    def complete(j):
        r = slice(0, cut) if j == 0 else slice(cut, full)
        projected = 0.0
        for k in range(n_phase):
            s = lax.rem(p + n_phase - k, n_phase)
            srcs = pl.ds(0, n_seq - 1) if j == 0 else pl.ds(n_seq - 1, 1)
            lhs = arrived[last, s, srcs].reshape(r.stop - r.start, HD)
            got = acc[k, r, :] + jnp.dot(lhs, upbuf[s, last * HD :, :], preferred_element_type=jnp.float32)
            projected = projected + got.astype(jnp.bfloat16).astype(jnp.float32)
        acc[0, r, :] = projected
        sq = jnp.sum(projected * projected, axis=1, keepdims=True)
        return jnp.broadcast_to(sq, (r.stop - r.start, 128))

    spread(last, 2, outside)
    landed(arrived.at[last, pl.ds(0, n_phase - 1), pl.ds(0, n_seq - 1)], all_recv.at[1])
    sq_top = complete(0)
    landed(arrived.at[last, pl.ds(0, n_phase - 1), pl.ds(0, 1)], all_recv.at[2])
    sq_all = jnp.concatenate([sq_top, complete(1)], axis=0)
    sqbuf[p] = sq_all.T[0:8, :]
    for other in partners:
        send(sqbuf.at[p], sqbuf.at[p], sq_send, sq_recv, {"phase": other})
    landed(sqbuf.at[pl.ds(0, n_phase - 1)], sq_recv)
    all_sq = sqbuf[0]
    for k in range(1, n_phase):
        all_sq = all_sq + sqbuf[k]
    all_sq = jnp.broadcast_to(all_sq[0:1, :], (128, full)).T[:, 0:1]
    norm = lax.rsqrt(all_sq / (n_phase * cols) + 1e-05)
    ss_ref[...] = (acc[0] * norm * og[...]).astype(jnp.bfloat16)
    sent(wbuf.at[:, :, pl.ds(0, half)], w_send, first | final)
    sent(wbuf.at[:, :, pl.ds(0, (n_seq + 1) * half)], w_send, jnp.logical_not(first | final))
    sent(wbuf.at[:, :, pl.ds(0, (n_seq - 1) * half)], p_send)
    sent(upbuf.at[pl.ds(0, n_phase - 1), up_half], up_send)
    sent(upbuf.at[pl.ds(0, n_phase - 1), up_half], upp_send)
    for dist in range(1, reach + 1):
        sent(halo.at[dist - 1, 0], h_send.at[dist - 1], (z >= dist - 1) & has_right)
        sent(halo.at[dist - 1, pl.ds(0, 3)], g_send.at[dist - 1], z >= dist)
    sent(outrows.at[:, pl.ds(0, n_seq - 1)], row_send)
    sent(arrived.at[:, pl.ds(0, n_phase - 1)], all_send)
    sent(sqbuf.at[pl.ds(0, n_phase - 1)], sq_send)


def flush_kernel(a_ref, b_ref, a_out, b_out, sems):
    copies = [
        pltpu.make_async_copy(a_ref, a_out, sems.at[0]),
        pltpu.make_async_copy(b_ref, b_out, sems.at[1]),
    ]
    for copy in copies:
        copy.start()
    for copy in copies:
        copy.wait()


def fused(n_seq, n_phase, byte_embed, in_gain, w_qkv, w_up, out_gain, bounds, owner):
    tok, d = byte_embed.shape
    rows, _, width = w_qkv.shape
    heads = width // HD
    crows = bounds.shape[0]
    cols = out_gain.shape[0]
    slot = 2 * crows // n_seq
    reach = -(-WINDOW // tok)
    bf, f32 = jnp.bfloat16, jnp.float32
    vmem = pl.BlockSpec(memory_space=pltpu.VMEM)
    hbm = pl.BlockSpec(memory_space=pltpu.HBM)
    dma = pltpu.SemaphoreType.DMA
    in_hbm = lambda a: pltpu.with_memory_space_constraint(a, pltpu.HBM)
    states, stretch = pl.pallas_call(
        functools.partial(fused_kernel, (n_seq, n_phase, reach, slot)),
        out_shape=(
            jax.ShapeDtypeStruct((tok, width), bf),
            jax.ShapeDtypeStruct((n_seq * slot, cols), bf),
        ),
        in_specs=[hbm] * 7,
        out_specs=(vmem, vmem),
        scratch_shapes=[
            pltpu.VMEM((tok, d), bf),
            pltpu.VMEM((1, d), f32),
            pltpu.VMEM((1, cols), f32),
            pltpu.VMEM((1, crows), jnp.int32),
            pltpu.VMEM((1, crows), jnp.int32),
            pltpu.VMEM((tok, d), bf),
            pltpu.VMEM((reach, n_phase, tok, width), bf),
            pltpu.VMEM((heads, 3, n_seq * rows, HD), bf),
            pltpu.VMEM((n_phase, w_up.shape[0], cols), bf),
            pltpu.VMEM((heads, tok, HD), bf),
            pltpu.VMEM((heads, reach + 1, tok, HD), bf),
            pltpu.VMEM((heads, reach + 1, tok, HD), bf),
            pltpu.VMEM((n_seq * slot, tok), bf),
            pltpu.VMEM((heads, n_seq, slot, HD), bf),
            pltpu.VMEM((heads, n_phase, n_seq, slot, HD), bf),
            pltpu.VMEM((n_phase, n_seq * slot, cols), f32),
            pltpu.VMEM((reach + 1, tok, 3 * HD), f32),
            pltpu.VMEM((n_phase, 8, n_seq * slot), f32),
            dma((7,)),
            dma(()),
            dma((heads, n_seq - 1)),
            dma(()),
            dma((heads + 1,)),
            dma(()),
            dma((2,)),
            dma(()),
            dma(()),
            dma((reach,)),
            dma((reach, 2)),
            dma((reach,)),
            dma((reach, 3)),
            dma(()),
            dma((heads, 3)),
            dma(()),
            dma((3,)),
            dma(()),
            dma(()),
            pltpu.SemaphoreType.REGULAR,
        ],
        compiler_params=pltpu.CompilerParams(
            collective_id=0, has_side_effects=True, vmem_limit_bytes=48 * 1024 * 1024
        ),
    )(
        in_hbm(byte_embed),
        in_hbm(in_gain),
        in_hbm(jnp.transpose(w_qkv, (1, 0, 2))),
        in_hbm(w_up),
        in_hbm(out_gain),
        in_hbm(bounds.reshape(1, crows)),
        in_hbm(owner.reshape(1, crows)),
    )
    return pl.pallas_call(
        flush_kernel,
        out_shape=(
            jax.ShapeDtypeStruct(states.shape, bf),
            jax.ShapeDtypeStruct(stretch.shape, bf),
        ),
        in_specs=[vmem] * 2,
        out_specs=(hbm, hbm),
        scratch_shapes=[dma((2,))],
        compiler_params=pltpu.CompilerParams(vmem_limit_bytes=4 * 1024 * 1024),
    )(states, stretch)


def passed_along(value, axis, by):
    devices = lax.axis_size(axis)
    pairs = [(i, i + by) for i in range(devices) if 0 <= i + by < devices]
    return lax.ppermute(value, axis, pairs)


def project_rows(rows, w_up, out_gain):
    groups = lax.axis_size("phase")
    full_rows = lax.all_gather(rows, "phase", axis=1, tiled=True)
    w_cols = lax.all_to_all(w_up, "phase", split_axis=1, concat_axis=0, tiled=True)
    count = full_rows.shape[0]
    width = rows.shape[1]
    columns = w_cols.shape[1]
    pieces = jnp.einsum(
        "nsg,sgc->snc",
        full_rows.reshape(count, groups, width),
        w_cols.reshape(groups, width, columns),
        preferred_element_type=jnp.float32,
    )
    projected = jnp.sum(pieces.astype(jnp.bfloat16).astype(jnp.float32), axis=0)
    squares = lax.psum(jnp.sum(projected * projected, axis=1), "phase")
    scale = lax.rsqrt(squares / DC + 1e-05)
    return (projected * scale[:, None] * out_gain).astype(jnp.bfloat16)


def on_device(byte_embed, in_gain, w_qkv, w_up, out_gain, bounds, owner):
    tok = byte_embed.shape[0]
    n_seq = lax.axis_size("seq")
    mine = lax.axis_index("seq")
    section = lax.axis_index("phase")
    width_dev = w_qkv.shape[2]
    heads_dev = width_dev // HD
    x32 = byte_embed.astype(jnp.float32)
    normed = (x32 * lax.rsqrt(jnp.mean(x32 * x32, axis=1, keepdims=True) + 1e-05) * in_gain).astype(
        jnp.bfloat16
    )
    piece = lax.all_gather(w_qkv, "seq", axis=0, tiled=True)
    qkv = jnp.dot(
        normed, piece.reshape(piece.shape[0], 3 * width_dev), preferred_element_type=jnp.float32
    ).astype(jnp.bfloat16)
    qkv = qkv.reshape(tok, 3, heads_dev, HD)
    query = qkv[:, 0]
    keys = qkv[:, 1]
    values = qkv[:, 2]
    reach = -(-WINDOW // tok)
    key_list = [keys]
    value_list = [values]
    for distance in range(1, reach + 1):
        earlier_keys, earlier_values = passed_along((keys, values), "seq", distance)
        key_list = [earlier_keys] + key_list
        value_list = [earlier_values] + value_list
    key_all = jnp.concatenate(key_list, axis=0)
    value_all = jnp.concatenate(value_list, axis=0)
    scores = jnp.einsum(
        "ihd,jhd->hij", query, key_all, preferred_element_type=jnp.float32
    ) * HD ** (-0.5)
    q_pos = mine * tok + jnp.arange(tok, dtype=jnp.int32)
    k_pos = mine * tok - reach * tok + jnp.arange((reach + 1) * tok, dtype=jnp.int32)
    keep = (
        (k_pos[None, :] <= q_pos[:, None])
        & (k_pos[None, :] > q_pos[:, None] - WINDOW)
        & (k_pos[None, :] >= 0)
    )
    scores = jnp.where(keep[None], scores, -jnp.inf)
    top = jnp.max(scores, axis=2, keepdims=True)
    expo = jnp.exp(scores - top)
    probs = (expo / jnp.sum(expo, axis=2, keepdims=True)).astype(jnp.bfloat16)
    attended = jnp.einsum(
        "hij,jhd->ihd", probs, value_all, preferred_element_type=jnp.float32
    ).astype(jnp.bfloat16)
    attended = attended.reshape(tok, width_dev)
    residual = lax.dynamic_slice_in_dim(x32, section * width_dev, width_dev, 1)
    byte_states = (residual + attended.astype(jnp.float32)).astype(jnp.bfloat16)
    local = bounds - mine * tok
    stretch_rows = jnp.take(byte_states, local, axis=0)
    owners = owner[:, 0]
    crows = owners.shape[0]
    slot_count = 2 * crows // n_seq
    place = jnp.arange(crows, dtype=jnp.int32)
    earlier = (owners[:, None] == owners[None, :]) & (place[None, :] < place[:, None])
    rank = jnp.sum(earlier.astype(jnp.int32), axis=1)
    target = owners * slot_count + rank
    placing = (target[None, :] == jnp.arange(n_seq * slot_count, dtype=jnp.int32)[:, None]).astype(
        jnp.bfloat16
    )
    outgoing = jnp.dot(placing, stretch_rows, preferred_element_type=jnp.float32).astype(
        jnp.bfloat16
    )
    outgoing = outgoing.reshape(n_seq, slot_count, width_dev)
    arrived = lax.all_to_all(outgoing, "seq", split_axis=0, concat_axis=0, tiled=True).reshape(
        n_seq * slot_count, width_dev
    )
    stretch_states = project_rows(arrived, w_up, out_gain)
    return (byte_states, stretch_states)


def solution(mesh):
    n_seq, n_phase, n_dp = (mesh.shape[axis] for axis in ("seq", "phase", "dp"))

    def body(byte_embed, in_gain, w_qkv, *rest):
        tok, (rows, _, width) = byte_embed.shape[0], w_qkv.shape
        slot = 2 * rest[2].shape[0] // n_seq
        tiled = rows % 128 == 0 and width % HD == 0 and tok % 256 == 0 and slot % 16 == 0
        fits = n_seq == n_phase and width == 3 * HD and WINDOW == 2 * tok
        if tiled and fits and n_dp == 2 and n_phase == 4 and w_qkv.shape[0] == rest[0].shape[0]:
            return fused(n_seq, n_phase, byte_embed, in_gain, w_qkv, *rest)
        return on_device(byte_embed, in_gain, w_qkv, *rest)

    return jax.shard_map(
        body,
        mesh=mesh,
        in_specs=(
            P(("dp", "seq"), None),
            P(),
            P("seq", None, "phase"),
            P("phase", None),
            P("phase"),
            P(("dp", "seq")),
            P(("dp", "seq"), None),
        ),
        out_specs=(P(("dp", "seq"), "phase"), P(("dp", "seq"), "phase")),
        check_vma=False,
    )
```

```python
import functools
import math
import jax
import jax.numpy as jnp
from jax import lax
from jax.experimental import pallas as pl
from jax.experimental.pallas import tpu as pltpu
from jax.sharding import PartitionSpec as P

DC = 3072
HD = 128
WINDOW = 1024
MESH = pl.DeviceIdType.MESH
NEG = -0.7 * 3.4e38


def fused_kernel(
    dims,
    x_ref,
    gain_ref,
    w_ref,
    up_ref,
    og_ref,
    bounds_ref,
    owner_ref,
    bs_ref,
    ss_ref,
    xbuf,
    gain,
    og,
    bnd,
    own,
    normed,
    halo,
    wbuf,
    upbuf,
    qbuf,
    kbuf,
    vbuf,
    place,
    outrows,
    arrived,
    acc,
    partial,
    sqbuf,
    loc_sem,
    w_send,
    w_recv,
    p_send,
    p_recv,
    up_send,
    up_recv,
    upp_send,
    upp_recv,
    h_send,
    h_recv,
    g_send,
    g_recv,
    row_send,
    row_recv,
    all_send,
    all_recv,
    sq_send,
    sq_recv,
    go,
):
    n_seq, n_phase, reach, slot = dims
    tok, d = xbuf.shape
    rows, width = w_ref.shape[1:]
    half = rows // 2
    heads = width // HD
    last = heads - 1
    crows = bnd.shape[1]
    cols = og.shape[1]
    z = lax.axis_index("seq")
    p = lax.axis_index("phase")
    c = lax.axis_index("dp")

    own_x = pltpu.make_async_copy(x_ref, xbuf, loc_sem.at[0])
    own_x.start()
    small = []
    for i, (src, dst) in enumerate(
        ((gain_ref, gain.at[0]), (bounds_ref, bnd), (owner_ref, own), (og_ref, og.at[0]))
    ):
        small.append(pltpu.make_async_copy(src, dst, loc_sem.at[3 + i]))
        small[i].start()

    twin_core = {"dp": 1 - c}
    peers = (
        [{"seq": lax.rem(z + k, n_seq)} for k in range(1, n_seq)]
        + [{"phase": lax.rem(p + k, n_phase)} for k in range(1, n_phase)]
        + [twin_core]
    )
    barrier = pltpu.get_barrier_semaphore()
    for peer in peers:
        pl.semaphore_signal(barrier, inc=1, device_id=peer, device_id_type=MESH)
    edge = (z == 0) | (z == n_seq - 1)

    @pl.when(edge)
    def _():
        for k in range(1, n_phase):
            other = {"seq": n_seq - 1 - z, "phase": lax.rem(p + k, n_phase)}
            pl.semaphore_signal(barrier, inc=1, device_id=other, device_id_type=MESH)


    pl.semaphore_wait(barrier, len(peers) + jnp.where(edge, n_phase - 1, 0))

    def when(cond, action):
        if cond is None:
            action()
        else:
            pl.when(cond)(action)

    def move(src, dst, ssem, rsem, peer):
        return pltpu.make_async_remote_copy(
            src_ref=src, dst_ref=dst, send_sem=ssem, recv_sem=rsem, device_id=peer, device_id_type=MESH
        )

    def send(src, dst, ssem, rsem, peer, cond=None):
        copy = move(src, dst, ssem, rsem, peer)
        when(cond, copy.start)
        return copy

    def sent(ref, ssem, cond=None):
        when(cond, move(ref, ref, ssem, ssem, twin_core).wait_send)

    def landed(ref, rsem, cond=None):
        when(cond, move(ref, ref, rsem, rsem, twin_core).wait_recv)

    right, left = {"seq": z + 1}, {"seq": z - 1}
    has_right, has_left = z < n_seq - 1, z > 0
    ways = ((right, has_right, -1), (left, has_left, 1))
    RIGHTWARD, LEFTWARD = 0, 1

    def chunk(h, shard):
        at = pl.multiple_of(shard * rows + c * half, half)
        return wbuf.at[h, :, pl.ds(at, half), :]

    def slot_of(t, way):
        return t - 1 if way == LEFTWARD else n_seq - t - 1

    def issue_own(h, way, also=None):
        src = w_ref.at[:, pl.ds(pl.multiple_of(c * half, half), half), pl.ds(h * HD, HD)]
        peer, cond, sign = ways[way]
        cond = cond if also is None else cond & also
        send(src, chunk(h, z), w_send, w_recv.at[h, slot_of(1, way)], peer, cond)

    def relay(h, t, way, also=None):
        if t >= n_seq:
            return
        peer, cond, sign = ways[way]
        shard = z + sign * t
        here = (shard >= 0) & (shard < n_seq)
        there = here if also is None else here & also
        piece = chunk(h, jnp.clip(shard, 0, n_seq - 1))
        landed(piece, w_recv.at[h, slot_of(t, way)], there)
        if t < n_seq - 1:
            send(piece, piece, w_send, w_recv.at[h, slot_of(t + 1, way)], peer, there & cond)
        late = (way == RIGHTWARD) & (t == z)
        group = jnp.where(late, last + 1, h) if h == last else h
        send(piece, piece, p_send, p_recv.at[group], twin_core, there)

    def finish(h, late=None, also=True):
        if h < last:
            landed(wbuf.at[h, :, pl.ds(0, (n_seq - 1) * half)], p_recv.at[h])
        elif late:
            landed(wbuf.at[h, :, pl.ds(0, half)], p_recv.at[last + 1], (z > 0) & also)
        else:
            landed(wbuf.at[h, :, pl.ds(0, (n_seq - 2) * half)], p_recv.at[h], (z > 0) & also)
            landed(wbuf.at[h, :, pl.ds(0, (n_seq - 1) * half)], p_recv.at[h], (z == 0) & also)

    across = {1: {"phase": p + 1 - 2 * lax.rem(p, 2)}, 2: {"phase": lax.rem(p + 2, n_phase)}}
    spots = {k: v["phase"] for k, v in across.items()}
    partners = (n_phase - 1 - p, spots[1], spots[2])
    parts = [pl.ds(i * (tok // 2), tok // 2) for i in range(2)]
    mine, gathers = {}, {}

    def halo_start(dist, i, cond):
        if dist == 1:
            src = normed.at[parts[i], pl.ds(pl.multiple_of(p * width, 128), width)]
        else:
            src = halo.at[dist - 2, p, parts[i]]
        mine[dist, i] = send(
            src, halo.at[dist - 1, p, parts[i]], h_send.at[dist - 1], h_recv.at[dist - 1, i], right, cond
        )

    def halo_spread(dist, i):
        there = z >= dist
        pl.when(there)(mine[dist, i].wait_recv)
        if dist < reach:
            halo_start(dist + 1, i, there & has_right)
        piece = halo.at[dist - 1, p, parts[i]]
        for k in (1, 2):
            group = i if k == i + 1 else 2
            gathers[dist, i, k] = send(
                piece, piece, g_send.at[dist - 1], g_recv.at[dist - 1, group], across[k], there
            )

    def halo_pass(dist, i, also=True):
        there = (z >= dist) & also
        k = i + 1
        pl.when(there)(gathers[dist, i, k].wait_recv)
        piece = halo.at[dist - 1, spots[k], parts[i]]
        send(piece, piece, g_send.at[dist - 1], g_recv.at[dist - 1, 2], across[3 - k], there)

    def halo_wait(dist):
        @pl.when(z >= dist)
        def _():
            landed(halo.at[dist - 1, pl.ds(0, 2)], g_recv.at[dist - 1, 2])

    issue_own(0, RIGHTWARD)
    for h in range(heads):
        issue_own(h, LEFTWARD)
    up_rows = up_ref.shape[0] // 2
    up_half = pl.ds(pl.multiple_of(c * up_rows, up_rows), up_rows)

    def up_out(k, also=None):
        other = spots[k] if k < 3 else n_phase - 1 - p
        part = pl.ds(pl.multiple_of(other * cols, 128), cols)
        group = 0 if k < 3 else 1
        dst = upbuf.at[p, up_half]
        send(up_ref.at[up_half, part], dst, up_send, up_recv.at[group], {"phase": other}, also)

    def up_in(k):
        piece = upbuf.at[spots[k] if k < 3 else n_phase - 1 - p, up_half]
        send(piece, piece, upp_send, upp_recv, twin_core)

    for k in (1, 2):
        up_out(k)
    mine_w = wbuf.at[:, :, pl.ds(pl.multiple_of(z * rows, rows), rows), :]
    for h in range(heads):
        pltpu.make_async_copy(
            w_ref.at[:, :, pl.ds(h * HD, HD)],
            wbuf.at[h, :, pl.ds(pl.multiple_of(z * rows, rows), rows), :],
            loc_sem.at[2],
        ).start()
    own_up = pltpu.make_async_copy(
        up_ref.at[:, pl.ds(pl.multiple_of(p * cols, 128), cols)], upbuf.at[p], loc_sem.at[1]
    )
    own_up.start()

    own_x.wait()
    small[0].wait()
    step_rows = 64


    @pl.loop(0, tok // step_rows)
    def _(i):
        r = pl.ds(pl.multiple_of(i * step_rows, step_rows), step_rows)
        xx = xbuf[r, :].astype(jnp.float32)
        scale = lax.rsqrt(jnp.mean(xx * xx, axis=1, keepdims=True) + 1e-05)
        normed[r, :] = (xx * scale * gain[...]).astype(jnp.bfloat16)

    for i in range(2):
        halo_start(1, i, has_right)
    first, second, final = z == 0, z == 1, z == n_seq - 1
    for h in range(1, heads):
        issue_own(h, RIGHTWARD, first)

    def column(ref):
        wide = jnp.broadcast_to(ref[...].astype(jnp.float32), (crows, crows))
        return wide.T

    relay(0, 1, RIGHTWARD)
    relay(0, 1, LEFTWARD)
    pltpu.make_async_copy(mine_w, mine_w, loc_sem.at[2]).wait()
    for copy in small[1:]:
        copy.wait()
    local = column(bnd)[:, 0:1] - (z * tok).astype(jnp.float32)
    spot = lax.broadcasted_iota(jnp.int32, (crows, tok), 1).astype(jnp.float32)
    pick = jnp.where(local == spot, 1.0, 0.0).astype(jnp.bfloat16)
    same = column(own) == own[...].astype(jnp.float32)
    before = lax.broadcasted_iota(jnp.int32, (crows, crows), 0) < lax.broadcasted_iota(
        jnp.int32, (crows, crows), 1
    )
    rank = jnp.sum(jnp.where(same & before, 1, 0), axis=0, keepdims=True)
    target = own[...] * slot + rank
    route = jnp.where(
        target == lax.broadcasted_iota(jnp.int32, (n_seq * slot, crows), 0), 1.0, 0.0
    ).astype(jnp.bfloat16)
    place[...] = jnp.dot(route, pick, preferred_element_type=jnp.float32).astype(jnp.bfloat16)

    tq = min(tok, 256)
    scale = HD ** (-0.5) * math.log2(math.e)

    def scores(h, r, q0, dist, k0, size):
        s = lax.dot_general(
            qbuf[h, r, :],
            kbuf[h, dist, k0 : k0 + size],
            (((1,), (1,)), ((), ())),
            preferred_element_type=jnp.float32,
        )
        ahead = k0 - dist * tok - q0
        if ahead + size - 1 > 0 or ahead - (tq - 1) <= -WINDOW:
            gap = lax.broadcasted_iota(jnp.int32, s.shape, 1) - lax.broadcasted_iota(jnp.int32, s.shape, 0)
            s = jnp.where((gap <= -ahead) & (gap > -ahead - WINDOW), s, NEG)
        return s

    def chunks(dist, q0, size=256):
        out = []
        for k0 in range(0, tok, size):
            ahead = k0 - dist * tok - q0
            if ahead - (tq - 1) <= 0 and ahead + size - 1 > -WINDOW:
                out.append((dist, k0, size))
        return out

    def attend(h, dists):
        tiles = []
        for q0 in range(0, tok, tq):
            r = pl.ds(q0, tq)
            where = [at for dist in dists for at in chunks(dist, q0)]
            tiles.append((r, where, [scores(h, r, q0, *at) for at in where]))
        for r, where, parts in tiles:
            top = jnp.max(functools.reduce(jnp.maximum, parts), axis=1, keepdims=True)
            low = top * scale
            es = [jnp.exp2(s * scale - low) for s in parts]
            total = jnp.sum(functools.reduce(jnp.add, es), axis=1, keepdims=True)
            e = jnp.concatenate([e.astype(jnp.bfloat16) for e in es], axis=1)
            v = jnp.concatenate([vbuf[h, dist, k0 : k0 + size] for dist, k0, size in where], axis=0)
            o = jnp.dot(e, v, preferred_element_type=jnp.float32)
            att = (o / total).astype(jnp.bfloat16).astype(jnp.float32)
            res = xbuf[r, pl.ds(pl.multiple_of(p * width + h * HD, HD), HD)].astype(jnp.float32)
            bs_ref[r, h * HD : (h + 1) * HD] = (res + att).astype(jnp.bfloat16)

    def store(h, dist, got):
        start = min(dist, 1) * HD
        if dist == 0:
            qbuf[h] = got[:, :HD]
        kbuf[h, dist] = got[:, HD - start : 2 * HD - start]
        vbuf[h, dist] = got[:, 2 * HD - start :]

    def project(h, dist, also=True):
        @pl.when((z >= dist) & also)
        def _():
            w = jnp.concatenate([wbuf[h, j] for j in range(min(dist, 1), 3)], axis=1)
            rows_in = (
                jnp.concatenate([halo[dist - 1, q] for q in range(n_phase)], axis=1)
                if dist
                else normed[...]
            )
            got = jnp.dot(rows_in, w, preferred_element_type=jnp.float32)
            store(h, dist, got.astype(jnp.bfloat16))

    def split_rows(dist):
        if dist == 0:
            return normed[:, :rows], normed[:, rows:]
        pieces = [halo[dist - 1, q] for q in range(n_phase)]
        return pieces[0], jnp.concatenate(pieces[1:], axis=1)

    def some_weights(dist, r):
        return jnp.concatenate([wbuf[last, j, r, :] for j in range(min(dist, 1), 3)], axis=1)

    def project_early(dist, also):
        @pl.when((z >= dist) & also)
        def _():
            got = jnp.dot(
                split_rows(dist)[1], some_weights(dist, slice(rows, None)), preferred_element_type=jnp.float32
            )
            partial[dist, :, pl.ds(min(dist, 1) * HD, got.shape[1])] = got

    def project_late(dist, also):
        @pl.when((z >= dist) & also)
        def _():
            got = jnp.dot(
                split_rows(dist)[0], some_weights(dist, slice(0, rows)), preferred_element_type=jnp.float32
            )
            start = min(dist, 1) * HD
            store(last, dist, (got + partial[dist, :, pl.ds(start, got.shape[1])]).astype(jnp.bfloat16))

    def heed(h):
        for n in range(reach + 1):

            @pl.when(z == n if n < reach else z >= n)
            def _():
                attend(h, list(range(n, -1, -1)))

    def hand_over(h):
        states = bs_ref[:, h * HD : (h + 1) * HD]
        routed = jnp.dot(place[...], states, preferred_element_type=jnp.float32).astype(jnp.bfloat16)
        for s in range(n_seq):
            outrows[h, s] = routed[s * slot : (s + 1) * slot]
        arrived[h, p, z] = outrows[h, z]
        rows_out(h, False)

    outer = n_seq - 2

    def close(h):
        heed(h)
        hand_over(h)

    def release(cond):
        @pl.when(cond)
        def _():
            for far in range(outer):
                pl.semaphore_signal(go, inc=1, device_id={"seq": far}, device_id_type=MESH)

    def rows_out(h, held):
        for k in range(1, n_seq):
            other = lax.rem(z + k, n_seq)
            wait = (z < outer) & (other >= outer)
            send(
                outrows.at[h, other],
                arrived.at[h, p, z],
                row_send,
                row_recv.at[h, jnp.maximum(z - (n_seq - 3), 0)],
                {"seq": other},
                wait if held else jnp.logical_not(wait),
            )
            if h == last and k == 1 and not held:
                for far in partners:
                    send(
                        outrows.at[h, 0],
                        arrived.at[h, p, n_seq - 1],
                        row_send,
                        all_recv.at[2],
                        {"seq": 0, "phase": far},
                        final,
                    )

    def rows_in(h, j, cond):
        if j == 0:
            landed(arrived.at[h, p, pl.ds(0, outer)], row_recv.at[h, 0], cond & (z >= outer))
            landed(arrived.at[h, p, pl.ds(0, outer - 1)], row_recv.at[h, 0], cond & (z < outer))
        else:
            src = outer + j - 1
            landed(arrived.at[h, p, src], row_recv.at[h, j], cond & (z != src))

    def spread(h, j, cond):
        rows_in(h, j, cond)
        piece = arrived.at[h, p, pl.ds(0, outer) if j == 0 else pl.ds(outer + j - 1, 1)]
        group = 1 + j // 2 if h == last else 0
        for other in partners:
            send(piece, piece, all_send.at[group], all_recv.at[group], {"phase": other}, cond)

    relay(1, 1, LEFTWARD)
    halo_spread(1, 0)
    relay(2, 1, LEFTWARD)
    landed(upbuf.at[pl.ds(0, 2), up_half], up_recv.at[0])
    for k in (1, 2):
        up_in(k)
    halo_spread(1, 1)
    for h in range(1, heads):
        issue_own(h, RIGHTWARD, second)
        relay(h, 1, RIGHTWARD, second)
    halo_pass(1, 0)
    relay(0, 2, RIGHTWARD)
    issue_own(1, RIGHTWARD, z > 1)
    halo_pass(1, 1)
    for t in range(2, n_seq):
        for h in range(heads):
            relay(h, t, LEFTWARD)
    for dist in range(2, reach + 1):
        for i in range(2):
            halo_spread(dist, i)
    for t in range(3, n_seq):
        relay(0, t, RIGHTWARD)
    inner, outside = z < n_seq - 1, z < outer
    halo_pass(reach, 0, final)
    finish(0)
    project(0, 0)
    relay(1, 1, RIGHTWARD, (z > 1) & inner)
    halo_pass(reach, 0, inner)
    relay(1, 2, RIGHTWARD, inner)
    issue_own(2, RIGHTWARD, z > 1)
    for dist in range(1, reach):
        halo_wait(dist)
        project(0, dist)
    halo_pass(reach, 1)
    relay(1, 1, RIGHTWARD, final)
    relay(1, 2, RIGHTWARD, final)
    up_out(3, inner)
    for t in range(3, n_seq):
        relay(1, t, RIGHTWARD)

    @pl.when(final)
    def _():
        halo_wait(reach)
        project(0, reach)
        heed(0)

    up_out(3, final)
    finish(1)
    project(1, 0)
    relay(2, 1, RIGHTWARD, (z > 1) & inner)
    for dist in range(1, reach):
        project(1, dist)
    relay(2, 1, RIGHTWARD, final)
    relay(2, 2, RIGHTWARD, inner)
    finish(last, False, inner)
    finish(last, True, inner)
    project(last, 0, inner)
    for dist in range(1, reach):
        project(last, dist, inner)

    @pl.when(inner)
    def _():
        halo_wait(reach)
        project(0, reach)
        heed(0)

    hand_over(0)
    for h in range(1, last):
        project(h, reach)
        close(h)
    relay(last, 2, RIGHTWARD, final)
    release(final)
    for t in range(3, n_seq):
        relay(last, t, RIGHTWARD, c == 1)
    for h in range(last):
        spread(h, 2, final)
    finish(last, False, final)
    for dist in range(reach + 1):
        project_early(dist, final)
    for t in range(3, n_seq):
        relay(last, t, RIGHTWARD, c == 0)
    spread(0, 1, final)
    finish(last, True, final)
    for dist in range(reach + 1):
        project_late(dist, final)
    for h in range(last):
        spread(h, 1, z == outer)
    project(last, reach, inner)
    close(last)
    spread(last, 1, z == outer)
    spread(last, 2, final)
    for h in range(1, last):
        spread(h, 1, final)
    for h in range(heads):
        spread(h, 0, final)
    landed(upbuf.at[0, up_half], up_recv.at[1])
    up_in(3)
    for h in range(heads):
        spread(h, 0, outside)

    @pl.when(outside)
    def _():
        pl.semaphore_wait(go, 1)
        for h in range(heads):
            rows_out(h, True)

    for h in range(last):
        spread(h, 1, outside)
        spread(h, 2, inner)
    for h in range(heads):
        spread(h, 0, z == outer)
    spread(last, 1, z != outer)
    spread(last, 2, z == outer)
    own_up.wait()
    landed(upbuf.at[pl.ds(0, n_phase - 1), up_half], upp_recv)
    landed(arrived.at[pl.ds(0, last), pl.ds(0, n_phase - 1)], all_recv.at[0])
    full = n_seq * slot
    cut = full - slot

    def rows_of(s, hs):
        return jnp.concatenate([arrived[h, s].reshape(full, HD) for h in hs], axis=1)

    for k in range(n_phase):
        s = lax.rem(p + n_phase - k, n_phase)
        acc[k] = jnp.dot(
            rows_of(s, range(last)), upbuf[s, : last * HD, :], preferred_element_type=jnp.float32
        )

    def complete(j):
        r = slice(0, cut) if j == 0 else slice(cut, full)
        projected = 0.0
        for k in range(n_phase):
            s = lax.rem(p + n_phase - k, n_phase)
            srcs = pl.ds(0, n_seq - 1) if j == 0 else pl.ds(n_seq - 1, 1)
            lhs = arrived[last, s, srcs].reshape(r.stop - r.start, HD)
            got = acc[k, r, :] + jnp.dot(lhs, upbuf[s, last * HD :, :], preferred_element_type=jnp.float32)
            projected = projected + got.astype(jnp.bfloat16).astype(jnp.float32)
        acc[0, r, :] = projected
        sq = jnp.sum(projected * projected, axis=1, keepdims=True)
        return jnp.broadcast_to(sq, (r.stop - r.start, 128))

    spread(last, 2, outside & (z > 0))
    landed(arrived.at[last, pl.ds(0, n_phase - 1), pl.ds(0, n_seq - 1)], all_recv.at[1])
    sq_top = complete(0)
    landed(arrived.at[last, pl.ds(0, n_phase - 1), pl.ds(0, 1)], all_recv.at[2])
    rows_in(last, 2, z == 0)
    sq_all = jnp.concatenate([sq_top, complete(1)], axis=0)
    sqbuf[p] = sq_all.T[0:1, :]
    for other in partners:
        send(sqbuf.at[p], sqbuf.at[p], sq_send, sq_recv, {"phase": other})
    landed(sqbuf.at[pl.ds(0, n_phase - 1)], sq_recv)
    all_sq = sqbuf[0]
    for k in range(1, n_phase):
        all_sq = all_sq + sqbuf[k]
    all_sq = jnp.broadcast_to(all_sq[0:1, :], (128, full)).T[:, 0:1]
    norm = lax.rsqrt(all_sq / (n_phase * cols) + 1e-05)
    ss_ref[...] = (acc[0] * norm * og[...]).astype(jnp.bfloat16)
    sent(wbuf.at[:, :, pl.ds(0, half)], w_send, first | final)
    sent(wbuf.at[:, :, pl.ds(0, (n_seq + 1) * half)], w_send, jnp.logical_not(first | final))
    sent(wbuf.at[:, :, pl.ds(0, (n_seq - 1) * half)], p_send)
    sent(upbuf.at[pl.ds(0, n_phase - 1), up_half], up_send)
    sent(upbuf.at[pl.ds(0, n_phase - 1), up_half], upp_send)
    for dist in range(1, reach + 1):
        sent(halo.at[dist - 1, 0], h_send.at[dist - 1], (z >= dist - 1) & has_right)
        sent(halo.at[dist - 1, pl.ds(0, 3)], g_send.at[dist - 1], z >= dist)
    sent(outrows.at[:, pl.ds(0, n_seq - 1)], row_send, inner)
    sent(outrows.at[:, pl.ds(0, n_seq)], row_send, final)
    sent(arrived.at[pl.ds(0, last), pl.ds(0, n_phase - 1)], all_send.at[0])
    sent(arrived.at[last, pl.ds(0, n_phase - 1), pl.ds(0, n_seq - 1)], all_send.at[1])
    sent(arrived.at[last, pl.ds(0, n_phase - 1), pl.ds(0, 1)], all_send.at[2], z > 0)
    sent(sqbuf.at[pl.ds(0, n_phase - 1)], sq_send)


def flush_kernel(a_ref, b_ref, a_out, b_out, sems):
    copies = [
        pltpu.make_async_copy(a_ref, a_out, sems.at[0]),
        pltpu.make_async_copy(b_ref, b_out, sems.at[1]),
    ]
    for copy in copies:
        copy.start()
    for copy in copies:
        copy.wait()


def fused(n_seq, n_phase, byte_embed, in_gain, w_qkv, w_up, out_gain, bounds, owner):
    tok, d = byte_embed.shape
    rows, _, width = w_qkv.shape
    heads = width // HD
    crows = bounds.shape[0]
    cols = out_gain.shape[0]
    slot = 2 * crows // n_seq
    reach = -(-WINDOW // tok)
    bf, f32 = jnp.bfloat16, jnp.float32
    vmem = pl.BlockSpec(memory_space=pltpu.VMEM)
    hbm = pl.BlockSpec(memory_space=pltpu.HBM)
    dma = pltpu.SemaphoreType.DMA
    in_hbm = lambda a: pltpu.with_memory_space_constraint(a, pltpu.HBM)
    states, stretch = pl.pallas_call(
        functools.partial(fused_kernel, (n_seq, n_phase, reach, slot)),
        out_shape=(
            jax.ShapeDtypeStruct((tok, width), bf),
            jax.ShapeDtypeStruct((n_seq * slot, cols), bf),
        ),
        in_specs=[hbm] * 7,
        out_specs=(vmem, vmem),
        scratch_shapes=[
            pltpu.VMEM((tok, d), bf),
            pltpu.VMEM((1, d), f32),
            pltpu.VMEM((1, cols), f32),
            pltpu.VMEM((1, crows), jnp.int32),
            pltpu.VMEM((1, crows), jnp.int32),
            pltpu.VMEM((tok, d), bf),
            pltpu.VMEM((reach, n_phase, tok, width), bf),
            pltpu.VMEM((heads, 3, n_seq * rows, HD), bf),
            pltpu.VMEM((n_phase, w_up.shape[0], cols), bf),
            pltpu.VMEM((heads, tok, HD), bf),
            pltpu.VMEM((heads, reach + 1, tok, HD), bf),
            pltpu.VMEM((heads, reach + 1, tok, HD), bf),
            pltpu.VMEM((n_seq * slot, tok), bf),
            pltpu.VMEM((heads, n_seq, slot, HD), bf),
            pltpu.VMEM((heads, n_phase, n_seq, slot, HD), bf),
            pltpu.VMEM((n_phase, n_seq * slot, cols), f32),
            pltpu.VMEM((reach + 1, tok, 3 * HD), f32),
            pltpu.VMEM((n_phase, 1, n_seq * slot), f32),
            dma((7,)),
            dma(()),
            dma((heads, n_seq - 1)),
            dma(()),
            dma((heads + 1,)),
            dma(()),
            dma((2,)),
            dma(()),
            dma(()),
            dma((reach,)),
            dma((reach, 2)),
            dma((reach,)),
            dma((reach, 3)),
            dma(()),
            dma((heads, 3)),
            dma((3,)),
            dma((3,)),
            dma(()),
            dma(()),
            pltpu.SemaphoreType.REGULAR,
        ],
        compiler_params=pltpu.CompilerParams(
            collective_id=0, has_side_effects=True, vmem_limit_bytes=48 * 1024 * 1024
        ),
    )(
        in_hbm(byte_embed),
        in_hbm(in_gain),
        in_hbm(jnp.transpose(w_qkv, (1, 0, 2))),
        in_hbm(w_up),
        in_hbm(out_gain),
        in_hbm(bounds.reshape(1, crows)),
        in_hbm(owner.reshape(1, crows)),
    )
    return pl.pallas_call(
        flush_kernel,
        out_shape=(
            jax.ShapeDtypeStruct(states.shape, bf),
            jax.ShapeDtypeStruct(stretch.shape, bf),
        ),
        in_specs=[vmem] * 2,
        out_specs=(hbm, hbm),
        scratch_shapes=[dma((2,))],
        compiler_params=pltpu.CompilerParams(vmem_limit_bytes=4 * 1024 * 1024),
    )(states, stretch)


def passed_along(value, axis, by):
    devices = lax.axis_size(axis)
    pairs = [(i, i + by) for i in range(devices) if 0 <= i + by < devices]
    return lax.ppermute(value, axis, pairs)


def project_rows(rows, w_up, out_gain):
    groups = lax.axis_size("phase")
    full_rows = lax.all_gather(rows, "phase", axis=1, tiled=True)
    w_cols = lax.all_to_all(w_up, "phase", split_axis=1, concat_axis=0, tiled=True)
    count = full_rows.shape[0]
    width = rows.shape[1]
    columns = w_cols.shape[1]
    pieces = jnp.einsum(
        "nsg,sgc->snc",
        full_rows.reshape(count, groups, width),
        w_cols.reshape(groups, width, columns),
        preferred_element_type=jnp.float32,
    )
    projected = jnp.sum(pieces.astype(jnp.bfloat16).astype(jnp.float32), axis=0)
    squares = lax.psum(jnp.sum(projected * projected, axis=1), "phase")
    scale = lax.rsqrt(squares / DC + 1e-05)
    return (projected * scale[:, None] * out_gain).astype(jnp.bfloat16)


def on_device(byte_embed, in_gain, w_qkv, w_up, out_gain, bounds, owner):
    tok = byte_embed.shape[0]
    n_seq = lax.axis_size("seq")
    mine = lax.axis_index("seq")
    section = lax.axis_index("phase")
    width_dev = w_qkv.shape[2]
    heads_dev = width_dev // HD
    x32 = byte_embed.astype(jnp.float32)
    normed = (x32 * lax.rsqrt(jnp.mean(x32 * x32, axis=1, keepdims=True) + 1e-05) * in_gain).astype(
        jnp.bfloat16
    )
    piece = lax.all_gather(w_qkv, "seq", axis=0, tiled=True)
    qkv = jnp.dot(
        normed, piece.reshape(piece.shape[0], 3 * width_dev), preferred_element_type=jnp.float32
    ).astype(jnp.bfloat16)
    qkv = qkv.reshape(tok, 3, heads_dev, HD)
    query = qkv[:, 0]
    keys = qkv[:, 1]
    values = qkv[:, 2]
    reach = -(-WINDOW // tok)
    key_list = [keys]
    value_list = [values]
    for distance in range(1, reach + 1):
        earlier_keys, earlier_values = passed_along((keys, values), "seq", distance)
        key_list = [earlier_keys] + key_list
        value_list = [earlier_values] + value_list
    key_all = jnp.concatenate(key_list, axis=0)
    value_all = jnp.concatenate(value_list, axis=0)
    scores = jnp.einsum(
        "ihd,jhd->hij", query, key_all, preferred_element_type=jnp.float32
    ) * HD ** (-0.5)
    q_pos = mine * tok + jnp.arange(tok, dtype=jnp.int32)
    k_pos = mine * tok - reach * tok + jnp.arange((reach + 1) * tok, dtype=jnp.int32)
    keep = (
        (k_pos[None, :] <= q_pos[:, None])
        & (k_pos[None, :] > q_pos[:, None] - WINDOW)
        & (k_pos[None, :] >= 0)
    )
    scores = jnp.where(keep[None], scores, -jnp.inf)
    top = jnp.max(scores, axis=2, keepdims=True)
    expo = jnp.exp(scores - top)
    probs = (expo / jnp.sum(expo, axis=2, keepdims=True)).astype(jnp.bfloat16)
    attended = jnp.einsum(
        "hij,jhd->ihd", probs, value_all, preferred_element_type=jnp.float32
    ).astype(jnp.bfloat16)
    attended = attended.reshape(tok, width_dev)
    residual = lax.dynamic_slice_in_dim(x32, section * width_dev, width_dev, 1)
    byte_states = (residual + attended.astype(jnp.float32)).astype(jnp.bfloat16)
    local = bounds - mine * tok
    stretch_rows = jnp.take(byte_states, local, axis=0)
    owners = owner[:, 0]
    crows = owners.shape[0]
    slot_count = 2 * crows // n_seq
    place = jnp.arange(crows, dtype=jnp.int32)
    earlier = (owners[:, None] == owners[None, :]) & (place[None, :] < place[:, None])
    rank = jnp.sum(earlier.astype(jnp.int32), axis=1)
    target = owners * slot_count + rank
    placing = (target[None, :] == jnp.arange(n_seq * slot_count, dtype=jnp.int32)[:, None]).astype(
        jnp.bfloat16
    )
    outgoing = jnp.dot(placing, stretch_rows, preferred_element_type=jnp.float32).astype(
        jnp.bfloat16
    )
    outgoing = outgoing.reshape(n_seq, slot_count, width_dev)
    arrived = lax.all_to_all(outgoing, "seq", split_axis=0, concat_axis=0, tiled=True).reshape(
        n_seq * slot_count, width_dev
    )
    stretch_states = project_rows(arrived, w_up, out_gain)
    return (byte_states, stretch_states)


def solution(mesh):
    n_seq, n_phase, n_dp = (mesh.shape[axis] for axis in ("seq", "phase", "dp"))

    def body(byte_embed, in_gain, w_qkv, *rest):
        tok, (rows, _, width) = byte_embed.shape[0], w_qkv.shape
        slot = 2 * rest[2].shape[0] // n_seq
        tiled = rows % 128 == 0 and width % HD == 0 and tok % 256 == 0 and slot % 16 == 0
        fits = n_seq == n_phase and width == 3 * HD and WINDOW == 2 * tok
        if tiled and fits and n_dp == 2 and n_phase == 4 and w_qkv.shape[0] == rest[0].shape[0]:
            return fused(n_seq, n_phase, byte_embed, in_gain, w_qkv, *rest)
        return on_device(byte_embed, in_gain, w_qkv, *rest)

    return jax.shard_map(
        body,
        mesh=mesh,
        in_specs=(
            P(("dp", "seq"), None),
            P(),
            P("seq", None, "phase"),
            P("phase", None),
            P("phase"),
            P(("dp", "seq")),
            P(("dp", "seq"), None),
        ),
        out_specs=(P(("dp", "seq"), "phase"), P(("dp", "seq"), "phase")),
        check_vma=False,
    )
```

```python
import functools
import math
import jax
import jax.numpy as jnp
from jax import lax
from jax.experimental import pallas as pl
from jax.experimental.pallas import tpu as pltpu
from jax.sharding import PartitionSpec as P

DC = 3072
HD = 128
WINDOW = 1024
MESH = pl.DeviceIdType.MESH
NEG = -0.7 * 3.4e38


def fused_kernel(
    dims,
    x_ref,
    gain_ref,
    w_ref,
    up_ref,
    og_ref,
    bounds_ref,
    owner_ref,
    bs_ref,
    ss_ref,
    xbuf,
    gain,
    og,
    bnd,
    own,
    normed,
    halo,
    wbuf,
    upbuf,
    qbuf,
    kbuf,
    vbuf,
    place,
    outrows,
    arrived,
    acc,
    partial,
    sqbuf,
    loc_sem,
    w_send,
    w_recv,
    p_send,
    p_recv,
    up_send,
    up_recv,
    upp_send,
    upp_recv,
    h_send,
    h_recv,
    g_send,
    g_recv,
    row_send,
    row_recv,
    all_send,
    all_recv,
    sq_send,
    sq_recv,
    go,
):
    n_seq, n_phase, reach, slot = dims
    tok, d = xbuf.shape
    rows, width = w_ref.shape[1:]
    half = rows // 2
    heads = width // HD
    last = heads - 1
    crows = bnd.shape[1]
    cols = og.shape[1]
    z = lax.axis_index("seq")
    p = lax.axis_index("phase")
    c = lax.axis_index("dp")

    own_x = pltpu.make_async_copy(x_ref, xbuf, loc_sem.at[0])
    own_x.start()
    small = []
    for i, (src, dst) in enumerate(
        ((gain_ref, gain.at[0]), (bounds_ref, bnd), (owner_ref, own), (og_ref, og.at[0]))
    ):
        small.append(pltpu.make_async_copy(src, dst, loc_sem.at[3 + i]))
        small[i].start()

    twin_core = {"dp": 1 - c}
    peers = (
        [{"seq": lax.rem(z + k, n_seq)} for k in range(1, n_seq)]
        + [{"phase": lax.rem(p + k, n_phase)} for k in range(1, n_phase)]
        + [twin_core]
    )
    barrier = pltpu.get_barrier_semaphore()
    for peer in peers:
        pl.semaphore_signal(barrier, inc=1, device_id=peer, device_id_type=MESH)
    edge = (z == 0) | (z == n_seq - 1)

    @pl.when(edge)
    def _():
        for k in range(1, n_phase):
            other = {"seq": n_seq - 1 - z, "phase": lax.rem(p + k, n_phase)}
            pl.semaphore_signal(barrier, inc=1, device_id=other, device_id_type=MESH)


    pl.semaphore_wait(barrier, len(peers) + jnp.where(edge, n_phase - 1, 0))

    def when(cond, action):
        if cond is None:
            action()
        else:
            pl.when(cond)(action)

    def move(src, dst, ssem, rsem, peer):
        return pltpu.make_async_remote_copy(
            src_ref=src, dst_ref=dst, send_sem=ssem, recv_sem=rsem, device_id=peer, device_id_type=MESH
        )

    def send(src, dst, ssem, rsem, peer, cond=None):
        copy = move(src, dst, ssem, rsem, peer)
        when(cond, copy.start)
        return copy

    def sent(ref, ssem, cond=None):
        when(cond, move(ref, ref, ssem, ssem, twin_core).wait_send)

    def landed(ref, rsem, cond=None):
        when(cond, move(ref, ref, rsem, rsem, twin_core).wait_recv)

    right, left = {"seq": z + 1}, {"seq": z - 1}
    has_right, has_left = z < n_seq - 1, z > 0
    ways = ((right, has_right, -1), (left, has_left, 1))
    RIGHTWARD, LEFTWARD = 0, 1

    def chunk(h, shard):
        at = pl.multiple_of(shard * rows + c * half, half)
        return wbuf.at[h, :, pl.ds(at, half), :]

    def slot_of(t, way):
        return t - 1 if way == LEFTWARD else n_seq - t - 1

    def issue_own(h, way, also=None):
        src = w_ref.at[:, pl.ds(pl.multiple_of(c * half, half), half), pl.ds(h * HD, HD)]
        peer, cond, sign = ways[way]
        cond = cond if also is None else cond & also
        send(src, chunk(h, z), w_send, w_recv.at[h, slot_of(1, way)], peer, cond)

    def relay(h, t, way, also=None):
        if t >= n_seq:
            return
        peer, cond, sign = ways[way]
        shard = z + sign * t
        here = (shard >= 0) & (shard < n_seq)
        there = here if also is None else here & also
        piece = chunk(h, jnp.clip(shard, 0, n_seq - 1))
        landed(piece, w_recv.at[h, slot_of(t, way)], there)
        if t < n_seq - 1:
            send(piece, piece, w_send, w_recv.at[h, slot_of(t + 1, way)], peer, there & cond)
        late = (way == RIGHTWARD) & (t == z)
        group = jnp.where(late, last + 1, h) if h == last else h
        send(piece, piece, p_send, p_recv.at[group], twin_core, there)

    def finish(h, late=None, also=True):
        if h < last:
            landed(wbuf.at[h, :, pl.ds(0, (n_seq - 1) * half)], p_recv.at[h])
        elif late:
            landed(wbuf.at[h, :, pl.ds(0, half)], p_recv.at[last + 1], (z > 0) & also)
        else:
            landed(wbuf.at[h, :, pl.ds(0, (n_seq - 2) * half)], p_recv.at[h], (z > 0) & also)
            landed(wbuf.at[h, :, pl.ds(0, (n_seq - 1) * half)], p_recv.at[h], (z == 0) & also)

    across = {1: {"phase": p + 1 - 2 * lax.rem(p, 2)}, 2: {"phase": lax.rem(p + 2, n_phase)}}
    spots = {k: v["phase"] for k, v in across.items()}
    partners = (n_phase - 1 - p, spots[1], spots[2])
    parts = [pl.ds(i * (tok // 2), tok // 2) for i in range(2)]
    mine, gathers = {}, {}

    def halo_start(dist, i, cond):
        if dist == 1:
            src = normed.at[parts[i], pl.ds(pl.multiple_of(p * width, 128), width)]
        else:
            src = halo.at[dist - 2, p, parts[i]]
        mine[dist, i] = send(
            src, halo.at[dist - 1, p, parts[i]], h_send.at[dist - 1], h_recv.at[dist - 1, i], right, cond
        )

    def halo_spread(dist, i):
        there = z >= dist
        pl.when(there)(mine[dist, i].wait_recv)
        if dist < reach:
            halo_start(dist + 1, i, there & has_right)
        piece = halo.at[dist - 1, p, parts[i]]
        for k in (1, 2):
            group = i if k == i + 1 else 2
            gathers[dist, i, k] = send(
                piece, piece, g_send.at[dist - 1], g_recv.at[dist - 1, group], across[k], there
            )

    def halo_pass(dist, i, also=True):
        there = (z >= dist) & also
        k = i + 1
        pl.when(there)(gathers[dist, i, k].wait_recv)
        piece = halo.at[dist - 1, spots[k], parts[i]]
        send(piece, piece, g_send.at[dist - 1], g_recv.at[dist - 1, 2], across[3 - k], there)

    def halo_wait(dist):
        @pl.when(z >= dist)
        def _():
            landed(halo.at[dist - 1, pl.ds(0, 2)], g_recv.at[dist - 1, 2])

    issue_own(0, RIGHTWARD)
    for h in range(heads):
        issue_own(h, LEFTWARD)
    up_rows = up_ref.shape[0] // 2
    up_half = pl.ds(pl.multiple_of(c * up_rows, up_rows), up_rows)

    def up_out(k, also=None):
        other = spots[k] if k < 3 else n_phase - 1 - p
        part = pl.ds(pl.multiple_of(other * cols, 128), cols)
        group = 0 if k < 3 else 1
        dst = upbuf.at[p, up_half]
        send(up_ref.at[up_half, part], dst, up_send, up_recv.at[group], {"phase": other}, also)

    def up_in(k):
        piece = upbuf.at[spots[k] if k < 3 else n_phase - 1 - p, up_half]
        send(piece, piece, upp_send, upp_recv, twin_core)

    for k in (1, 2):
        up_out(k)
    mine_w = wbuf.at[:, :, pl.ds(pl.multiple_of(z * rows, rows), rows), :]
    for h in range(heads):
        pltpu.make_async_copy(
            w_ref.at[:, :, pl.ds(h * HD, HD)],
            wbuf.at[h, :, pl.ds(pl.multiple_of(z * rows, rows), rows), :],
            loc_sem.at[2],
        ).start()
    own_up = pltpu.make_async_copy(
        up_ref.at[:, pl.ds(pl.multiple_of(p * cols, 128), cols)], upbuf.at[p], loc_sem.at[1]
    )
    own_up.start()

    own_x.wait()
    small[0].wait()
    step_rows = 64


    @pl.loop(0, tok // step_rows)
    def _(i):
        r = pl.ds(pl.multiple_of(i * step_rows, step_rows), step_rows)
        xx = xbuf[r, :].astype(jnp.float32)
        scale = lax.rsqrt(jnp.mean(xx * xx, axis=1, keepdims=True) + 1e-05)
        normed[r, :] = (xx * scale * gain[...]).astype(jnp.bfloat16)

    for i in range(2):
        halo_start(1, i, has_right)
    first, second, final = z == 0, z == 1, z == n_seq - 1
    for h in range(1, heads):
        issue_own(h, RIGHTWARD, first)

    def column(ref):
        wide = jnp.broadcast_to(ref[...].astype(jnp.float32), (crows, crows))
        return wide.T

    relay(0, 1, RIGHTWARD)
    relay(0, 1, LEFTWARD)
    pltpu.make_async_copy(mine_w, mine_w, loc_sem.at[2]).wait()
    for copy in small[1:]:
        copy.wait()
    local = column(bnd)[:, 0:1] - (z * tok).astype(jnp.float32)
    spot = lax.broadcasted_iota(jnp.int32, (crows, tok), 1).astype(jnp.float32)
    pick = jnp.where(local == spot, 1.0, 0.0).astype(jnp.bfloat16)
    same = column(own) == own[...].astype(jnp.float32)
    before = lax.broadcasted_iota(jnp.int32, (crows, crows), 0) < lax.broadcasted_iota(
        jnp.int32, (crows, crows), 1
    )
    rank = jnp.sum(jnp.where(same & before, 1, 0), axis=0, keepdims=True)
    target = own[...] * slot + rank
    route = jnp.where(
        target == lax.broadcasted_iota(jnp.int32, (n_seq * slot, crows), 0), 1.0, 0.0
    ).astype(jnp.bfloat16)
    place[...] = jnp.dot(route, pick, preferred_element_type=jnp.float32).astype(jnp.bfloat16)

    tq = min(tok, 256)
    scale = HD ** (-0.5) * math.log2(math.e)

    def scores(h, r, q0, dist, k0, size):
        s = lax.dot_general(
            qbuf[h, r, :],
            kbuf[h, dist, k0 : k0 + size],
            (((1,), (1,)), ((), ())),
            preferred_element_type=jnp.float32,
        )
        ahead = k0 - dist * tok - q0
        if ahead + size - 1 > 0 or ahead - (tq - 1) <= -WINDOW:
            gap = lax.broadcasted_iota(jnp.int32, s.shape, 1) - lax.broadcasted_iota(jnp.int32, s.shape, 0)
            s = jnp.where((gap <= -ahead) & (gap > -ahead - WINDOW), s, NEG)
        return s

    def chunks(dist, q0, size=256):
        out = []
        for k0 in range(0, tok, size):
            ahead = k0 - dist * tok - q0
            if ahead - (tq - 1) <= 0 and ahead + size - 1 > -WINDOW:
                out.append((dist, k0, size))
        return out

    def attend(h, dists):
        tiles = []
        for q0 in range(0, tok, tq):
            r = pl.ds(q0, tq)
            where = [at for dist in dists for at in chunks(dist, q0)]
            tiles.append((r, where, [scores(h, r, q0, *at) for at in where]))
        for r, where, parts in tiles:
            top = jnp.max(functools.reduce(jnp.maximum, parts), axis=1, keepdims=True)
            low = top * scale
            es = [jnp.exp2(s * scale - low) for s in parts]
            total = jnp.sum(functools.reduce(jnp.add, es), axis=1, keepdims=True)
            e = jnp.concatenate([e.astype(jnp.bfloat16) for e in es], axis=1)
            v = jnp.concatenate([vbuf[h, dist, k0 : k0 + size] for dist, k0, size in where], axis=0)
            o = jnp.dot(e, v, preferred_element_type=jnp.float32)
            att = (o / total).astype(jnp.bfloat16).astype(jnp.float32)
            res = xbuf[r, pl.ds(pl.multiple_of(p * width + h * HD, HD), HD)].astype(jnp.float32)
            bs_ref[r, h * HD : (h + 1) * HD] = (res + att).astype(jnp.bfloat16)

    def store(h, dist, got):
        start = min(dist, 1) * HD
        if dist == 0:
            qbuf[h] = got[:, :HD]
        kbuf[h, dist] = got[:, HD - start : 2 * HD - start]
        vbuf[h, dist] = got[:, 2 * HD - start :]

    def project(h, dist, also=True):
        @pl.when((z >= dist) & also)
        def _():
            w = jnp.concatenate([wbuf[h, j] for j in range(min(dist, 1), 3)], axis=1)
            rows_in = (
                jnp.concatenate([halo[dist - 1, q] for q in range(n_phase)], axis=1)
                if dist
                else normed[...]
            )
            got = jnp.dot(rows_in, w, preferred_element_type=jnp.float32)
            store(h, dist, got.astype(jnp.bfloat16))

    def split_rows(dist):
        if dist == 0:
            return normed[:, :rows], normed[:, rows:]
        pieces = [halo[dist - 1, q] for q in range(n_phase)]
        return pieces[0], jnp.concatenate(pieces[1:], axis=1)

    def some_weights(dist, r):
        return jnp.concatenate([wbuf[last, j, r, :] for j in range(min(dist, 1), 3)], axis=1)

    def project_early(dist, also):
        @pl.when((z >= dist) & also)
        def _():
            got = jnp.dot(
                split_rows(dist)[1], some_weights(dist, slice(rows, None)), preferred_element_type=jnp.float32
            )
            partial[dist, :, pl.ds(min(dist, 1) * HD, got.shape[1])] = got

    def project_late(dist, also):
        @pl.when((z >= dist) & also)
        def _():
            got = jnp.dot(
                split_rows(dist)[0], some_weights(dist, slice(0, rows)), preferred_element_type=jnp.float32
            )
            start = min(dist, 1) * HD
            store(last, dist, (got + partial[dist, :, pl.ds(start, got.shape[1])]).astype(jnp.bfloat16))

    def heed(h):
        for n in range(reach + 1):

            @pl.when(z == n if n < reach else z >= n)
            def _():
                attend(h, list(range(n, -1, -1)))

    def hand_over(h):
        states = bs_ref[:, h * HD : (h + 1) * HD]
        routed = jnp.dot(place[...], states, preferred_element_type=jnp.float32).astype(jnp.bfloat16)
        for s in range(n_seq):
            outrows[h, s] = routed[s * slot : (s + 1) * slot]
        arrived[h, p, z] = outrows[h, z]
        rows_out(h, False)

    outer = n_seq - 2

    def close(h):
        heed(h)
        hand_over(h)

    def release(cond):
        @pl.when(cond)
        def _():
            for far in range(outer):
                pl.semaphore_signal(go, inc=1, device_id={"seq": far}, device_id_type=MESH)

    def rows_out(h, held):
        for k in range(1, n_seq):
            other = lax.rem(z + k, n_seq)
            wait = (z < outer) & (other >= outer)
            send(
                outrows.at[h, other],
                arrived.at[h, p, z],
                row_send,
                row_recv.at[h, jnp.maximum(z - (n_seq - 3), 0)],
                {"seq": other},
                wait if held else jnp.logical_not(wait),
            )
            if h == last and k == 1 and not held:
                for far in partners:
                    send(
                        outrows.at[h, 0],
                        arrived.at[h, p, n_seq - 1],
                        row_send,
                        all_recv.at[2],
                        {"seq": 0, "phase": far},
                        final,
                    )

    def rows_in(h, j, cond):
        if j == 0:
            landed(arrived.at[h, p, pl.ds(0, outer)], row_recv.at[h, 0], cond & (z >= outer))
            landed(arrived.at[h, p, pl.ds(0, outer - 1)], row_recv.at[h, 0], cond & (z < outer))
        else:
            src = outer + j - 1
            landed(arrived.at[h, p, src], row_recv.at[h, j], cond & (z != src))

    def spread(h, j, cond):
        rows_in(h, j, cond)
        piece = arrived.at[h, p, pl.ds(0, outer) if j == 0 else pl.ds(outer + j - 1, 1)]
        group = 1 + j // 2 if h == last else 0
        for other in partners:
            send(piece, piece, all_send.at[group], all_recv.at[group], {"phase": other}, cond)

    relay(1, 1, LEFTWARD)
    halo_spread(1, 0)
    relay(2, 1, LEFTWARD)
    landed(upbuf.at[pl.ds(0, 2), up_half], up_recv.at[0])
    for k in (1, 2):
        up_in(k)
    halo_spread(1, 1)
    for h in range(1, heads):
        issue_own(h, RIGHTWARD, second)
        relay(h, 1, RIGHTWARD, second)
    halo_pass(1, 0)
    relay(0, 2, RIGHTWARD)
    issue_own(1, RIGHTWARD, z > 1)
    halo_pass(1, 1)
    for t in range(2, n_seq):
        for h in range(heads):
            relay(h, t, LEFTWARD)
    for dist in range(2, reach + 1):
        for i in range(2):
            halo_spread(dist, i)
    for t in range(3, n_seq):
        relay(0, t, RIGHTWARD)
    inner, outside = z < n_seq - 1, z < outer
    halo_pass(reach, 0, final)
    finish(0)
    project(0, 0)
    relay(1, 1, RIGHTWARD, (z > 1) & inner)
    halo_pass(reach, 0, inner)
    relay(1, 2, RIGHTWARD, inner)
    issue_own(2, RIGHTWARD, z > 1)
    for dist in range(1, reach):
        halo_wait(dist)
        project(0, dist)
    halo_pass(reach, 1)
    relay(1, 1, RIGHTWARD, final)
    relay(1, 2, RIGHTWARD, final)
    up_out(3, inner)
    for t in range(3, n_seq):
        relay(1, t, RIGHTWARD)

    @pl.when(final)
    def _():
        halo_wait(reach)
        project(0, reach)
        heed(0)

    up_out(3, final)
    finish(1)
    project(1, 0)
    relay(2, 1, RIGHTWARD, (z > 1) & inner)
    for dist in range(1, reach):
        project(1, dist)
    relay(2, 1, RIGHTWARD, final)
    relay(2, 2, RIGHTWARD, inner)
    finish(last, False, inner)
    finish(last, True, inner)
    project(last, 0, inner)
    for dist in range(1, reach):
        project(last, dist, inner)

    @pl.when(inner)
    def _():
        halo_wait(reach)
        project(0, reach)
        heed(0)

    hand_over(0)
    for h in range(1, last):
        project(h, reach)
        close(h)
    release(final)
    relay(last, 2, RIGHTWARD, final)
    for t in range(3, n_seq):
        relay(last, t, RIGHTWARD, c == 1)
    for h in range(last):
        spread(h, 2, final)
    finish(last, False, final)
    for dist in range(reach + 1):
        project_early(dist, final)
    for t in range(3, n_seq):
        relay(last, t, RIGHTWARD, c == 0)
    spread(0, 1, final)
    finish(last, True, final)
    for dist in range(reach + 1):
        project_late(dist, final)
    for h in range(1, last):
        spread(h, 1, final)
    for h in range(last):
        spread(h, 1, z == outer)
    project(last, reach, inner)
    close(last)
    spread(last, 1, z == outer)
    spread(last, 2, final)
    for h in range(heads):
        spread(h, 0, final)
    landed(upbuf.at[0, up_half], up_recv.at[1])
    up_in(3)
    for h in range(heads):
        spread(h, 0, outside)

    @pl.when(outside)
    def _():
        pl.semaphore_wait(go, 1)
        for h in range(heads):
            rows_out(h, True)

    for h in range(last):
        spread(h, 1, outside)
        spread(h, 2, inner)
    for h in range(heads):
        spread(h, 0, z == outer)
    spread(last, 1, z != outer)
    spread(last, 2, z == outer)
    own_up.wait()
    landed(upbuf.at[pl.ds(0, n_phase - 1), up_half], upp_recv)
    landed(arrived.at[pl.ds(0, last), pl.ds(0, n_phase - 1)], all_recv.at[0])
    full = n_seq * slot
    cut = full - slot

    def rows_of(s, hs):
        return jnp.concatenate([arrived[h, s].reshape(full, HD) for h in hs], axis=1)

    for k in range(n_phase):
        s = lax.rem(p + n_phase - k, n_phase)
        acc[k] = jnp.dot(
            rows_of(s, range(last)), upbuf[s, : last * HD, :], preferred_element_type=jnp.float32
        )

    def complete(j):
        r = slice(0, cut) if j == 0 else slice(cut, full)
        projected = 0.0
        for k in range(n_phase):
            s = lax.rem(p + n_phase - k, n_phase)
            srcs = pl.ds(0, n_seq - 1) if j == 0 else pl.ds(n_seq - 1, 1)
            lhs = arrived[last, s, srcs].reshape(r.stop - r.start, HD)
            got = acc[k, r, :] + jnp.dot(lhs, upbuf[s, last * HD :, :], preferred_element_type=jnp.float32)
            projected = projected + got.astype(jnp.bfloat16).astype(jnp.float32)
        acc[0, r, :] = projected
        sq = jnp.sum(projected * projected, axis=1, keepdims=True)
        return jnp.broadcast_to(sq, (r.stop - r.start, 128))

    spread(last, 2, outside & (z > 0))
    landed(arrived.at[last, pl.ds(0, n_phase - 1), pl.ds(0, n_seq - 1)], all_recv.at[1])
    sq_top = complete(0)
    landed(arrived.at[last, pl.ds(0, n_phase - 1), pl.ds(0, 1)], all_recv.at[2])
    rows_in(last, 2, z == 0)
    sq_all = jnp.concatenate([sq_top, complete(1)], axis=0)
    sqbuf[p] = sq_all.T[0:1, :]
    for other in partners:
        send(sqbuf.at[p], sqbuf.at[p], sq_send, sq_recv, {"phase": other})
    landed(sqbuf.at[pl.ds(0, n_phase - 1)], sq_recv)
    all_sq = sqbuf[0]
    for k in range(1, n_phase):
        all_sq = all_sq + sqbuf[k]
    all_sq = jnp.broadcast_to(all_sq[0:1, :], (128, full)).T[:, 0:1]
    norm = lax.rsqrt(all_sq / (n_phase * cols) + 1e-05)
    ss_ref[...] = (acc[0] * norm * og[...]).astype(jnp.bfloat16)
    sent(wbuf.at[:, :, pl.ds(0, half)], w_send, first | final)
    sent(wbuf.at[:, :, pl.ds(0, (n_seq + 1) * half)], w_send, jnp.logical_not(first | final))
    sent(wbuf.at[:, :, pl.ds(0, (n_seq - 1) * half)], p_send)
    sent(upbuf.at[pl.ds(0, n_phase - 1), up_half], up_send)
    sent(upbuf.at[pl.ds(0, n_phase - 1), up_half], upp_send)
    for dist in range(1, reach + 1):
        sent(halo.at[dist - 1, 0], h_send.at[dist - 1], (z >= dist - 1) & has_right)
        sent(halo.at[dist - 1, pl.ds(0, 3)], g_send.at[dist - 1], z >= dist)
    sent(outrows.at[:, pl.ds(0, n_seq - 1)], row_send, inner)
    sent(outrows.at[:, pl.ds(0, n_seq)], row_send, final)
    sent(arrived.at[pl.ds(0, last), pl.ds(0, n_phase - 1)], all_send.at[0])
    sent(arrived.at[last, pl.ds(0, n_phase - 1), pl.ds(0, n_seq - 1)], all_send.at[1])
    sent(arrived.at[last, pl.ds(0, n_phase - 1), pl.ds(0, 1)], all_send.at[2], z > 0)
    sent(sqbuf.at[pl.ds(0, n_phase - 1)], sq_send)


def flush_kernel(a_ref, b_ref, a_out, b_out, sems):
    copies = [
        pltpu.make_async_copy(a_ref, a_out, sems.at[0]),
        pltpu.make_async_copy(b_ref, b_out, sems.at[1]),
    ]
    for copy in copies:
        copy.start()
    for copy in copies:
        copy.wait()


def fused(n_seq, n_phase, byte_embed, in_gain, w_qkv, w_up, out_gain, bounds, owner):
    tok, d = byte_embed.shape
    rows, _, width = w_qkv.shape
    heads = width // HD
    crows = bounds.shape[0]
    cols = out_gain.shape[0]
    slot = 2 * crows // n_seq
    reach = -(-WINDOW // tok)
    bf, f32 = jnp.bfloat16, jnp.float32
    vmem = pl.BlockSpec(memory_space=pltpu.VMEM)
    hbm = pl.BlockSpec(memory_space=pltpu.HBM)
    dma = pltpu.SemaphoreType.DMA
    in_hbm = lambda a: pltpu.with_memory_space_constraint(a, pltpu.HBM)
    states, stretch = pl.pallas_call(
        functools.partial(fused_kernel, (n_seq, n_phase, reach, slot)),
        out_shape=(
            jax.ShapeDtypeStruct((tok, width), bf),
            jax.ShapeDtypeStruct((n_seq * slot, cols), bf),
        ),
        in_specs=[hbm] * 7,
        out_specs=(vmem, vmem),
        scratch_shapes=[
            pltpu.VMEM((tok, d), bf),
            pltpu.VMEM((1, d), f32),
            pltpu.VMEM((1, cols), f32),
            pltpu.VMEM((1, crows), jnp.int32),
            pltpu.VMEM((1, crows), jnp.int32),
            pltpu.VMEM((tok, d), bf),
            pltpu.VMEM((reach, n_phase, tok, width), bf),
            pltpu.VMEM((heads, 3, n_seq * rows, HD), bf),
            pltpu.VMEM((n_phase, w_up.shape[0], cols), bf),
            pltpu.VMEM((heads, tok, HD), bf),
            pltpu.VMEM((heads, reach + 1, tok, HD), bf),
            pltpu.VMEM((heads, reach + 1, tok, HD), bf),
            pltpu.VMEM((n_seq * slot, tok), bf),
            pltpu.VMEM((heads, n_seq, slot, HD), bf),
            pltpu.VMEM((heads, n_phase, n_seq, slot, HD), bf),
            pltpu.VMEM((n_phase, n_seq * slot, cols), f32),
            pltpu.VMEM((reach + 1, tok, 3 * HD), f32),
            pltpu.VMEM((n_phase, 1, n_seq * slot), f32),
            dma((7,)),
            dma(()),
            dma((heads, n_seq - 1)),
            dma(()),
            dma((heads + 1,)),
            dma(()),
            dma((2,)),
            dma(()),
            dma(()),
            dma((reach,)),
            dma((reach, 2)),
            dma((reach,)),
            dma((reach, 3)),
            dma(()),
            dma((heads, 3)),
            dma((3,)),
            dma((3,)),
            dma(()),
            dma(()),
            pltpu.SemaphoreType.REGULAR,
        ],
        compiler_params=pltpu.CompilerParams(
            collective_id=0, has_side_effects=True, vmem_limit_bytes=48 * 1024 * 1024
        ),
    )(
        in_hbm(byte_embed),
        in_hbm(in_gain),
        in_hbm(jnp.transpose(w_qkv, (1, 0, 2))),
        in_hbm(w_up),
        in_hbm(out_gain),
        in_hbm(bounds.reshape(1, crows)),
        in_hbm(owner.reshape(1, crows)),
    )
    return pl.pallas_call(
        flush_kernel,
        out_shape=(
            jax.ShapeDtypeStruct(states.shape, bf),
            jax.ShapeDtypeStruct(stretch.shape, bf),
        ),
        in_specs=[vmem] * 2,
        out_specs=(hbm, hbm),
        scratch_shapes=[dma((2,))],
        compiler_params=pltpu.CompilerParams(vmem_limit_bytes=4 * 1024 * 1024),
    )(states, stretch)


def passed_along(value, axis, by):
    devices = lax.axis_size(axis)
    pairs = [(i, i + by) for i in range(devices) if 0 <= i + by < devices]
    return lax.ppermute(value, axis, pairs)


def project_rows(rows, w_up, out_gain):
    groups = lax.axis_size("phase")
    full_rows = lax.all_gather(rows, "phase", axis=1, tiled=True)
    w_cols = lax.all_to_all(w_up, "phase", split_axis=1, concat_axis=0, tiled=True)
    count = full_rows.shape[0]
    width = rows.shape[1]
    columns = w_cols.shape[1]
    pieces = jnp.einsum(
        "nsg,sgc->snc",
        full_rows.reshape(count, groups, width),
        w_cols.reshape(groups, width, columns),
        preferred_element_type=jnp.float32,
    )
    projected = jnp.sum(pieces.astype(jnp.bfloat16).astype(jnp.float32), axis=0)
    squares = lax.psum(jnp.sum(projected * projected, axis=1), "phase")
    scale = lax.rsqrt(squares / DC + 1e-05)
    return (projected * scale[:, None] * out_gain).astype(jnp.bfloat16)


def on_device(byte_embed, in_gain, w_qkv, w_up, out_gain, bounds, owner):
    tok = byte_embed.shape[0]
    n_seq = lax.axis_size("seq")
    mine = lax.axis_index("seq")
    section = lax.axis_index("phase")
    width_dev = w_qkv.shape[2]
    heads_dev = width_dev // HD
    x32 = byte_embed.astype(jnp.float32)
    normed = (x32 * lax.rsqrt(jnp.mean(x32 * x32, axis=1, keepdims=True) + 1e-05) * in_gain).astype(
        jnp.bfloat16
    )
    piece = lax.all_gather(w_qkv, "seq", axis=0, tiled=True)
    qkv = jnp.dot(
        normed, piece.reshape(piece.shape[0], 3 * width_dev), preferred_element_type=jnp.float32
    ).astype(jnp.bfloat16)
    qkv = qkv.reshape(tok, 3, heads_dev, HD)
    query = qkv[:, 0]
    keys = qkv[:, 1]
    values = qkv[:, 2]
    reach = -(-WINDOW // tok)
    key_list = [keys]
    value_list = [values]
    for distance in range(1, reach + 1):
        earlier_keys, earlier_values = passed_along((keys, values), "seq", distance)
        key_list = [earlier_keys] + key_list
        value_list = [earlier_values] + value_list
    key_all = jnp.concatenate(key_list, axis=0)
    value_all = jnp.concatenate(value_list, axis=0)
    scores = jnp.einsum(
        "ihd,jhd->hij", query, key_all, preferred_element_type=jnp.float32
    ) * HD ** (-0.5)
    q_pos = mine * tok + jnp.arange(tok, dtype=jnp.int32)
    k_pos = mine * tok - reach * tok + jnp.arange((reach + 1) * tok, dtype=jnp.int32)
    keep = (
        (k_pos[None, :] <= q_pos[:, None])
        & (k_pos[None, :] > q_pos[:, None] - WINDOW)
        & (k_pos[None, :] >= 0)
    )
    scores = jnp.where(keep[None], scores, -jnp.inf)
    top = jnp.max(scores, axis=2, keepdims=True)
    expo = jnp.exp(scores - top)
    probs = (expo / jnp.sum(expo, axis=2, keepdims=True)).astype(jnp.bfloat16)
    attended = jnp.einsum(
        "hij,jhd->ihd", probs, value_all, preferred_element_type=jnp.float32
    ).astype(jnp.bfloat16)
    attended = attended.reshape(tok, width_dev)
    residual = lax.dynamic_slice_in_dim(x32, section * width_dev, width_dev, 1)
    byte_states = (residual + attended.astype(jnp.float32)).astype(jnp.bfloat16)
    local = bounds - mine * tok
    stretch_rows = jnp.take(byte_states, local, axis=0)
    owners = owner[:, 0]
    crows = owners.shape[0]
    slot_count = 2 * crows // n_seq
    place = jnp.arange(crows, dtype=jnp.int32)
    earlier = (owners[:, None] == owners[None, :]) & (place[None, :] < place[:, None])
    rank = jnp.sum(earlier.astype(jnp.int32), axis=1)
    target = owners * slot_count + rank
    placing = (target[None, :] == jnp.arange(n_seq * slot_count, dtype=jnp.int32)[:, None]).astype(
        jnp.bfloat16
    )
    outgoing = jnp.dot(placing, stretch_rows, preferred_element_type=jnp.float32).astype(
        jnp.bfloat16
    )
    outgoing = outgoing.reshape(n_seq, slot_count, width_dev)
    arrived = lax.all_to_all(outgoing, "seq", split_axis=0, concat_axis=0, tiled=True).reshape(
        n_seq * slot_count, width_dev
    )
    stretch_states = project_rows(arrived, w_up, out_gain)
    return (byte_states, stretch_states)


def solution(mesh):
    n_seq, n_phase, n_dp = (mesh.shape[axis] for axis in ("seq", "phase", "dp"))

    def body(byte_embed, in_gain, w_qkv, *rest):
        tok, (rows, _, width) = byte_embed.shape[0], w_qkv.shape
        slot = 2 * rest[2].shape[0] // n_seq
        tiled = rows % 128 == 0 and width % HD == 0 and tok % 256 == 0 and slot % 16 == 0
        fits = n_seq == n_phase and width == 3 * HD and WINDOW == 2 * tok
        if tiled and fits and n_dp == 2 and n_phase == 4 and w_qkv.shape[0] == rest[0].shape[0]:
            return fused(n_seq, n_phase, byte_embed, in_gain, w_qkv, *rest)
        return on_device(byte_embed, in_gain, w_qkv, *rest)

    return jax.shard_map(
        body,
        mesh=mesh,
        in_specs=(
            P(("dp", "seq"), None),
            P(),
            P("seq", None, "phase"),
            P("phase", None),
            P("phase"),
            P(("dp", "seq")),
            P(("dp", "seq"), None),
        ),
        out_specs=(P(("dp", "seq"), "phase"), P(("dp", "seq"), "phase")),
        check_vma=False,
    )
```

```python
import functools
import math
import jax
import jax.numpy as jnp
from jax import lax
from jax.experimental import pallas as pl
from jax.experimental.pallas import tpu as pltpu
from jax.sharding import PartitionSpec as P

DC = 3072
HD = 128
WINDOW = 1024
MESH = pl.DeviceIdType.MESH
NEG = -0.7 * 3.4e38


def fused_kernel(
    dims,
    x_ref,
    gain_ref,
    w_ref,
    up_ref,
    og_ref,
    bounds_ref,
    owner_ref,
    bs_ref,
    ss_ref,
    xbuf,
    gain,
    og,
    bnd,
    own,
    normed,
    halo,
    wbuf,
    upbuf,
    qbuf,
    kbuf,
    vbuf,
    place,
    outrows,
    arrived,
    acc,
    partial,
    sqbuf,
    loc_sem,
    w_send,
    w_recv,
    p_send,
    p_recv,
    up_send,
    up_recv,
    upp_send,
    upp_recv,
    h_send,
    h_recv,
    g_send,
    g_recv,
    row_send,
    row_recv,
    all_send,
    all_recv,
    sq_send,
    sq_recv,
    go,
):
    n_seq, n_phase, reach, slot = dims
    tok, d = xbuf.shape
    rows, width = w_ref.shape[1:]
    half = rows // 2
    heads = width // HD
    last = heads - 1
    crows = bnd.shape[1]
    cols = og.shape[1]
    z = lax.axis_index("seq")
    p = lax.axis_index("phase")
    c = lax.axis_index("dp")

    own_x = pltpu.make_async_copy(x_ref, xbuf, loc_sem.at[0])
    own_x.start()
    small = []
    for i, (src, dst) in enumerate(
        ((gain_ref, gain.at[0]), (bounds_ref, bnd), (owner_ref, own), (og_ref, og.at[0]))
    ):
        small.append(pltpu.make_async_copy(src, dst, loc_sem.at[3 + i]))
        small[i].start()

    twin_core = {"dp": 1 - c}
    peers = (
        [{"seq": lax.rem(z + k, n_seq)} for k in range(1, n_seq)]
        + [{"phase": lax.rem(p + k, n_phase)} for k in range(1, n_phase)]
        + [twin_core]
    )
    barrier = pltpu.get_barrier_semaphore()
    for peer in peers:
        pl.semaphore_signal(barrier, inc=1, device_id=peer, device_id_type=MESH)
    edge = (z == 0) | (z == n_seq - 1)

    @pl.when(edge)
    def _():
        for k in range(1, n_phase):
            other = {"seq": n_seq - 1 - z, "phase": lax.rem(p + k, n_phase)}
            pl.semaphore_signal(barrier, inc=1, device_id=other, device_id_type=MESH)


    pl.semaphore_wait(barrier, len(peers) + jnp.where(edge, n_phase - 1, 0))

    def when(cond, action):
        if cond is None:
            action()
        else:
            pl.when(cond)(action)

    def move(src, dst, ssem, rsem, peer):
        return pltpu.make_async_remote_copy(
            src_ref=src, dst_ref=dst, send_sem=ssem, recv_sem=rsem, device_id=peer, device_id_type=MESH
        )

    def send(src, dst, ssem, rsem, peer, cond=None):
        copy = move(src, dst, ssem, rsem, peer)
        when(cond, copy.start)
        return copy

    def sent(ref, ssem, cond=None):
        when(cond, move(ref, ref, ssem, ssem, twin_core).wait_send)

    def landed(ref, rsem, cond=None):
        when(cond, move(ref, ref, rsem, rsem, twin_core).wait_recv)

    right, left = {"seq": z + 1}, {"seq": z - 1}
    has_right, has_left = z < n_seq - 1, z > 0
    ways = ((right, has_right, -1), (left, has_left, 1))
    RIGHTWARD, LEFTWARD = 0, 1

    def chunk(h, shard):
        at = pl.multiple_of(shard * rows + c * half, half)
        return wbuf.at[h, :, pl.ds(at, half), :]

    def slot_of(t, way):
        return t - 1 if way == LEFTWARD else n_seq - t - 1

    def issue_own(h, way, also=None):
        src = w_ref.at[:, pl.ds(pl.multiple_of(c * half, half), half), pl.ds(h * HD, HD)]
        peer, cond, sign = ways[way]
        cond = cond if also is None else cond & also
        send(src, chunk(h, z), w_send, w_recv.at[h, slot_of(1, way)], peer, cond)

    def relay(h, t, way, also=None):
        if t >= n_seq:
            return
        peer, cond, sign = ways[way]
        shard = z + sign * t
        here = (shard >= 0) & (shard < n_seq)
        there = here if also is None else here & also
        piece = chunk(h, jnp.clip(shard, 0, n_seq - 1))
        landed(piece, w_recv.at[h, slot_of(t, way)], there)
        if t < n_seq - 1:
            send(piece, piece, w_send, w_recv.at[h, slot_of(t + 1, way)], peer, there & cond)
        late = (way == RIGHTWARD) & (t == z)
        group = jnp.where(late, last + 1, h) if h == last else h
        send(piece, piece, p_send, p_recv.at[group], twin_core, there)

    def finish(h, late=None, also=True):
        if h < last:
            landed(wbuf.at[h, :, pl.ds(0, (n_seq - 1) * half)], p_recv.at[h])
        elif late:
            landed(wbuf.at[h, :, pl.ds(0, half)], p_recv.at[last + 1], (z > 0) & also)
        else:
            landed(wbuf.at[h, :, pl.ds(0, (n_seq - 2) * half)], p_recv.at[h], (z > 0) & also)
            landed(wbuf.at[h, :, pl.ds(0, (n_seq - 1) * half)], p_recv.at[h], (z == 0) & also)

    across = {1: {"phase": p + 1 - 2 * lax.rem(p, 2)}, 2: {"phase": lax.rem(p + 2, n_phase)}}
    spots = {k: v["phase"] for k, v in across.items()}
    partners = (n_phase - 1 - p, spots[1], spots[2])
    parts = [pl.ds(i * (tok // 2), tok // 2) for i in range(2)]
    mine, gathers = {}, {}

    def halo_start(dist, i, cond):
        if dist == 1:
            src = normed.at[parts[i], pl.ds(pl.multiple_of(p * width, 128), width)]
        else:
            src = halo.at[dist - 2, p, parts[i]]
        mine[dist, i] = send(
            src, halo.at[dist - 1, p, parts[i]], h_send.at[dist - 1], h_recv.at[dist - 1, i], right, cond
        )

    def halo_spread(dist, i):
        there = z >= dist
        pl.when(there)(mine[dist, i].wait_recv)
        if dist < reach:
            halo_start(dist + 1, i, there & has_right)
        piece = halo.at[dist - 1, p, parts[i]]
        for k in (1, 2):
            group = i if k == i + 1 else 2
            gathers[dist, i, k] = send(
                piece, piece, g_send.at[dist - 1], g_recv.at[dist - 1, group], across[k], there
            )

    def halo_pass(dist, i, also=True):
        there = (z >= dist) & also
        k = i + 1
        pl.when(there)(gathers[dist, i, k].wait_recv)
        piece = halo.at[dist - 1, spots[k], parts[i]]
        send(piece, piece, g_send.at[dist - 1], g_recv.at[dist - 1, 2], across[3 - k], there)

    def halo_wait(dist):
        @pl.when(z >= dist)
        def _():
            landed(halo.at[dist - 1, pl.ds(0, 2)], g_recv.at[dist - 1, 2])

    issue_own(0, RIGHTWARD)
    for h in range(heads):
        issue_own(h, LEFTWARD)
    up_rows = up_ref.shape[0] // 2
    up_half = pl.ds(pl.multiple_of(c * up_rows, up_rows), up_rows)

    def up_out(k, also=None):
        other = spots[k] if k < 3 else n_phase - 1 - p
        part = pl.ds(pl.multiple_of(other * cols, 128), cols)
        group = 0 if k < 3 else 1
        dst = upbuf.at[p, up_half]
        send(up_ref.at[up_half, part], dst, up_send, up_recv.at[group], {"phase": other}, also)

    def up_in(k):
        piece = upbuf.at[spots[k] if k < 3 else n_phase - 1 - p, up_half]
        send(piece, piece, upp_send, upp_recv, twin_core)

    for k in (1, 2):
        up_out(k)
    mine_w = wbuf.at[:, :, pl.ds(pl.multiple_of(z * rows, rows), rows), :]
    for h in range(heads):
        pltpu.make_async_copy(
            w_ref.at[:, :, pl.ds(h * HD, HD)],
            wbuf.at[h, :, pl.ds(pl.multiple_of(z * rows, rows), rows), :],
            loc_sem.at[2],
        ).start()
    own_up = pltpu.make_async_copy(
        up_ref.at[:, pl.ds(pl.multiple_of(p * cols, 128), cols)], upbuf.at[p], loc_sem.at[1]
    )
    own_up.start()

    own_x.wait()
    small[0].wait()
    step_rows = 64


    @pl.loop(0, tok // step_rows)
    def _(i):
        r = pl.ds(pl.multiple_of(i * step_rows, step_rows), step_rows)
        xx = xbuf[r, :].astype(jnp.float32)
        scale = lax.rsqrt(jnp.mean(xx * xx, axis=1, keepdims=True) + 1e-05)
        normed[r, :] = (xx * scale * gain[...]).astype(jnp.bfloat16)

    for i in range(2):
        halo_start(1, i, has_right)
    first, second, final = z == 0, z == 1, z == n_seq - 1
    for h in range(1, heads):
        issue_own(h, RIGHTWARD, first)

    def column(ref):
        wide = jnp.broadcast_to(ref[...].astype(jnp.float32), (crows, crows))
        return wide.T

    relay(0, 1, RIGHTWARD)
    relay(0, 1, LEFTWARD)
    pltpu.make_async_copy(mine_w, mine_w, loc_sem.at[2]).wait()
    for copy in small[1:]:
        copy.wait()
    local = column(bnd)[:, 0:1] - (z * tok).astype(jnp.float32)
    spot = lax.broadcasted_iota(jnp.int32, (crows, tok), 1).astype(jnp.float32)
    pick = jnp.where(local == spot, 1.0, 0.0).astype(jnp.bfloat16)
    same = column(own) == own[...].astype(jnp.float32)
    before = lax.broadcasted_iota(jnp.int32, (crows, crows), 0) < lax.broadcasted_iota(
        jnp.int32, (crows, crows), 1
    )
    rank = jnp.sum(jnp.where(same & before, 1, 0), axis=0, keepdims=True)
    target = own[...] * slot + rank
    route = jnp.where(
        target == lax.broadcasted_iota(jnp.int32, (n_seq * slot, crows), 0), 1.0, 0.0
    ).astype(jnp.bfloat16)
    place[...] = jnp.dot(route, pick, preferred_element_type=jnp.float32).astype(jnp.bfloat16)

    tq = min(tok, 256)
    scale = HD ** (-0.5) * math.log2(math.e)

    def scores(h, r, q0, dist, k0, size):
        s = lax.dot_general(
            qbuf[h, r, :],
            kbuf[h, dist, k0 : k0 + size],
            (((1,), (1,)), ((), ())),
            preferred_element_type=jnp.float32,
        )
        ahead = k0 - dist * tok - q0
        if ahead + size - 1 > 0 or ahead - (tq - 1) <= -WINDOW:
            gap = lax.broadcasted_iota(jnp.int32, s.shape, 1) - lax.broadcasted_iota(jnp.int32, s.shape, 0)
            s = jnp.where((gap <= -ahead) & (gap > -ahead - WINDOW), s, NEG)
        return s

    def chunks(dist, q0, size=256):
        out = []
        for k0 in range(0, tok, size):
            ahead = k0 - dist * tok - q0
            if ahead - (tq - 1) <= 0 and ahead + size - 1 > -WINDOW:
                out.append((dist, k0, size))
        return out

    def attend(h, dists):
        tiles = []
        for q0 in range(0, tok, tq):
            r = pl.ds(q0, tq)
            where = [at for dist in dists for at in chunks(dist, q0)]
            tiles.append((r, where, [scores(h, r, q0, *at) for at in where]))
        for r, where, parts in tiles:
            top = jnp.max(functools.reduce(jnp.maximum, parts), axis=1, keepdims=True)
            low = top * scale
            es = [jnp.exp2(s * scale - low) for s in parts]
            total = jnp.sum(functools.reduce(jnp.add, es), axis=1, keepdims=True)
            e = jnp.concatenate([e.astype(jnp.bfloat16) for e in es], axis=1)
            v = jnp.concatenate([vbuf[h, dist, k0 : k0 + size] for dist, k0, size in where], axis=0)
            o = jnp.dot(e, v, preferred_element_type=jnp.float32)
            att = (o / total).astype(jnp.bfloat16).astype(jnp.float32)
            res = xbuf[r, pl.ds(pl.multiple_of(p * width + h * HD, HD), HD)].astype(jnp.float32)
            bs_ref[r, h * HD : (h + 1) * HD] = (res + att).astype(jnp.bfloat16)

    def store(h, dist, got):
        start = min(dist, 1) * HD
        if dist == 0:
            qbuf[h] = got[:, :HD]
        kbuf[h, dist] = got[:, HD - start : 2 * HD - start]
        vbuf[h, dist] = got[:, 2 * HD - start :]

    def project(h, dist, also=True):
        @pl.when((z >= dist) & also)
        def _():
            w = jnp.concatenate([wbuf[h, j] for j in range(min(dist, 1), 3)], axis=1)
            rows_in = (
                jnp.concatenate([halo[dist - 1, q] for q in range(n_phase)], axis=1)
                if dist
                else normed[...]
            )
            got = jnp.dot(rows_in, w, preferred_element_type=jnp.float32)
            store(h, dist, got.astype(jnp.bfloat16))

    def split_rows(dist):
        if dist == 0:
            return normed[:, :rows], normed[:, rows:]
        pieces = [halo[dist - 1, q] for q in range(n_phase)]
        return pieces[0], jnp.concatenate(pieces[1:], axis=1)

    def some_weights(dist, r):
        return jnp.concatenate([wbuf[last, j, r, :] for j in range(min(dist, 1), 3)], axis=1)

    def project_early(dist, also):
        @pl.when((z >= dist) & also)
        def _():
            got = jnp.dot(
                split_rows(dist)[1], some_weights(dist, slice(rows, None)), preferred_element_type=jnp.float32
            )
            partial[dist, :, pl.ds(min(dist, 1) * HD, got.shape[1])] = got

    def project_late(dist, also):
        @pl.when((z >= dist) & also)
        def _():
            got = jnp.dot(
                split_rows(dist)[0], some_weights(dist, slice(0, rows)), preferred_element_type=jnp.float32
            )
            start = min(dist, 1) * HD
            store(last, dist, (got + partial[dist, :, pl.ds(start, got.shape[1])]).astype(jnp.bfloat16))

    def heed(h):
        for n in range(reach + 1):

            @pl.when(z == n if n < reach else z >= n)
            def _():
                attend(h, list(range(n, -1, -1)))

    def hand_over(h):
        states = bs_ref[:, h * HD : (h + 1) * HD]
        routed = jnp.dot(place[...], states, preferred_element_type=jnp.float32).astype(jnp.bfloat16)
        for s in range(n_seq):
            outrows[h, s] = routed[s * slot : (s + 1) * slot]
        arrived[h, p, z] = outrows[h, z]
        rows_out(h, False)

    outer = n_seq - 2

    def close(h):
        heed(h)
        hand_over(h)

    def release(cond):
        @pl.when(cond)
        def _():
            for far in range(outer):
                pl.semaphore_signal(go, inc=1, device_id={"seq": far}, device_id_type=MESH)

    def rows_out(h, held):
        for k in reversed(range(1, n_seq)) if held else range(1, n_seq):
            other = lax.rem(z + k, n_seq)
            wait = (z < outer) & (other >= outer)
            send(
                outrows.at[h, other],
                arrived.at[h, p, z],
                row_send,
                row_recv.at[h, jnp.maximum(z - (n_seq - 3), 0)],
                {"seq": other},
                wait if held else jnp.logical_not(wait),
            )
            if h == last and k == 1 and not held:
                for far in partners:
                    send(
                        outrows.at[h, 0],
                        arrived.at[h, p, n_seq - 1],
                        row_send,
                        all_recv.at[2],
                        {"seq": 0, "phase": far},
                        final,
                    )

    def rows_in(h, j, cond):
        if j == 0:
            landed(arrived.at[h, p, pl.ds(0, outer)], row_recv.at[h, 0], cond & (z >= outer))
            landed(arrived.at[h, p, pl.ds(0, outer - 1)], row_recv.at[h, 0], cond & (z < outer))
        else:
            src = outer + j - 1
            landed(arrived.at[h, p, src], row_recv.at[h, j], cond & (z != src))

    def spread(h, j, cond):
        rows_in(h, j, cond)
        piece = arrived.at[h, p, pl.ds(0, outer) if j == 0 else pl.ds(outer + j - 1, 1)]
        group = 1 + j // 2 if h == last else 0
        for other in partners:
            send(piece, piece, all_send.at[group], all_recv.at[group], {"phase": other}, cond)

    relay(1, 1, LEFTWARD)
    halo_spread(1, 0)
    relay(2, 1, LEFTWARD)
    landed(upbuf.at[pl.ds(0, 2), up_half], up_recv.at[0])
    for k in (1, 2):
        up_in(k)
    halo_spread(1, 1)
    for h in range(1, heads):
        issue_own(h, RIGHTWARD, second)
        relay(h, 1, RIGHTWARD, second)
    halo_pass(1, 0)
    relay(0, 2, RIGHTWARD)
    issue_own(1, RIGHTWARD, z > 1)
    halo_pass(1, 1)
    for t in range(2, n_seq):
        for h in range(heads):
            relay(h, t, LEFTWARD)
    for dist in range(2, reach + 1):
        for i in range(2):
            halo_spread(dist, i)
    for t in range(3, n_seq):
        relay(0, t, RIGHTWARD)
    inner, outside = z < n_seq - 1, z < outer
    halo_pass(reach, 0, final)
    finish(0)
    project(0, 0)
    relay(1, 1, RIGHTWARD, (z > 1) & inner)
    halo_pass(reach, 0, inner)
    relay(1, 2, RIGHTWARD, inner)
    issue_own(2, RIGHTWARD, z > 1)
    for dist in range(1, reach):
        halo_wait(dist)
        project(0, dist)
    halo_pass(reach, 1)
    relay(1, 1, RIGHTWARD, final)
    relay(1, 2, RIGHTWARD, final)
    up_out(3, inner)
    for t in range(3, n_seq):
        relay(1, t, RIGHTWARD)

    @pl.when(final)
    def _():
        halo_wait(reach)
        project(0, reach)
        heed(0)

    up_out(3, final)
    finish(1)
    project(1, 0)
    relay(2, 1, RIGHTWARD, (z > 1) & inner)
    for dist in range(1, reach):
        project(1, dist)
    relay(2, 1, RIGHTWARD, final)
    relay(2, 2, RIGHTWARD, inner)
    finish(last, False, inner)
    finish(last, True, inner)
    project(last, 0, inner)
    for dist in range(1, reach):
        project(last, dist, inner)

    @pl.when(inner)
    def _():
        halo_wait(reach)
        project(0, reach)
        heed(0)

    hand_over(0)
    for h in range(1, last):
        project(h, reach)
        close(h)
    release(final)
    relay(last, 2, RIGHTWARD, final)
    for t in range(3, n_seq):
        relay(last, t, RIGHTWARD, c == 1)
    for h in range(last):
        spread(h, 2, final)
    finish(last, False, final)
    for dist in range(reach + 1):
        project_early(dist, final)
    for t in range(3, n_seq):
        relay(last, t, RIGHTWARD, c == 0)
    spread(0, 1, final)
    finish(last, True, final)
    for dist in range(reach + 1):
        project_late(dist, final)
    for h in range(1, last):
        spread(h, 1, final)
    for h in range(last):
        spread(h, 1, z == outer)
    project(last, reach, inner)
    close(last)
    spread(last, 1, z == outer)
    spread(last, 2, final)
    for h in range(heads):
        spread(h, 0, final)
    landed(upbuf.at[0, up_half], up_recv.at[1])
    up_in(3)
    for h in range(heads):
        spread(h, 0, outside)

    @pl.when(outside)
    def _():
        pl.semaphore_wait(go, 1)
        for h in range(heads):
            rows_out(h, True)

    for h in range(last):
        spread(h, 1, outside)
        spread(h, 2, inner)
    for h in range(heads):
        spread(h, 0, z == outer)
    spread(last, 1, z != outer)
    spread(last, 2, z == outer)
    own_up.wait()
    landed(upbuf.at[pl.ds(0, n_phase - 1), up_half], upp_recv)
    landed(arrived.at[pl.ds(0, last), pl.ds(0, n_phase - 1)], all_recv.at[0])
    full = n_seq * slot
    cut = full - slot

    def rows_of(s, hs):
        return jnp.concatenate([arrived[h, s].reshape(full, HD) for h in hs], axis=1)

    for k in range(n_phase):
        s = lax.rem(p + n_phase - k, n_phase)
        acc[k] = jnp.dot(
            rows_of(s, range(last)), upbuf[s, : last * HD, :], preferred_element_type=jnp.float32
        )

    def complete(j):
        r = slice(0, cut) if j == 0 else slice(cut, full)
        projected = 0.0
        for k in range(n_phase):
            s = lax.rem(p + n_phase - k, n_phase)
            srcs = pl.ds(0, n_seq - 1) if j == 0 else pl.ds(n_seq - 1, 1)
            lhs = arrived[last, s, srcs].reshape(r.stop - r.start, HD)
            got = acc[k, r, :] + jnp.dot(lhs, upbuf[s, last * HD :, :], preferred_element_type=jnp.float32)
            projected = projected + got.astype(jnp.bfloat16).astype(jnp.float32)
        acc[0, r, :] = projected
        sq = jnp.sum(projected * projected, axis=1, keepdims=True)
        return jnp.broadcast_to(sq, (r.stop - r.start, 128))

    spread(last, 2, outside & (z > 0))
    landed(arrived.at[last, pl.ds(0, n_phase - 1), pl.ds(0, n_seq - 1)], all_recv.at[1])
    sq_top = complete(0)
    landed(arrived.at[last, pl.ds(0, n_phase - 1), pl.ds(0, 1)], all_recv.at[2])
    rows_in(last, 2, z == 0)
    sq_all = jnp.concatenate([sq_top, complete(1)], axis=0)
    sqbuf[p] = sq_all.T[0:1, :]
    for other in partners:
        send(sqbuf.at[p], sqbuf.at[p], sq_send, sq_recv, {"phase": other})
    landed(sqbuf.at[pl.ds(0, n_phase - 1)], sq_recv)
    all_sq = sqbuf[0]
    for k in range(1, n_phase):
        all_sq = all_sq + sqbuf[k]
    all_sq = jnp.broadcast_to(all_sq[0:1, :], (128, full)).T[:, 0:1]
    norm = lax.rsqrt(all_sq / (n_phase * cols) + 1e-05)
    ss_ref[...] = (acc[0] * norm * og[...]).astype(jnp.bfloat16)
    sent(wbuf.at[:, :, pl.ds(0, half)], w_send, first | final)
    sent(wbuf.at[:, :, pl.ds(0, (n_seq + 1) * half)], w_send, jnp.logical_not(first | final))
    sent(wbuf.at[:, :, pl.ds(0, (n_seq - 1) * half)], p_send)
    sent(upbuf.at[pl.ds(0, n_phase - 1), up_half], up_send)
    sent(upbuf.at[pl.ds(0, n_phase - 1), up_half], upp_send)
    for dist in range(1, reach + 1):
        sent(halo.at[dist - 1, 0], h_send.at[dist - 1], (z >= dist - 1) & has_right)
        sent(halo.at[dist - 1, pl.ds(0, 3)], g_send.at[dist - 1], z >= dist)
    sent(outrows.at[:, pl.ds(0, n_seq - 1)], row_send, inner)
    sent(outrows.at[:, pl.ds(0, n_seq)], row_send, final)
    sent(arrived.at[pl.ds(0, last), pl.ds(0, n_phase - 1)], all_send.at[0])
    sent(arrived.at[last, pl.ds(0, n_phase - 1), pl.ds(0, n_seq - 1)], all_send.at[1])
    sent(arrived.at[last, pl.ds(0, n_phase - 1), pl.ds(0, 1)], all_send.at[2], z > 0)
    sent(sqbuf.at[pl.ds(0, n_phase - 1)], sq_send)


def flush_kernel(a_ref, b_ref, a_out, b_out, sems):
    copies = [
        pltpu.make_async_copy(a_ref, a_out, sems.at[0]),
        pltpu.make_async_copy(b_ref, b_out, sems.at[1]),
    ]
    for copy in copies:
        copy.start()
    for copy in copies:
        copy.wait()


def fused(n_seq, n_phase, byte_embed, in_gain, w_qkv, w_up, out_gain, bounds, owner):
    tok, d = byte_embed.shape
    rows, _, width = w_qkv.shape
    heads = width // HD
    crows = bounds.shape[0]
    cols = out_gain.shape[0]
    slot = 2 * crows // n_seq
    reach = -(-WINDOW // tok)
    bf, f32 = jnp.bfloat16, jnp.float32
    vmem = pl.BlockSpec(memory_space=pltpu.VMEM)
    hbm = pl.BlockSpec(memory_space=pltpu.HBM)
    dma = pltpu.SemaphoreType.DMA
    in_hbm = lambda a: pltpu.with_memory_space_constraint(a, pltpu.HBM)
    states, stretch = pl.pallas_call(
        functools.partial(fused_kernel, (n_seq, n_phase, reach, slot)),
        out_shape=(
            jax.ShapeDtypeStruct((tok, width), bf),
            jax.ShapeDtypeStruct((n_seq * slot, cols), bf),
        ),
        in_specs=[hbm] * 7,
        out_specs=(vmem, vmem),
        scratch_shapes=[
            pltpu.VMEM((tok, d), bf),
            pltpu.VMEM((1, d), f32),
            pltpu.VMEM((1, cols), f32),
            pltpu.VMEM((1, crows), jnp.int32),
            pltpu.VMEM((1, crows), jnp.int32),
            pltpu.VMEM((tok, d), bf),
            pltpu.VMEM((reach, n_phase, tok, width), bf),
            pltpu.VMEM((heads, 3, n_seq * rows, HD), bf),
            pltpu.VMEM((n_phase, w_up.shape[0], cols), bf),
            pltpu.VMEM((heads, tok, HD), bf),
            pltpu.VMEM((heads, reach + 1, tok, HD), bf),
            pltpu.VMEM((heads, reach + 1, tok, HD), bf),
            pltpu.VMEM((n_seq * slot, tok), bf),
            pltpu.VMEM((heads, n_seq, slot, HD), bf),
            pltpu.VMEM((heads, n_phase, n_seq, slot, HD), bf),
            pltpu.VMEM((n_phase, n_seq * slot, cols), f32),
            pltpu.VMEM((reach + 1, tok, 3 * HD), f32),
            pltpu.VMEM((n_phase, 1, n_seq * slot), f32),
            dma((7,)),
            dma(()),
            dma((heads, n_seq - 1)),
            dma(()),
            dma((heads + 1,)),
            dma(()),
            dma((2,)),
            dma(()),
            dma(()),
            dma((reach,)),
            dma((reach, 2)),
            dma((reach,)),
            dma((reach, 3)),
            dma(()),
            dma((heads, 3)),
            dma((3,)),
            dma((3,)),
            dma(()),
            dma(()),
            pltpu.SemaphoreType.REGULAR,
        ],
        compiler_params=pltpu.CompilerParams(
            collective_id=0, has_side_effects=True, vmem_limit_bytes=48 * 1024 * 1024
        ),
    )(
        in_hbm(byte_embed),
        in_hbm(in_gain),
        in_hbm(jnp.transpose(w_qkv, (1, 0, 2))),
        in_hbm(w_up),
        in_hbm(out_gain),
        in_hbm(bounds.reshape(1, crows)),
        in_hbm(owner.reshape(1, crows)),
    )
    return pl.pallas_call(
        flush_kernel,
        out_shape=(
            jax.ShapeDtypeStruct(states.shape, bf),
            jax.ShapeDtypeStruct(stretch.shape, bf),
        ),
        in_specs=[vmem] * 2,
        out_specs=(hbm, hbm),
        scratch_shapes=[dma((2,))],
        compiler_params=pltpu.CompilerParams(vmem_limit_bytes=4 * 1024 * 1024),
    )(states, stretch)


def passed_along(value, axis, by):
    devices = lax.axis_size(axis)
    pairs = [(i, i + by) for i in range(devices) if 0 <= i + by < devices]
    return lax.ppermute(value, axis, pairs)


def project_rows(rows, w_up, out_gain):
    groups = lax.axis_size("phase")
    full_rows = lax.all_gather(rows, "phase", axis=1, tiled=True)
    w_cols = lax.all_to_all(w_up, "phase", split_axis=1, concat_axis=0, tiled=True)
    count = full_rows.shape[0]
    width = rows.shape[1]
    columns = w_cols.shape[1]
    pieces = jnp.einsum(
        "nsg,sgc->snc",
        full_rows.reshape(count, groups, width),
        w_cols.reshape(groups, width, columns),
        preferred_element_type=jnp.float32,
    )
    projected = jnp.sum(pieces.astype(jnp.bfloat16).astype(jnp.float32), axis=0)
    squares = lax.psum(jnp.sum(projected * projected, axis=1), "phase")
    scale = lax.rsqrt(squares / DC + 1e-05)
    return (projected * scale[:, None] * out_gain).astype(jnp.bfloat16)


def on_device(byte_embed, in_gain, w_qkv, w_up, out_gain, bounds, owner):
    tok = byte_embed.shape[0]
    n_seq = lax.axis_size("seq")
    mine = lax.axis_index("seq")
    section = lax.axis_index("phase")
    width_dev = w_qkv.shape[2]
    heads_dev = width_dev // HD
    x32 = byte_embed.astype(jnp.float32)
    normed = (x32 * lax.rsqrt(jnp.mean(x32 * x32, axis=1, keepdims=True) + 1e-05) * in_gain).astype(
        jnp.bfloat16
    )
    piece = lax.all_gather(w_qkv, "seq", axis=0, tiled=True)
    qkv = jnp.dot(
        normed, piece.reshape(piece.shape[0], 3 * width_dev), preferred_element_type=jnp.float32
    ).astype(jnp.bfloat16)
    qkv = qkv.reshape(tok, 3, heads_dev, HD)
    query = qkv[:, 0]
    keys = qkv[:, 1]
    values = qkv[:, 2]
    reach = -(-WINDOW // tok)
    key_list = [keys]
    value_list = [values]
    for distance in range(1, reach + 1):
        earlier_keys, earlier_values = passed_along((keys, values), "seq", distance)
        key_list = [earlier_keys] + key_list
        value_list = [earlier_values] + value_list
    key_all = jnp.concatenate(key_list, axis=0)
    value_all = jnp.concatenate(value_list, axis=0)
    scores = jnp.einsum(
        "ihd,jhd->hij", query, key_all, preferred_element_type=jnp.float32
    ) * HD ** (-0.5)
    q_pos = mine * tok + jnp.arange(tok, dtype=jnp.int32)
    k_pos = mine * tok - reach * tok + jnp.arange((reach + 1) * tok, dtype=jnp.int32)
    keep = (
        (k_pos[None, :] <= q_pos[:, None])
        & (k_pos[None, :] > q_pos[:, None] - WINDOW)
        & (k_pos[None, :] >= 0)
    )
    scores = jnp.where(keep[None], scores, -jnp.inf)
    top = jnp.max(scores, axis=2, keepdims=True)
    expo = jnp.exp(scores - top)
    probs = (expo / jnp.sum(expo, axis=2, keepdims=True)).astype(jnp.bfloat16)
    attended = jnp.einsum(
        "hij,jhd->ihd", probs, value_all, preferred_element_type=jnp.float32
    ).astype(jnp.bfloat16)
    attended = attended.reshape(tok, width_dev)
    residual = lax.dynamic_slice_in_dim(x32, section * width_dev, width_dev, 1)
    byte_states = (residual + attended.astype(jnp.float32)).astype(jnp.bfloat16)
    local = bounds - mine * tok
    stretch_rows = jnp.take(byte_states, local, axis=0)
    owners = owner[:, 0]
    crows = owners.shape[0]
    slot_count = 2 * crows // n_seq
    place = jnp.arange(crows, dtype=jnp.int32)
    earlier = (owners[:, None] == owners[None, :]) & (place[None, :] < place[:, None])
    rank = jnp.sum(earlier.astype(jnp.int32), axis=1)
    target = owners * slot_count + rank
    placing = (target[None, :] == jnp.arange(n_seq * slot_count, dtype=jnp.int32)[:, None]).astype(
        jnp.bfloat16
    )
    outgoing = jnp.dot(placing, stretch_rows, preferred_element_type=jnp.float32).astype(
        jnp.bfloat16
    )
    outgoing = outgoing.reshape(n_seq, slot_count, width_dev)
    arrived = lax.all_to_all(outgoing, "seq", split_axis=0, concat_axis=0, tiled=True).reshape(
        n_seq * slot_count, width_dev
    )
    stretch_states = project_rows(arrived, w_up, out_gain)
    return (byte_states, stretch_states)


def solution(mesh):
    n_seq, n_phase, n_dp = (mesh.shape[axis] for axis in ("seq", "phase", "dp"))

    def body(byte_embed, in_gain, w_qkv, *rest):
        tok, (rows, _, width) = byte_embed.shape[0], w_qkv.shape
        slot = 2 * rest[2].shape[0] // n_seq
        tiled = rows % 128 == 0 and width % HD == 0 and tok % 256 == 0 and slot % 16 == 0
        fits = n_seq == n_phase and width == 3 * HD and WINDOW == 2 * tok
        if tiled and fits and n_dp == 2 and n_phase == 4 and w_qkv.shape[0] == rest[0].shape[0]:
            return fused(n_seq, n_phase, byte_embed, in_gain, w_qkv, *rest)
        return on_device(byte_embed, in_gain, w_qkv, *rest)

    return jax.shard_map(
        body,
        mesh=mesh,
        in_specs=(
            P(("dp", "seq"), None),
            P(),
            P("seq", None, "phase"),
            P("phase", None),
            P("phase"),
            P(("dp", "seq")),
            P(("dp", "seq"), None),
        ),
        out_specs=(P(("dp", "seq"), "phase"), P(("dp", "seq"), "phase")),
        check_vma=False,
    )
```
